256 devices in a mesh: band: 2 (over core), grow: 8 (over z), gcol: 16 (over y, x).
Axes of the slice: x: 4, y: 4, z: 8, core: 2. Of those that a mesh axis runs over, the one named last changes fastest.
Arguments:
- valence_orbitals: bfloat16 [16, 98304], replicated, may hold values from -6 to 6
- conduction_orbitals: bfloat16 [1024, 98304], P(('band', 'grow', 'gcol')), may hold values from -6 to 6
- valence_energy: float32 [16], replicated, may hold values from -3 to -0.5
- conduction_energy: float32 [1024], replicated, may hold values from 0.5 to 3
- coulomb_root: float32 [12288], replicated, may hold values from 0.2 to 2
- pair_bands: int32 [2, 5120], P(None, ('band', 'grow', 'gcol')), may hold values from 0 to 1023, as said below
- slot_counts: int32 [256], P(('band', 'grow', 'gcol')), may hold values from 1 to 19, as said below
Outputs:
- chi_zero: float32 [2, 12288, 12288], P('band', 'grow', 'gcol')
The draws below stay inside these ranges and needn't reach their ends.
Inputs may be any that keep to these rules, and one draw needn't show every extreme that they name: `pair_bands`: the slots of device d name conduction orbitals d * 4 to (d + 1) * 4 - 1 only, each of them at least once; no (valence, conduction) pair appears in two slots anywhere. `slot_counts`: the two devices of one chip (same grow and gcol index, band 0 and band 1) hold at most 20 live slots together; some chip holds exactly 20, and some device holds exactly 19.
All inputs are finite; a program needn't handle non-finite values.
Results may differ from the reference program's by a relative error of at most 0.012.
Values may be sent and summed in bfloat16 or wider, within the bound.
No kernel may reach another device: no remote copies, remote signals or barrier semaphores. Data moves between devices by JAX's collectives and lax.ppermute only.
A program may use at most 128 MiB of HBM per device.

```python
import math
import jax
import jax.numpy as jnp
from jax import lax

N1 = 16
N2 = 24
N3 = 32
M1 = 32
M2 = 48
M3 = 64
NG = 12288
MG = 98304
VALENCE = 16
CON_DEV = 4
CONDUCTION = 1024
SLOTS = 20
FREQS = 2
N_BAND = 2
N_GROW = 8
N_GCOL = 16
DEVICES = 256


def draw_pair_bands(key, part):
    key_val = jax.random.fold_in(key, 21)
    key_order = jax.random.fold_in(key, 22)
    val_keys = jax.random.split(key_val, DEVICES * CON_DEV)
    val_perms = jax.vmap(lambda k: jax.random.permutation(k, VALENCE))(val_keys).reshape(DEVICES, CON_DEV, VALENCE)
    order_keys = jax.random.split(key_order, DEVICES)
    slot_order = jax.vmap(lambda k: jax.random.permutation(k, SLOTS))(order_keys)
    drawn = jnp.arange(SLOTS).astype(jnp.int32)
    local_con = (drawn % CON_DEV)[slot_order]
    which_val = (drawn // CON_DEV)[slot_order]
    owner = jnp.arange(DEVICES).astype(jnp.int32)[:, None]
    valence = val_perms[owner, local_con, which_val]
    conduction = owner * CON_DEV + local_con
    return jnp.stack([valence.reshape(-1), conduction.reshape(-1)]).astype(jnp.int32)


def draw_slot_counts(key, part):
    chips = DEVICES // 2
    key_total = jax.random.fold_in(key, 11)
    key_first = jax.random.fold_in(key, 12)
    key_pick = jax.random.fold_in(key, 13)
    totals = jax.random.randint(key_total, (chips,), SLOTS // 2 + 1, SLOTS + 1)
    first_count = jax.random.randint(key_first, (chips,), 0, 1 << 20) % (totals - 1) + 1
    chosen = jax.random.randint(key_pick, (), 0, chips)
    is_hit = jnp.arange(chips) == chosen
    totals = jnp.where(is_hit, SLOTS, totals)
    first_count = jnp.where(is_hit, SLOTS - 1, first_count)
    return jnp.concatenate([first_count, totals - first_count]).astype(jnp.int32)


def block_scale(stream_key, dims, cuts, smallest, largest):
    level, own = 1.0, jax.random.fold_in(stream_key, 6)
    for axis_at, shards_of in cuts:
        draws = jnp.exp(jax.random.uniform(jax.random.fold_in(own, axis_at), (shards_of,), jnp.float32, smallest / len(cuts), largest / len(cuts)))
        level = level * jnp.repeat(draws, dims[axis_at] // shards_of).reshape([-1 if axis == axis_at else 1 for axis in range(len(dims))])
    return level


def noise(stream_key, extent, deviation, limit, shards=(), held_as=jnp.bfloat16):
    drawn = jax.random.normal(stream_key, extent, jnp.float32) * deviation
    if len(shards) > 0:
        drawn = block_scale(stream_key, extent, shards, -0.22, 0.18) * drawn
    return jnp.clip(drawn, min=-limit, max=limit).astype(held_as)


def setup_inputs(seed: int = 0) -> dict:
    key_of = jax.random.split(jax.random.key(seed), 8)
    valence_orbitals = noise(key_of[0], (VALENCE, MG), 1.0, 6.0)
    conduction_orbitals = noise(key_of[1], (CONDUCTION, MG), 1.0, 6.0, ((0, 256),))
    valence_energy = jnp.clip(jax.random.uniform(key_of[2], (VALENCE,), jnp.float32, -3.0, -0.5), -3.0, -0.5)
    conduction_energy = jnp.clip(jax.random.uniform(key_of[3], (CONDUCTION,), jnp.float32, 0.5, 3.0), 0.5, 3.0)
    coulomb_root = jnp.clip(jnp.exp(jax.random.uniform(key_of[4], (NG,), jnp.float32, math.log(0.2), math.log(2.0))), 0.2, 2.0)
    pair_bands = draw_pair_bands(jax.random.fold_in(key_of[7], 71), 0)
    slot_counts = draw_slot_counts(jax.random.fold_in(key_of[7], 71), 0)
    return {"valence_orbitals": valence_orbitals, "conduction_orbitals": conduction_orbitals, "valence_energy": valence_energy, "conduction_energy": conduction_energy, "coulomb_root": coulomb_root, "pair_bands": pair_bands, "slot_counts": slot_counts}


def pruned_table(keep, length):
    rows_i = lax.broadcasted_iota(jnp.int32, (keep, length), 0)
    cols_i = lax.broadcasted_iota(jnp.int32, (keep, length), 1)
    wave = (rows_i - keep // 2) % length
    angles = (wave * cols_i % length).astype(jnp.float32) * (2.0 * math.pi / length)
    return (jnp.cos(angles) + jnp.sin(angles)) / math.sqrt(length)

def reference(valence_orbitals, conduction_orbitals, valence_energy, conduction_energy, coulomb_root, pair_bands, slot_counts):
    highest = lax.Precision.HIGHEST
    total_slots = pair_bands.shape[1]
    val_index = pair_bands[0]
    con_index = pair_bands[1]
    products = valence_orbitals[val_index].astype(jnp.float32) * conduction_orbitals[con_index].astype(jnp.float32)
    lattice = products.reshape(total_slots, M1, M2, M3)
    lattice = jnp.einsum('pabc,kc->pabk', lattice, pruned_table(N3, M3), precision=highest)
    lattice = jnp.einsum('pabc,kb->pakc', lattice, pruned_table(N2, M2), precision=highest)
    lattice = jnp.einsum('pabc,ka->pkbc', lattice, pruned_table(N1, M1), precision=highest)
    density = (lattice.reshape(total_slots, N1 * N2 * N3) * coulomb_root).astype(jnp.bfloat16)
    slot_pos = (jnp.arange(total_slots) % SLOTS).astype(jnp.int32)
    is_live = slot_pos < jnp.repeat(slot_counts, SLOTS)
    energy_gap = conduction_energy[con_index] - valence_energy[val_index]
    frequency = jnp.arange(FREQS).astype(jnp.float32)[:, None]
    factor = 1.0 / math.sqrt(N_BAND * N_GROW * N_GCOL * SLOTS)
    response = 2.0 * energy_gap / (energy_gap * energy_gap + frequency * frequency)
    pair_weight = jnp.where(is_live, response, 0.0) * factor
    dense_wide = density.astype(jnp.float32)
    results = []
    for which in range(FREQS):
        weighted = (density.astype(jnp.float32) * pair_weight[which][:, None]).astype(jnp.bfloat16)
        chi_part = jnp.dot(dense_wide.T, weighted.astype(jnp.float32), precision=highest, preferred_element_type=jnp.float32)
        results.append(-chi_part)
    return jnp.stack(results)
```

```python
import math

import jax
import jax.numpy as jnp
import numpy as np
from jax import lax
from jax.experimental import pallas as pl
from jax.experimental.pallas import tpu as pltpu
from jax.sharding import Mesh
from jax.sharding import PartitionSpec as P

N1, N2, N3 = 16, 24, 32
M1, M2, M3 = 32, 48, 64
NP = N2 * N3
KP = M2 * M3
MG = M1 * KP
ROW = 2 * NP
TOTAL = 5120
SLOTS = 20
HALF = 10
GROW, GCOL = 8, 16
LANES = 128
CHUNKS = KP // LANES
LINES = MG // LANES
PANEL = GROW * GCOL * HALF
COLROWS = (HALF + 1) * GCOL
F32, BF16 = jnp.float32, jnp.bfloat16
VMEM = pltpu.VMEM
SMEM = pltpu.SMEM


def wave_table(keep, length):
    wave = (np.arange(keep)[:, None] - keep // 2) % length
    angles = 2.0 * np.pi * (wave * np.arange(length)[None, :] % length) / length
    return np.cos(angles) + np.sin(angles)


def halves(table):
    high = table.astype(np.float32).astype(BF16)
    return high, (table - high.astype(np.float64)).astype(np.float32).astype(BF16)


def tables():
    second = np.repeat(wave_table(N2, M2).T, N3, axis=1)
    third = np.tile(wave_table(N3, M3).T, (1, N2))
    first = wave_table(N1, M1)
    eye = np.eye(HALF)
    by_pair = np.einsum("pq,ka->pkqa", eye, first).reshape(HALF * N1, HALF * M1)
    parity = first.reshape(GROW, 2, M1)
    by_parity = np.einsum("pq,rsa->sprqa", eye, parity).reshape(HALF * N1, HALF * M1)
    return (
        second.astype(np.float32),
        third.astype(np.float32),
        halves(np.concatenate([by_pair, by_parity], 0)),
    )


def density_kernel(
    place, mine, other, val_e, con_e, val, con_mine, con_other, scale, second, third, mix_hi, mix_lo,
    col_out, row_out, vals, cons, lhs, acc, table,
):
    band = place[0] >> 7

    def spread(a, carry):
        for t in range(CHUNKS):
            where = pl.ds(pl.multiple_of(a * KP + t * LANES, LANES), LANES)
            line = t * M1 + a
            vals[pl.ds(line, 16, stride=LINES), :] = val[:, where].astype(F32)
            cons[pl.ds(line, 4, stride=LINES), :] = con_mine[:, where].astype(F32)
            cons[pl.ds(4 * LINES + line, 4, stride=LINES), :] = con_other[:, where].astype(F32)
        return carry

    lax.fori_loop(0, M1, spread, 0)

    is_first = band == 0
    first_count = jnp.where(is_first, mine[2 * SLOTS], other[2 * SLOTS])
    both_count = mine[2 * SLOTS] + other[2 * SLOTS]
    lane = lax.broadcasted_iota(jnp.int32, (1, LANES), 1) & 15
    gap = jnp.ones((1, LANES), F32)
    for p in range(HALF):
        pos = band * HALF + p
        from_first = pos < first_count
        slot = jnp.minimum(jnp.where(from_first, pos, pos - first_count), SLOTS - 1)
        own = from_first == is_first
        v = jnp.where(own, mine[slot], other[slot])
        c = jnp.where(own, mine[SLOTS + slot], other[SLOTS + slot])
        gap = jnp.where(lane == p, con_e[c] - val_e[v], gap)
        v_line = pl.multiple_of(v * LINES, M1)
        c_line = pl.multiple_of((jnp.where(own, 0, 4) + (c & 3)) * LINES, M1)

        def product(t, carry):
            made = vals[pl.ds(v_line + t * M1, M1), :] * cons[pl.ds(c_line + t * M1, M1), :]
            high = made.astype(BF16)
            where = pl.ds(pl.multiple_of(t * LANES, LANES), LANES)
            lhs[p * M1 : (p + 1) * M1, where] = high
            lhs[HALF * M1 + p * M1 : HALF * M1 + (p + 1) * M1, where] = (
                made - high.astype(F32)
            ).astype(BF16)
            return carry

        lax.fori_loop(0, CHUNKS, product, 0, unroll=4)

    acc[...] = jnp.zeros_like(acc)

    def transform(k, carry):
        for i in range(4):
            table[i * M3 : (i + 1) * M3, :] = (
                second[pl.ds(k * 4 + i, 1), :] * third[...]
            ).astype(BF16)
        where = pl.ds(pl.multiple_of(k * 256, 256), 256)
        acc[...] += jnp.dot(lhs[:, where], table[...], preferred_element_type=F32)
        return carry

    lax.fori_loop(0, KP // 256, transform, 0)
    mid = acc[: HALF * M1, :] + acc[HALF * M1 :, :]
    mid_hi = mid.astype(BF16)
    mid_lo = (mid - mid_hi.astype(F32)).astype(BF16)
    done = (
        jnp.dot(mix_hi[...], mid_hi, preferred_element_type=F32)
        + jnp.dot(mix_hi[...], mid_lo, preferred_element_type=F32)
        + jnp.dot(mix_lo[...], mid_hi, preferred_element_type=F32)
    )
    norm = 1.0 / math.sqrt(MG)
    wide = scale[...] * norm
    count = HALF * GROW
    for p in range(HALF):
        col_out[p] = (done[p * N1 : (p + 1) * N1] * wide[:N1]).astype(BF16)
        for s in range(2):
            at = HALF * N1 + s * count + p * GROW
            row_out[p, :, s * NP : (s + 1) * NP] = (
                done[at : at + GROW] * wide[N1 + s * GROW : N1 + (s + 1) * GROW]
            ).astype(BF16)

    at_lane = lax.broadcasted_iota(jnp.int32, (1, LANES), 1)
    frequency = (at_lane >> 4).astype(F32)
    live = (band * HALF + lane < both_count) & (lane < HALF) & (at_lane < 32)
    weight = jnp.where(
        live, 2.0 * gap / (gap * gap + frequency * frequency), 0.0
    ) * (1.0 / math.sqrt(TOTAL))
    w_hi = weight.astype(BF16)
    left = weight - w_hi.astype(F32)
    w_mid = left.astype(BF16)
    w_lo = (left - w_mid.astype(F32)).astype(BF16)
    zero = jnp.zeros((N1, NP - 3 * LANES), BF16)
    for i, part in enumerate((w_hi, w_mid, w_lo)):
        col_out[HALF, :, i * LANES : (i + 1) * LANES] = jnp.broadcast_to(
            part.astype(F32), (N1, LANES)
        ).astype(BF16)
    col_out[HALF, :, 3 * LANES :] = zero


def density_call(place, mine, other, val_e, con_e, val, con_mine, con_other, scale, interpret=False):
    second, third, (mix_hi, mix_lo) = tables()
    smem = pl.BlockSpec(memory_space=SMEM)
    vmem = pl.BlockSpec(memory_space=VMEM)
    return pl.pallas_call(
        density_kernel,
        out_shape=(
            jax.ShapeDtypeStruct((HALF + 1, N1, NP), BF16),
            jax.ShapeDtypeStruct((HALF, GROW, ROW), BF16),
        ),
        in_specs=[smem] * 5 + [vmem] * 8,
        out_specs=(vmem, vmem),
        scratch_shapes=[
            VMEM((16 * LINES, LANES), F32),
            VMEM((8 * LINES, LANES), F32),
            VMEM((2 * HALF * M1, KP), BF16),
            VMEM((2 * HALF * M1, NP), F32),
            VMEM((256, NP), BF16),
        ],
        interpret=interpret,
        name="density",
    )(place, mine, other, val_e, con_e, val, con_mine, con_other, scale,
      jnp.asarray(second), jnp.asarray(third), jnp.asarray(mix_hi), jnp.asarray(mix_lo))


AROUND = (0, 3, 1, 2)


def panel_kernel(place, *refs):
    cols = refs[:GROW]
    pieces = refs[GROW : GROW + 5]
    away_out, home_out = refs[GROW + 5 : GROW + 7]
    spread, weighted, rows, sems = refs[GROW + 7 :]
    me = place[0]
    band, z, y, x = me >> 7, (me >> 4) & 7, (me >> 2) & 3, me & 3
    copies = []
    at = 0
    for i, piece in enumerate(pieces):
        size = piece.shape[0]
        copies.append(pltpu.make_async_copy(piece, rows.at[pl.ds(at, size), :], sems.at[i]))
        copies[-1].start()
        at += size
    for i, col in enumerate(cols):
        start = pl.multiple_of(((z + ZAROUND[i]) & 7) * COLROWS, 8)
        for ch in range(NP // LANES):
            spread[ch, pl.ds(start, COLROWS), :] = col[:, ch * LANES : (ch + 1) * LANES].astype(F32)

    def assemble(j, carry):
        outer, inner = j >> 2, j & 3
        outer = jnp.where(outer == 0, 0, jnp.where(outer == 1, 3, jnp.where(outer == 2, 1, 2)))
        inner = jnp.where(inner == 0, 0, jnp.where(inner == 1, 3, jnp.where(inner == 2, 1, 2)))
        dy = jnp.where(band == 0, outer, inner)
        dx = jnp.where(band == 0, inner, outer)
        plane = ((y + dy) & 3) * 4 + ((x + dx) & 3)
        weight = jnp.zeros((GROW, LANES), F32)
        for part in range(3):
            weight += spread[part, pl.ds(HALF * GCOL + plane, GROW, stride=COLROWS), :]
        other = pltpu.roll(weight, LANES - 16, 1)
        away = jnp.where(band == 0, other, weight)
        home = jnp.where(band == 0, weight, other)
        for pp in range(HALF // 2):
            ws = [
                [jnp.broadcast_to(w[:, 2 * pp + q : 2 * pp + q + 1], (GROW, LANES)) for q in range(2)]
                for w in (away, home)
            ]
            to = pl.ds(pl.multiple_of(j * GROW * HALF + pp * 16, 16), 16)
            for ch in range(NP // LANES):
                got = [
                    spread[ch, pl.ds((2 * pp + q) * GCOL + plane, GROW, stride=COLROWS), :]
                    for q in range(2)
                ]
                for f in range(2):
                    weighted[to, f * NP + ch * LANES : f * NP + (ch + 1) * LANES] = jnp.concatenate(
                        [got[0] * ws[f][0], got[1] * ws[f][1]], 0
                    ).astype(BF16)
        return carry

    lax.fori_loop(0, GCOL, assemble, 0)
    for copy in copies:
        copy.wait()

    def product(m, carry):
        where = pl.ds(pl.multiple_of(m * 256, 256), 256)
        made = lax.dot_general(
            rows[:, where], weighted[...], (((0,), (0,)), ((), ())), preferred_element_type=F32
        )
        away_out[where, :] = made[:, :NP].astype(BF16)
        home_out[where, :] = made[:, NP:]
        return carry

    lax.fori_loop(0, ROW // 256, product, 0)


ZAROUND = (0, 7, 6, 5, 4, 1, 2, 3)


def panel_call(place, cols, pieces, interpret=False):
    vmem = pl.BlockSpec(memory_space=VMEM)
    return pl.pallas_call(
        panel_kernel,
        out_shape=(
            jax.ShapeDtypeStruct((ROW, NP), BF16),
            jax.ShapeDtypeStruct((ROW, NP), F32),
        ),
        in_specs=[pl.BlockSpec(memory_space=SMEM)] + [vmem] * GROW + [pl.BlockSpec(memory_space=pl.ANY)] * 5,
        out_specs=(vmem, vmem),
        scratch_shapes=[
            VMEM((NP // LANES, GROW * COLROWS, LANES), F32),
            VMEM((PANEL, 2 * NP), BF16),
            VMEM((PANEL, ROW), BF16),
            pltpu.SemaphoreType.DMA((5,)),
        ],
        interpret=interpret,
        name="panel",
    )(place, *cols, *pieces)


PLANE = ("band", "gcol_0", "gcol_1")


def turned(array, phase, step):
    pairs = []
    for band in range(2):
        along_x = (band == 0) == (phase == 0)
        for y in range(4):
            for x in range(4):
                to = (y, (x + step) % 4) if along_x else ((y + step) % 4, x)
                pairs.append((band * 16 + y * 4 + x, band * 16 + to[0] * 4 + to[1]))
    return lax.ppermute(array, PLANE, pairs)


def up(array, step):
    return lax.ppermute(array, "grow", [(i, (i + step) % GROW) for i in range(GROW)])


def swap(array):
    return lax.ppermute(array, "band", [(0, 1), (1, 0)])


def per_device(
    valence_orbitals,
    conduction_orbitals,
    valence_energy,
    conduction_energy,
    coulomb_root,
    pair_bands,
    slot_counts,
):
    place = lax.axis_index(("band", "grow", "gcol_0", "gcol_1")).astype(jnp.int32).reshape(1)
    meta = jnp.concatenate([pair_bands.reshape(2 * SLOTS), slot_counts, jnp.zeros(7, jnp.int32)])
    other_con = swap(conduction_orbitals)
    other_meta = swap(meta)
    planes = coulomb_root.reshape(GROW, 2, NP)
    scale = jnp.concatenate([coulomb_root.reshape(N1, NP), planes[:, 0], planes[:, 1]], 0)
    col, row = density_call(
        place, meta, other_meta, valence_energy, conduction_energy,
        valence_orbitals, conduction_orbitals, other_con, scale,
    )
    row = lax.all_to_all(row, "grow", 1, 1, tiled=True).reshape(GROW * HALF, ROW)
    col = lax.all_to_all(col, ("gcol_0", "gcol_1"), 1, 1, tiled=True).reshape(COLROWS, NP)

    half = row.shape[0] // 2
    below, above = turned(row, 0, 1), turned(row, 0, -1)
    ups, downs = [col], [col]
    ups.append(up(ups[-1], 1))
    downs.append(up(downs[-1], -1))
    far_a, far_b = turned(below[:half], 0, 1), turned(above[half:], 0, -1)
    ups.append(up(ups[-1], 1))
    downs.append(up(downs[-1], -1))
    line = jnp.concatenate([row, below, above, far_a, far_b], 0)
    half = line.shape[0] // 2
    below, above = turned(line, 1, 1), turned(line, 1, -1)
    ups.append(up(ups[-1], 1))
    downs.append(up(downs[-1], -1))
    far_a, far_b = turned(below[:half], 1, 1), turned(above[half:], 1, -1)
    ups.append(up(ups[-1], 1))
    away, home = panel_call(place, ups + downs[1:], [line, below, above, far_a, far_b])
    return -(home + swap(away).astype(F32))[None]


def solution(mesh):
    finer = Mesh(
        mesh.devices.reshape(mesh.shape["band"], mesh.shape["grow"], 4, 4),
        ("band", "grow", "gcol_0", "gcol_1"),
    )
    everywhere = ("band", "grow", "gcol_0", "gcol_1")
    in_specs = (P(), P(everywhere, None), P(), P(), P(), P(None, everywhere), P(everywhere))
    return jax.shard_map(
        per_device,
        mesh=finer,
        in_specs=in_specs,
        out_specs=P("band", "grow", ("gcol_0", "gcol_1")),
        check_vma=False,
    )
```

```python
import math

import jax
import jax.numpy as jnp
import numpy as np
from jax import lax
from jax.experimental import pallas as pl
from jax.experimental.pallas import tpu as pltpu
from jax.sharding import Mesh
from jax.sharding import PartitionSpec as P


N1, N2, N3 = 16, 24, 32
M1, M2, M3 = 32, 48, 64
NP = N2 * N3
KP = M2 * M3
MG = M1 * KP
ROW = 2 * NP
TOTAL = 5120
SLOTS = 20
HALF = 10
GROW, GCOL = 8, 16
LANES = 128
CHUNKS = KP // LANES
LINES = MG // LANES + 4
PANEL = GROW * GCOL * HALF
BLOCK = 64
ROWBLOCK = 120
COLROWS = GCOL * BLOCK + 4
WIDTH = NP // LANES
STEP = 512
ZAROUND = (0, 7, 6, 5, 4, 1, 2, 3)
F32, BF16 = jnp.float32, jnp.bfloat16
VMEM = pltpu.VMEM
SMEM = pltpu.SMEM


def wave_table(keep, length):
    wave = (np.arange(keep)[:, None] - keep // 2) % length
    angles = 2.0 * np.pi * (wave * np.arange(length)[None, :] % length) / length
    return np.cos(angles) + np.sin(angles)


def halves(table):
    high = table.astype(np.float32).astype(BF16)
    return high, (table - high.astype(np.float64)).astype(np.float32).astype(BF16)


def tables():
    second = np.repeat(wave_table(N2, M2).T, N3, axis=1)
    third = np.tile(wave_table(N3, M3).T, (1, N2))
    first = wave_table(N1, M1)
    mixed = np.zeros((N1, 16, HALF, M1))
    for p in range(HALF):
        mixed[:, p, p] = first
    return (
        second.astype(np.float32),
        third.astype(np.float32),
        halves(mixed.reshape(N1 * 16, HALF * M1)),
    )


def density_kernel(
    place, mine, other, val_e, con_e, val, con_mine, con_other, scale, second, third, mix_hi, mix_lo,
    *refs,
):
    col_out, row_out, vals, cons, lhs, acc, table, done, lines, row_lines = refs
    band = place[0] >> 7

    def spread(a, carry):
        for t in range(CHUNKS):
            where = pl.ds(pl.multiple_of(a * KP + t * LANES, LANES), LANES)
            line = t * M1 + a
            vals[pl.ds(line, 16, stride=LINES), :] = val[:, where].astype(F32)
            cons[pl.ds(line, 4, stride=LINES), :] = con_mine[:, where].astype(F32)
            cons[pl.ds(4 * LINES + line, 4, stride=LINES), :] = con_other[:, where].astype(F32)
        return carry

    lax.fori_loop(0, M1, spread, 0)

    is_first = band == 0
    first_count = jnp.where(is_first, mine[2 * SLOTS], other[2 * SLOTS])
    both_count = mine[2 * SLOTS] + other[2 * SLOTS]
    lane = lax.broadcasted_iota(jnp.int32, (1, LANES), 1) & 15
    gap = jnp.ones((1, LANES), F32)
    for p in range(HALF):
        pos = band * HALF + p
        from_first = pos < first_count
        slot = jnp.minimum(jnp.where(from_first, pos, pos - first_count), SLOTS - 1)
        own = from_first == is_first
        v = jnp.where(own, mine[slot], other[slot])
        c = jnp.where(own, mine[SLOTS + slot], other[SLOTS + slot])
        gap = jnp.where(lane == p, con_e[c] - val_e[v], gap)
        v_line = v * LINES
        c_line = (jnp.where(own, 0, 4) + (c & 3)) * LINES

        def product(t, carry):
            made = vals[pl.ds(v_line + t * M1, M1), :] * cons[pl.ds(c_line + t * M1, M1), :]
            high = made.astype(BF16)
            where = pl.ds(pl.multiple_of(t * LANES, LANES), LANES)
            lhs[p * M1 : (p + 1) * M1, where] = high
            lhs[HALF * M1 + p * M1 : HALF * M1 + (p + 1) * M1, where] = (
                made - high.astype(F32)
            ).astype(BF16)
            return carry

        lax.fori_loop(0, CHUNKS, product, 0, unroll=4)

    acc[...] = jnp.zeros_like(acc)

    def transform(k, carry):
        for i in range(STEP // M3):
            table[i * M3 : (i + 1) * M3, :] = (
                second[pl.ds(k * (STEP // M3) + i, 1), :] * third[...]
            ).astype(BF16)
        where = pl.ds(pl.multiple_of(k * STEP, STEP), STEP)
        acc[...] += jnp.dot(
            lhs[: HALF * M1, where], table[...], preferred_element_type=F32
        ) + jnp.dot(lhs[HALF * M1 :, where], table[...], preferred_element_type=F32)
        return carry

    lax.fori_loop(0, KP // STEP, transform, 0)
    mid = acc[...]
    mid_hi = mid.astype(BF16)
    mid_lo = (mid - mid_hi.astype(F32)).astype(BF16)
    done[...] = (
        jnp.dot(mix_hi[...], mid_hi, preferred_element_type=F32)
        + jnp.dot(mix_hi[...], mid_lo, preferred_element_type=F32)
        + jnp.dot(mix_lo[...], mid_hi, preferred_element_type=F32)
    )

    at_lane = lax.broadcasted_iota(jnp.int32, (1, LANES), 1)
    frequency = (at_lane >> 4).astype(F32)
    live = (band * HALF + lane < both_count) & (lane < HALF) & (at_lane < 32)
    weight = jnp.where(
        live, 2.0 * gap / (gap * gap + frequency * frequency), 0.0
    ) * (1.0 / math.sqrt(TOTAL))
    w_hi = weight.astype(BF16).astype(F32)
    w_mid = (weight - w_hi).astype(BF16).astype(F32)
    lines[WIDTH * HALF : WIDTH * HALF + 1, :] = w_hi
    lines[WIDTH * HALF + 1 : WIDTH * HALF + 2, :] = w_mid
    lines[WIDTH * HALF + 2 : WIDTH * HALF + 3, :] = weight - w_hi - w_mid
    lines[WIDTH * HALF + 3 : WIDTH * HALF + 4, :] = jnp.zeros((1, LANES), F32)

    norm = 1.0 / math.sqrt(MG)
    for k in range(N1):
        block = done[k * 16 : (k + 1) * 16, :] * (scale[k : k + 1, :] * norm)
        for ch in range(WIDTH):
            piece = block[:HALF, ch * LANES : (ch + 1) * LANES]
            lines[ch * HALF : (ch + 1) * HALF, :] = piece
            at = (k % 2 * WIDTH + ch) * HALF
            row_lines[at : at + HALF, :] = piece
        col_out[k] = lines[...].astype(BF16)
        if k % 2 == 1:
            row_out[k // 2] = row_lines[...].astype(BF16)


def density_call(place, mine, other, val_e, con_e, val, con_mine, con_other, scale, interpret=False):
    second, third, (mix_hi, mix_lo) = tables()
    smem = pl.BlockSpec(memory_space=SMEM)
    vmem = pl.BlockSpec(memory_space=VMEM)
    return pl.pallas_call(
        density_kernel,
        out_shape=[
            jax.ShapeDtypeStruct((N1, BLOCK, LANES), BF16),
            jax.ShapeDtypeStruct((GROW, ROWBLOCK, LANES), BF16),
        ],
        in_specs=[smem] * 5 + [vmem] * 8,
        out_specs=[vmem] * 2,
        scratch_shapes=[
            VMEM((16 * LINES, LANES), F32),
            VMEM((8 * LINES, LANES), F32),
            VMEM((2 * HALF * M1, KP), BF16),
            VMEM((HALF * M1, NP), F32),
            VMEM((STEP, NP), BF16),
            VMEM((N1 * 16, NP), F32),
            VMEM((BLOCK, LANES), F32),
            VMEM((ROWBLOCK, LANES), F32),
        ],
        compiler_params=pltpu.CompilerParams(vmem_limit_bytes=34 << 20),
        interpret=interpret,
        name="density",
    )(place, mine, other, val_e, con_e, val, con_mine, con_other, scale,
      jnp.asarray(second), jnp.asarray(third), jnp.asarray(mix_hi), jnp.asarray(mix_lo))


def pack_kernel(place, blocks, out, spread):
    z = (place[0] >> 4) & 7
    stride = ROWBLOCK + 4
    for i in range(GROW):
        spread[i * stride : i * stride + ROWBLOCK, :] = blocks[(z + ZAROUND[i]) & 7].astype(F32)
    for ch in range(2 * WIDTH):
        for pp in range(HALF // 2):
            got = [
                spread[pl.ds(ch * HALF + 2 * pp + q, GROW, stride=stride), :] for q in range(2)
            ]
            out[pp * 16 : (pp + 1) * 16, ch * LANES : (ch + 1) * LANES] = jnp.concatenate(
                got, 0
            ).astype(BF16)


def pack_call(place, blocks, interpret=False):
    vmem = pl.BlockSpec(memory_space=VMEM)
    return pl.pallas_call(
        pack_kernel,
        out_shape=jax.ShapeDtypeStruct((GROW * HALF, ROW), BF16),
        in_specs=[pl.BlockSpec(memory_space=SMEM), vmem],
        out_specs=vmem,
        scratch_shapes=[VMEM((GROW * (ROWBLOCK + 4), LANES), F32)],
        compiler_params=pltpu.CompilerParams(vmem_limit_bytes=4 << 20),
        interpret=interpret,
        name="pack",
    )(place, blocks)


def fetch(pieces, rows, sems):
    copies = []
    at = 0
    for i, piece in enumerate(pieces):
        size = piece.shape[0]
        copies.append(pltpu.make_async_copy(piece, rows.at[pl.ds(at, size), :], sems.at[i]))
        copies[-1].start()
        at += size
    return copies


def around(step):
    return jnp.where(step == 0, 0, jnp.where(step == 1, 3, jnp.where(step == 2, 1, 2)))


def assemble_kernel(place, *refs):
    cols = refs[:GROW]
    away_out, home_out, spread = refs[GROW:]
    me = place[0]
    band, y, x = me >> 7, (me >> 2) & 3, me & 3
    for i, col in enumerate(cols):
        for q in range(GCOL):
            at = i * COLROWS + q * BLOCK
            spread[at : at + BLOCK, :] = col[q].astype(F32)

    def assemble(j, carry):
        outer, inner = around(j >> 2), around(j & 3)
        dy = jnp.where(band == 0, outer, inner)
        dx = jnp.where(band == 0, inner, outer)
        base = (((y + dy) & 3) * 4 + ((x + dx) & 3)) * BLOCK
        weight = jnp.zeros((GROW, LANES), F32)
        for part in range(3):
            weight += spread[pl.ds(base + WIDTH * HALF + part, GROW, stride=COLROWS), :]
        other = pltpu.roll(weight, LANES - 16, 1)
        away = jnp.where(band == 0, other, weight)
        home = jnp.where(band == 0, weight, other)
        for pp in range(HALF // 2):
            ws = [
                [jnp.broadcast_to(w[:, 2 * pp + q : 2 * pp + q + 1], (GROW, LANES)) for q in range(2)]
                for w in (away, home)
            ]
            to = pl.ds(pl.multiple_of(j * GROW * HALF + pp * 16, 16), 16)
            for ch in range(WIDTH):
                got = [
                    spread[pl.ds(base + ch * HALF + 2 * pp + q, GROW, stride=COLROWS), :]
                    for q in range(2)
                ]
                where = slice(ch * LANES, (ch + 1) * LANES)
                for f, dest in enumerate((away_out, home_out)):
                    dest[to, where] = jnp.concatenate(
                        [got[0] * ws[f][0], got[1] * ws[f][1]], 0
                    ).astype(BF16)
        return carry

    lax.fori_loop(0, GCOL, assemble, 0)


def assemble_call(place, cols, interpret=False):
    vmem = pl.BlockSpec(memory_space=VMEM)
    return pl.pallas_call(
        assemble_kernel,
        out_shape=[jax.ShapeDtypeStruct((PANEL, NP), BF16)] * 2,
        in_specs=[pl.BlockSpec(memory_space=SMEM)] + [vmem] * GROW,
        out_specs=[vmem] * 2,
        scratch_shapes=[VMEM((GROW * COLROWS, LANES), F32)],
        compiler_params=pltpu.CompilerParams(vmem_limit_bytes=14 << 20),
        interpret=interpret,
        name="assemble",
    )(place, *cols)


def away_kernel(weighted, *refs):
    pieces = refs[:5]
    away_out, turned_out, rows, sems = refs[5:]
    for copy in fetch(pieces, rows, sems):
        copy.wait()

    def product(m, carry):
        where = pl.ds(pl.multiple_of(m * 256, 256), 256)
        part = rows[:, where].T
        turned_out[where, :] = part
        away_out[where, :] = jnp.dot(part, weighted[...], preferred_element_type=F32).astype(BF16)
        return carry

    lax.fori_loop(0, ROW // 256, product, 0)


def away_call(weighted, pieces, interpret=False):
    vmem = pl.BlockSpec(memory_space=VMEM)
    return pl.pallas_call(
        away_kernel,
        out_shape=(
            jax.ShapeDtypeStruct((ROW, NP), BF16),
            jax.ShapeDtypeStruct((ROW, PANEL), BF16),
        ),
        in_specs=[vmem] + [pl.BlockSpec(memory_space=pl.ANY)] * 5,
        out_specs=(vmem, vmem),
        scratch_shapes=[VMEM((PANEL, ROW), BF16), pltpu.SemaphoreType.DMA((5,))],
        compiler_params=pltpu.CompilerParams(vmem_limit_bytes=20 << 20),
        interpret=interpret,
        name="away",
    )(weighted, *pieces)


def home_kernel(weighted, rows, home_out):
    def product(m, carry):
        where = pl.ds(pl.multiple_of(m * 256, 256), 256)
        home_out[where, :] = jnp.dot(rows[where, :], weighted[...], preferred_element_type=F32)
        return carry

    lax.fori_loop(0, ROW // 256, product, 0)


def home_call(weighted, rows, interpret=False):
    vmem = pl.BlockSpec(memory_space=VMEM)
    return pl.pallas_call(
        home_kernel,
        out_shape=jax.ShapeDtypeStruct((ROW, NP), F32),
        in_specs=[vmem, vmem],
        out_specs=vmem,
        compiler_params=pltpu.CompilerParams(vmem_limit_bytes=16 << 20),
        interpret=interpret,
        name="home",
    )(weighted, rows)


PLANE = ("band", "gcol_0", "gcol_1")


def turned(array, phase, step):
    pairs = []
    for band in range(2):
        along_x = (band == 0) == (phase == 0)
        for y in range(4):
            for x in range(4):
                to = (y, (x + step) % 4) if along_x else ((y + step) % 4, x)
                pairs.append((band * 16 + y * 4 + x, band * 16 + to[0] * 4 + to[1]))
    return lax.ppermute(array, PLANE, pairs)


def up(array, step):
    return lax.ppermute(array, "grow", [(i, (i + step) % GROW) for i in range(GROW)])


def swap(array):
    return lax.ppermute(array, "band", [(0, 1), (1, 0)])


def per_device(
    valence_orbitals,
    conduction_orbitals,
    valence_energy,
    conduction_energy,
    coulomb_root,
    pair_bands,
    slot_counts,
):
    place = lax.axis_index(("band", "grow", "gcol_0", "gcol_1")).astype(jnp.int32).reshape(1)
    meta = jnp.concatenate([pair_bands.reshape(2 * SLOTS), slot_counts, jnp.zeros(7, jnp.int32)])
    other_con = swap(conduction_orbitals)
    other_meta = swap(meta)
    scale = coulomb_root.reshape(N1, NP)
    col, row = density_call(
        place, meta, other_meta, valence_energy, conduction_energy,
        valence_orbitals, conduction_orbitals, other_con, scale,
    )
    return exchange(place, col, row)


def exchange(place, col, row):
    row = lax.all_to_all(row, "grow", 0, 0, tiled=True)
    col = lax.all_to_all(col, ("gcol_0", "gcol_1"), 0, 0, tiled=True)
    row = pack_call(place, row)
    ups, downs = [col], [col]
    for _ in range(1, 5):
        ups.append(up(ups[-1], 1))
    for _ in range(1, 4):
        downs.append(up(downs[-1], -1))
    half = row.shape[0] // 2
    below, above = turned(row, 0, 1), turned(row, 0, -1)
    far_a, far_b = turned(below[:half], 0, 1), turned(above[half:], 0, -1)
    line = jnp.concatenate([row, below, above, far_a, far_b], 0)
    half = line.shape[0] // 2
    below, above = turned(line, 1, 1), turned(line, 1, -1)
    far_a, far_b = turned(below[:half], 1, 1), turned(above[half:], 1, -1)
    weighted_away, weighted_home = assemble_call(place, ups + downs[1:])
    away, turned_rows = away_call(weighted_away, [line, below, above, far_a, far_b])
    received = swap(away)
    home = home_call(weighted_home, turned_rows)
    return -(home + received.astype(F32))[None]


def solution(mesh):
    finer = Mesh(
        mesh.devices.reshape(mesh.shape["band"], mesh.shape["grow"], 4, 4),
        ("band", "grow", "gcol_0", "gcol_1"),
    )
    everywhere = ("band", "grow", "gcol_0", "gcol_1")
    in_specs = (P(), P(everywhere, None), P(), P(), P(), P(None, everywhere), P(everywhere))
    return jax.shard_map(
        per_device,
        mesh=finer,
        in_specs=in_specs,
        out_specs=P("band", "grow", ("gcol_0", "gcol_1")),
        check_vma=False,
    )
```

```python
import math

import jax
import jax.numpy as jnp
import numpy as np
from jax import lax
from jax.experimental import pallas as pl
from jax.experimental.pallas import tpu as pltpu
from jax.sharding import Mesh
from jax.sharding import PartitionSpec as P


N1, N2, N3 = 16, 24, 32
M1, M2, M3 = 32, 48, 64
NP = N2 * N3
KP = M2 * M3
MG = M1 * KP
ROW = 2 * NP
TOTAL = 5120
SLOTS = 20
HALF = 10
GROW, GCOL = 8, 16
LANES = 128
CHUNKS = KP // LANES
LINES = MG // LANES + 4
PANEL = GROW * GCOL * HALF
BLOCK = 64
ROWBLOCK = 120
COLROWS = GCOL * BLOCK + 4
WIDTH = NP // LANES
STEP = 512
ZAROUND = (0, 7, 6, 5, 4, 1, 2, 3)
F32, BF16 = jnp.float32, jnp.bfloat16
VMEM = pltpu.VMEM
SMEM = pltpu.SMEM


def wave_table(keep, length):
    wave = (np.arange(keep)[:, None] - keep // 2) % length
    angles = 2.0 * np.pi * (wave * np.arange(length)[None, :] % length) / length
    return np.cos(angles) + np.sin(angles)


def halves(table):
    high = table.astype(np.float32).astype(BF16)
    return high, (table - high.astype(np.float64)).astype(np.float32).astype(BF16)


def tables():
    second = np.repeat(wave_table(N2, M2).T, N3, axis=1)
    third = np.tile(wave_table(N3, M3).T, (1, N2))
    first = wave_table(N1, M1)
    mixed = np.zeros((N1, 16, HALF, M1))
    for p in range(HALF):
        mixed[:, p, p] = first
    return (
        second.astype(np.float32),
        third.astype(np.float32),
        halves(mixed.reshape(N1 * 16, HALF * M1)),
    )


def density_kernel(
    place, mine, other, *refs,
):
    hbm, refs = refs[:10], refs[10:]
    col_out, row_out, vals, cons, lhs, acc, table_a, table_b, done, lines, row_lines = refs[:11]
    local, sems = refs[11:21], refs[21]
    copies = [pltpu.make_async_copy(a, b, sems.at[i]) for i, (a, b) in enumerate(zip(hbm, local))]
    for copy in copies:
        copy.start()
    val, con_mine, con_other, second, third, mix_hi, mix_lo, scale, val_e, con_e = local
    band = place[0] >> 7
    for copy in copies[:3]:
        copy.wait()

    def spread(a, carry):
        for t in range(CHUNKS):
            where = pl.ds(pl.multiple_of(a * KP + t * LANES, LANES), LANES)
            line = t * M1 + a
            vals[pl.ds(line, 16, stride=LINES), :] = val[:, where].astype(F32)
            cons[pl.ds(line, 8, stride=LINES), :] = jnp.concatenate(
                [con_mine[:, where].astype(F32), con_other[:, where].astype(F32)], 0
            )
        return carry

    lax.fori_loop(0, M1, spread, 0)
    for copy in copies[3:]:
        copy.wait()

    is_first = band == 0
    first_count = jnp.where(is_first, mine[2 * SLOTS], other[2 * SLOTS])
    both_count = mine[2 * SLOTS] + other[2 * SLOTS]
    lane = lax.broadcasted_iota(jnp.int32, (1, LANES), 1) & 15
    gap = jnp.ones((1, LANES), F32)
    for p in range(HALF):
        pos = band * HALF + p
        from_first = pos < first_count
        slot = jnp.minimum(jnp.where(from_first, pos, pos - first_count), SLOTS - 1)
        own = from_first == is_first
        v = jnp.where(own, mine[slot], other[slot])
        c = jnp.where(own, mine[SLOTS + slot], other[SLOTS + slot])
        gap = jnp.where(lane == p, con_e[c] - val_e[v], gap)
        v_line = v * LINES
        c_line = (jnp.where(own, 0, 4) + (c & 3)) * LINES

        def product(t, carry):
            made = vals[pl.ds(v_line + t * M1, M1), :] * cons[pl.ds(c_line + t * M1, M1), :]
            high = made.astype(BF16)
            where = pl.ds(pl.multiple_of(t * LANES, LANES), LANES)
            lhs[p * M1 : (p + 1) * M1, where] = high
            lhs[HALF * M1 + p * M1 : HALF * M1 + (p + 1) * M1, where] = (
                made - high.astype(F32)
            ).astype(BF16)
            return carry

        lax.fori_loop(0, CHUNKS, product, 0, unroll=4)

    acc[...] = jnp.zeros_like(acc)

    def make(table, k):
        for i in range(STEP // M3):
            table[i * M3 : (i + 1) * M3, :] = (
                second[pl.ds(k * (STEP // M3) + i, 1), :] * third[...]
            ).astype(BF16)

    def add(table, k):
        where = pl.ds(pl.multiple_of(k * STEP, STEP), STEP)
        acc[...] += jnp.dot(
            lhs[: HALF * M1, where], table[...], preferred_element_type=F32
        ) + jnp.dot(lhs[HALF * M1 :, where], table[...], preferred_element_type=F32)

    last = KP // STEP - 1
    make(table_a, 0)

    def transform(k, carry):
        make(table_b, 2 * k + 1)
        add(table_a, 2 * k)
        make(table_a, jnp.minimum(2 * k + 2, last))
        add(table_b, 2 * k + 1)
        return carry

    lax.fori_loop(0, KP // STEP // 2, transform, 0)
    mid = acc[...]
    mid_hi = mid.astype(BF16)
    mid_lo = (mid - mid_hi.astype(F32)).astype(BF16)
    done[...] = (
        jnp.dot(mix_hi[...], mid_hi, preferred_element_type=F32)
        + jnp.dot(mix_hi[...], mid_lo, preferred_element_type=F32)
        + jnp.dot(mix_lo[...], mid_hi, preferred_element_type=F32)
    )

    at_lane = lax.broadcasted_iota(jnp.int32, (1, LANES), 1)
    frequency = (at_lane >> 4).astype(F32)
    live = (band * HALF + lane < both_count) & (lane < HALF) & (at_lane < 32)
    weight = jnp.where(
        live, 2.0 * gap / (gap * gap + frequency * frequency), 0.0
    ) * (1.0 / math.sqrt(TOTAL))
    w_hi = weight.astype(BF16).astype(F32)
    w_mid = (weight - w_hi).astype(BF16).astype(F32)
    lines[WIDTH * HALF : WIDTH * HALF + 1, :] = w_hi
    lines[WIDTH * HALF + 1 : WIDTH * HALF + 2, :] = w_mid
    lines[WIDTH * HALF + 2 : WIDTH * HALF + 3, :] = weight - w_hi - w_mid
    lines[WIDTH * HALF + 3 : WIDTH * HALF + 4, :] = jnp.zeros((1, LANES), F32)

    norm = 1.0 / math.sqrt(MG)
    for k in range(N1):
        block = done[k * 16 : (k + 1) * 16, :] * (scale[k : k + 1, :] * norm)
        for ch in range(WIDTH):
            piece = block[:HALF, ch * LANES : (ch + 1) * LANES]
            lines[ch * HALF : (ch + 1) * HALF, :] = piece
            at = (k % 2 * WIDTH + ch) * HALF
            row_lines[at : at + HALF, :] = piece
        col_out[k] = lines[...].astype(BF16)
        if k % 2 == 1:
            row_out[k // 2] = row_lines[...].astype(BF16)


def stay(array):
    return pltpu.with_memory_space_constraint(jnp.asarray(array), pltpu.HBM)


def density_call(place, mine, other, val_e, con_e, val, con_mine, con_other, scale, interpret=False):
    second, third, (mix_hi, mix_lo) = tables()
    smem = pl.BlockSpec(memory_space=SMEM)
    vmem = pl.BlockSpec(memory_space=VMEM)
    hbm = pl.BlockSpec(memory_space=pltpu.HBM)
    anywhere = pl.BlockSpec(memory_space=pl.ANY)
    return pl.pallas_call(
        density_kernel,
        out_shape=[
            jax.ShapeDtypeStruct((N1, BLOCK, LANES), BF16),
            jax.ShapeDtypeStruct((GROW, ROWBLOCK, LANES), BF16),
        ],
        in_specs=[smem] * 3 + [hbm, hbm, anywhere] + [hbm] * 4 + [anywhere, hbm, hbm],
        out_specs=[vmem] * 2,
        scratch_shapes=[
            VMEM((16 * LINES, LANES), F32),
            VMEM((8 * LINES, LANES), F32),
            VMEM((2 * HALF * M1, KP), BF16),
            VMEM((HALF * M1, NP), F32),
            VMEM((STEP, NP), BF16),
            VMEM((STEP, NP), BF16),
            VMEM((N1 * 16, NP), F32),
            VMEM((BLOCK, LANES), F32),
            VMEM((ROWBLOCK, LANES), F32),
            VMEM((16, MG), BF16),
            VMEM((4, MG), BF16),
            VMEM((4, MG), BF16),
            VMEM((M2, NP), F32),
            VMEM((M3, NP), F32),
            VMEM((N1 * 16, HALF * M1), BF16),
            VMEM((N1 * 16, HALF * M1), BF16),
            VMEM((N1, NP), F32),
            SMEM((16,), F32),
            SMEM((1024,), F32),
            pltpu.SemaphoreType.DMA((10,)),
        ],
        compiler_params=pltpu.CompilerParams(vmem_limit_bytes=34 << 20),
        interpret=interpret,
        name="density",
    )(place, mine, other, stay(val), stay(con_mine), con_other, stay(second), stay(third),
      stay(mix_hi), stay(mix_lo), scale, stay(val_e), stay(con_e))


def pack_kernel(place, blocks, out, spread):
    z = (place[0] >> 4) & 7
    stride = ROWBLOCK + 4
    for i in range(GROW):
        spread[i * stride : i * stride + ROWBLOCK, :] = blocks[(z + ZAROUND[i]) & 7].astype(F32)
    for ch in range(2 * WIDTH):
        for pp in range(HALF // 2):
            got = [
                spread[pl.ds(ch * HALF + 2 * pp + q, GROW, stride=stride), :] for q in range(2)
            ]
            out[pp * 16 : (pp + 1) * 16, ch * LANES : (ch + 1) * LANES] = jnp.concatenate(
                got, 0
            ).astype(BF16)


def pack_call(place, blocks, interpret=False):
    vmem = pl.BlockSpec(memory_space=VMEM)
    return pl.pallas_call(
        pack_kernel,
        out_shape=jax.ShapeDtypeStruct((GROW * HALF, ROW), BF16),
        in_specs=[pl.BlockSpec(memory_space=SMEM), vmem],
        out_specs=vmem,
        scratch_shapes=[VMEM((GROW * (ROWBLOCK + 4), LANES), F32)],
        compiler_params=pltpu.CompilerParams(vmem_limit_bytes=4 << 20),
        interpret=interpret,
        name="pack",
    )(place, blocks)


def fetch(pieces, rows, sems):
    copies = []
    at = 0
    for i, piece in enumerate(pieces):
        size = piece.shape[0]
        copies.append(pltpu.make_async_copy(piece, rows.at[pl.ds(at, size), :], sems.at[i]))
        copies[-1].start()
        at += size
    return copies


def around(step):
    return jnp.where(step == 0, 0, jnp.where(step == 1, 3, jnp.where(step == 2, 1, 2)))


def assemble_kernel(place, *refs):
    cols = refs[:GROW]
    away_out, home_out, spread = refs[GROW:]
    me = place[0]
    band, y, x = me >> 7, (me >> 2) & 3, me & 3
    for i, col in enumerate(cols):
        for q in range(GCOL):
            at = i * COLROWS + q * BLOCK
            spread[at : at + BLOCK, :] = col[q].astype(F32)

    def assemble(j, carry):
        outer, inner = around(j >> 2), around(j & 3)
        dy = jnp.where(band == 0, outer, inner)
        dx = jnp.where(band == 0, inner, outer)
        base = (((y + dy) & 3) * 4 + ((x + dx) & 3)) * BLOCK
        weight = jnp.zeros((GROW, LANES), F32)
        for part in range(3):
            weight += spread[pl.ds(base + WIDTH * HALF + part, GROW, stride=COLROWS), :]
        other = pltpu.roll(weight, LANES - 16, 1)
        away = jnp.where(band == 0, other, weight)
        home = jnp.where(band == 0, weight, other)
        for pp in range(HALF // 2):
            ws = [
                [jnp.broadcast_to(w[:, 2 * pp + q : 2 * pp + q + 1], (GROW, LANES)) for q in range(2)]
                for w in (away, home)
            ]
            to = pl.ds(pl.multiple_of(j * GROW * HALF + pp * 16, 16), 16)
            for ch in range(WIDTH):
                got = [
                    spread[pl.ds(base + ch * HALF + 2 * pp + q, GROW, stride=COLROWS), :]
                    for q in range(2)
                ]
                where = slice(ch * LANES, (ch + 1) * LANES)
                for f, dest in enumerate((away_out, home_out)):
                    dest[to, where] = jnp.concatenate(
                        [got[0] * ws[f][0], got[1] * ws[f][1]], 0
                    ).astype(BF16)
        return carry

    lax.fori_loop(0, GCOL, assemble, 0)


def assemble_call(place, cols, interpret=False):
    vmem = pl.BlockSpec(memory_space=VMEM)
    return pl.pallas_call(
        assemble_kernel,
        out_shape=[jax.ShapeDtypeStruct((PANEL, NP), BF16)] * 2,
        in_specs=[pl.BlockSpec(memory_space=SMEM)] + [vmem] * GROW,
        out_specs=[vmem] * 2,
        scratch_shapes=[VMEM((GROW * COLROWS, LANES), F32)],
        compiler_params=pltpu.CompilerParams(vmem_limit_bytes=14 << 20),
        interpret=interpret,
        name="assemble",
    )(place, *cols)


def away_kernel(weighted, *refs):
    pieces = refs[:5]
    away_out, turned_out, rows, sems = refs[5:]
    for copy in fetch(pieces, rows, sems):
        copy.wait()

    def product(m, carry):
        where = pl.ds(pl.multiple_of(m * 256, 256), 256)
        part = rows[:, where].T
        turned_out[where, :] = part
        away_out[where, :] = jnp.dot(part, weighted[...], preferred_element_type=F32).astype(BF16)
        return carry

    lax.fori_loop(0, ROW // 256, product, 0)


def away_call(weighted, pieces, interpret=False):
    vmem = pl.BlockSpec(memory_space=VMEM)
    return pl.pallas_call(
        away_kernel,
        out_shape=(
            jax.ShapeDtypeStruct((ROW, NP), BF16),
            jax.ShapeDtypeStruct((ROW, PANEL), BF16),
        ),
        in_specs=[vmem] + [pl.BlockSpec(memory_space=pl.ANY)] * 5,
        out_specs=(vmem, vmem),
        scratch_shapes=[VMEM((PANEL, ROW), BF16), pltpu.SemaphoreType.DMA((5,))],
        compiler_params=pltpu.CompilerParams(vmem_limit_bytes=20 << 20),
        interpret=interpret,
        name="away",
    )(weighted, *pieces)


def home_kernel(weighted, rows, home_out):
    def product(m, carry):
        where = pl.ds(pl.multiple_of(m * 256, 256), 256)
        home_out[where, :] = jnp.dot(rows[where, :], weighted[...], preferred_element_type=F32)
        return carry

    lax.fori_loop(0, ROW // 256, product, 0)


def home_call(weighted, rows, interpret=False):
    vmem = pl.BlockSpec(memory_space=VMEM)
    return pl.pallas_call(
        home_kernel,
        out_shape=jax.ShapeDtypeStruct((ROW, NP), F32),
        in_specs=[vmem, vmem],
        out_specs=vmem,
        compiler_params=pltpu.CompilerParams(vmem_limit_bytes=16 << 20),
        interpret=interpret,
        name="home",
    )(weighted, rows)


PLANE = ("band", "gcol_0", "gcol_1")


def turned(array, phase, step):
    pairs = []
    for band in range(2):
        along_x = (band == 0) == (phase == 0)
        for y in range(4):
            for x in range(4):
                to = (y, (x + step) % 4) if along_x else ((y + step) % 4, x)
                pairs.append((band * 16 + y * 4 + x, band * 16 + to[0] * 4 + to[1]))
    return lax.ppermute(array, PLANE, pairs)


def up(array, step):
    return lax.ppermute(array, "grow", [(i, (i + step) % GROW) for i in range(GROW)])


def swap(array):
    return lax.ppermute(array, "band", [(0, 1), (1, 0)])


def per_device(
    valence_orbitals,
    conduction_orbitals,
    valence_energy,
    conduction_energy,
    coulomb_root,
    pair_bands,
    slot_counts,
):
    place = lax.axis_index(("band", "grow", "gcol_0", "gcol_1")).astype(jnp.int32).reshape(1)
    meta = jnp.concatenate([pair_bands.reshape(2 * SLOTS), slot_counts, jnp.zeros(7, jnp.int32)])
    other_con = swap(conduction_orbitals)
    other_meta = swap(meta)
    scale = coulomb_root.reshape(N1, NP)
    col, row = density_call(
        place, meta, other_meta, valence_energy, conduction_energy,
        valence_orbitals, conduction_orbitals, other_con, scale,
    )
    return exchange(place, col, row)


def exchange(place, col, row):
    row = lax.all_to_all(row, "grow", 0, 0, tiled=True)
    col = lax.all_to_all(col, ("gcol_0", "gcol_1"), 0, 0, tiled=True)
    row = pack_call(place, row)
    ups, downs = [col], [col]
    for _ in range(1, 5):
        ups.append(up(ups[-1], 1))
    for _ in range(1, 4):
        downs.append(up(downs[-1], -1))
    below, above, far = turned(row, 0, 1), turned(row, 0, -1), turned(row, 0, 2)
    line = jnp.concatenate([row, below, above, far], 0)
    half = line.shape[0] // 2
    below, above = turned(line, 1, 1), turned(line, 1, -1)
    far_a, far_b = turned(below[:half], 1, 1), turned(above[half:], 1, -1)
    weighted_away, weighted_home = assemble_call(place, ups + downs[1:])
    away, turned_rows = away_call(weighted_away, [line, below, above, far_a, far_b])
    received = swap(away)
    home = home_call(weighted_home, turned_rows)
    return -(home + received.astype(F32))[None]


def solution(mesh):
    finer = Mesh(
        mesh.devices.reshape(mesh.shape["band"], mesh.shape["grow"], 4, 4),
        ("band", "grow", "gcol_0", "gcol_1"),
    )
    everywhere = ("band", "grow", "gcol_0", "gcol_1")
    in_specs = (P(), P(everywhere, None), P(), P(), P(), P(None, everywhere), P(everywhere))
    return jax.shard_map(
        per_device,
        mesh=finer,
        in_specs=in_specs,
        out_specs=P("band", "grow", ("gcol_0", "gcol_1")),
        check_vma=False,
    )
```

```python
import math

import jax
import jax.numpy as jnp
import numpy as np
from jax import lax
from jax.experimental import pallas as pl
from jax.experimental.pallas import tpu as pltpu
from jax.sharding import Mesh
from jax.sharding import PartitionSpec as P


N1, N2, N3 = 16, 24, 32
M1, M2, M3 = 32, 48, 64
NP = N2 * N3
KP = M2 * M3
MG = M1 * KP
ROW = 2 * NP
TOTAL = 5120
SLOTS = 20
HALF = 10
GROW, GCOL = 8, 16
LANES = 128
CHUNKS = KP // LANES
LINES = MG // LANES + 4
PANEL = GROW * GCOL * HALF
BLOCK = 64
ROWBLOCK = 120
COLROWS = GCOL * BLOCK + 4
WIDTH = NP // LANES
STEP = 512
F32, BF16 = jnp.float32, jnp.bfloat16
VMEM = pltpu.VMEM
SMEM = pltpu.SMEM


def wave_table(keep, length):
    wave = (np.arange(keep)[:, None] - keep // 2) % length
    angles = 2.0 * np.pi * (wave * np.arange(length)[None, :] % length) / length
    return np.cos(angles) + np.sin(angles)


def halves(table):
    high = table.astype(np.float32).astype(BF16)
    return high, (table - high.astype(np.float64)).astype(np.float32).astype(BF16)


def tables():
    second = np.repeat(wave_table(N2, M2).T, N3, axis=1)
    third = np.tile(wave_table(N3, M3).T, (1, N2))
    first = wave_table(N1, M1)
    mixed = np.zeros((N1, 16, HALF, M1))
    for p in range(HALF):
        mixed[:, p, p] = first
    return (
        second.astype(np.float32),
        third.astype(np.float32),
        halves(mixed.reshape(N1 * 16, HALF * M1)),
    )


def density_kernel(
    place, mine, other, *refs,
):
    hbm, refs = refs[:10], refs[10:]
    col_out = refs[0]
    row_outs = refs[1:5]
    vals, cons, lhs, acc, table_a, table_b, done, lines, row_lines = refs[5:14]
    local, sems = refs[14:24], refs[24]
    copies = [pltpu.make_async_copy(a, b, sems.at[i]) for i, (a, b) in enumerate(zip(hbm, local))]
    for copy in copies:
        copy.start()
    val, con_mine, con_other, second, third, mix_hi, mix_lo, scale, val_e, con_e = local
    band = place[0] >> 7
    z = (place[0] >> 4) & 7
    for copy in copies[:3]:
        copy.wait()

    def spread(a, carry):
        for t in range(CHUNKS):
            where = pl.ds(pl.multiple_of(a * KP + t * LANES, LANES), LANES)
            line = t * M1 + a
            vals[pl.ds(line, 16, stride=LINES), :] = val[:, where].astype(F32)
            cons[pl.ds(line, 8, stride=LINES), :] = jnp.concatenate(
                [con_mine[:, where].astype(F32), con_other[:, where].astype(F32)], 0
            )
        return carry

    lax.fori_loop(0, M1, spread, 0)
    for copy in copies[3:]:
        copy.wait()

    is_first = band == 0
    first_count = jnp.where(is_first, mine[2 * SLOTS], other[2 * SLOTS])
    both_count = mine[2 * SLOTS] + other[2 * SLOTS]
    lane = lax.broadcasted_iota(jnp.int32, (1, LANES), 1) & 15
    gaps = []
    for h in range(2):
        gap = jnp.ones((1, LANES), F32)
        for p in range(HALF):
            pos = h * HALF + p
            from_first = pos < first_count
            slot = jnp.minimum(jnp.where(from_first, pos, pos - first_count), SLOTS - 1)
            own = from_first == is_first
            v = jnp.where(own, mine[slot], other[slot])
            c = jnp.where(own, mine[SLOTS + slot], other[SLOTS + slot])
            gap = jnp.where(lane == p, con_e[c] - val_e[v], gap)
            v_line = v * LINES
            c_line = (jnp.where(own, 0, 4) + (c & 3)) * LINES
            top = pos * M1

            def product(t, carry):
                made = vals[pl.ds(v_line + t * M1, M1), :] * cons[pl.ds(c_line + t * M1, M1), :]
                where = pl.ds(pl.multiple_of(t * LANES, LANES), LANES)
                lhs[top : top + M1, where] = made.astype(BF16)
                return carry

            lax.fori_loop(0, CHUNKS, product, 0, unroll=6)
        gaps.append(gap)

    acc[...] = jnp.zeros_like(acc)

    def make(table, k):
        for i in range(STEP // M3):
            table[i * M3 : (i + 1) * M3, :] = (
                second[pl.ds(k * (STEP // M3) + i, 1), :] * third[...]
            ).astype(BF16)

    def add(table, k):
        where = pl.ds(pl.multiple_of(k * STEP, STEP), STEP)
        acc[...] += jnp.dot(lhs[:, where], table[...], preferred_element_type=F32)

    last = KP // STEP - 1
    make(table_a, 0)

    def transform(k, carry):
        make(table_b, 2 * k + 1)
        add(table_a, 2 * k)
        make(table_a, jnp.minimum(2 * k + 2, last))
        add(table_b, 2 * k + 1)
        return carry

    lax.fori_loop(0, KP // STEP // 2, transform, 0)
    at_lane = lax.broadcasted_iota(jnp.int32, (1, LANES), 1)
    frequency = (at_lane >> 4).astype(F32)
    norm = 1.0 / math.sqrt(MG)
    for h in range(2):
        mid = acc[h * HALF * M1 : (h + 1) * HALF * M1, :]
        mid_hi = mid.astype(BF16)
        mid_lo = (mid - mid_hi.astype(F32)).astype(BF16)
        done[...] = (
            jnp.dot(mix_hi[...], mid_hi, preferred_element_type=F32)
            + jnp.dot(mix_hi[...], mid_lo, preferred_element_type=F32)
            + jnp.dot(mix_lo[...], mid_hi, preferred_element_type=F32)
        )
        gap = gaps[h]
        live = (h * HALF + lane < both_count) & (lane < HALF) & (at_lane < 32)
        weight = jnp.where(
            live, 2.0 * gap / (gap * gap + frequency * frequency), 0.0
        ) * (1.0 / math.sqrt(TOTAL))
        w_hi = weight.astype(BF16).astype(F32)
        w_mid = (weight - w_hi).astype(BF16).astype(F32)
        lines[WIDTH * HALF : WIDTH * HALF + 1, :] = w_hi
        lines[WIDTH * HALF + 1 : WIDTH * HALF + 2, :] = w_mid
        lines[WIDTH * HALF + 2 : WIDTH * HALF + 3, :] = weight - w_hi - w_mid
        lines[WIDTH * HALF + 3 : WIDTH * HALF + 4, :] = jnp.zeros((1, LANES), F32)
        for k in range(N1):
            block = done[k * 16 : (k + 1) * 16, :] * (scale[k : k + 1, :] * norm)
            done[k * 16 : (k + 1) * 16, :] = block
            for ch in range(WIDTH):
                lines[ch * HALF : (ch + 1) * HALF, :] = block[:HALF, ch * LANES : (ch + 1) * LANES]
            col_out[k, h] = lines[...].astype(BF16)
        for i in range(4):
            target = jnp.where(band == 0, z + i + 1, z - i + GROW) & 7
            for s in range(2):
                block = done[pl.ds(pl.multiple_of((2 * target + s) * 16, 16), 16), :]
                for ch in range(WIDTH):
                    at = (s * WIDTH + ch) * HALF
                    row_lines[at : at + HALF, :] = block[:HALF, ch * LANES : (ch + 1) * LANES]
            row_outs[i][h] = row_lines[...].astype(BF16)


def stay(array):
    return pltpu.with_memory_space_constraint(jnp.asarray(array), pltpu.HBM)


def density_call(place, mine, other, val_e, con_e, val, con_mine, con_other, scale, interpret=False):
    second, third, (mix_hi, mix_lo) = tables()
    smem = pl.BlockSpec(memory_space=SMEM)
    vmem = pl.BlockSpec(memory_space=VMEM)
    hbm = pl.BlockSpec(memory_space=pltpu.HBM)
    anywhere = pl.BlockSpec(memory_space=pl.ANY)
    return pl.pallas_call(
        density_kernel,
        out_shape=[
            jax.ShapeDtypeStruct((N1, 2, BLOCK, LANES), BF16),
        ]
        + [jax.ShapeDtypeStruct((2, ROWBLOCK, LANES), BF16)] * 4,
        in_specs=[smem] * 3 + [hbm, hbm, anywhere] + [hbm] * 4 + [anywhere, hbm, hbm],
        out_specs=[vmem] * 5,
        scratch_shapes=[
            VMEM((16 * LINES, LANES), F32),
            VMEM((8 * LINES, LANES), F32),
            VMEM((2 * HALF * M1, KP), BF16),
            VMEM((2 * HALF * M1, NP), F32),
            VMEM((STEP, NP), BF16),
            VMEM((STEP, NP), BF16),
            VMEM((N1 * 16, NP), F32),
            VMEM((BLOCK, LANES), F32),
            VMEM((ROWBLOCK, LANES), F32),
            VMEM((16, MG), BF16),
            VMEM((4, MG), BF16),
            VMEM((4, MG), BF16),
            VMEM((M2, NP), F32),
            VMEM((M3, NP), F32),
            VMEM((N1 * 16, HALF * M1), BF16),
            VMEM((N1 * 16, HALF * M1), BF16),
            VMEM((N1, NP), F32),
            SMEM((16,), F32),
            SMEM((1024,), F32),
            pltpu.SemaphoreType.DMA((10,)),
        ],
        compiler_params=pltpu.CompilerParams(vmem_limit_bytes=34 << 20),
        interpret=interpret,
        name="density",
    )(place, mine, other, stay(val), stay(con_mine), con_other, stay(second), stay(third),
      stay(mix_hi), stay(mix_lo), scale, stay(val_e), stay(con_e))


def pack_kernel(*refs):
    blocks, out, spread = refs[:4], refs[4], refs[5]
    stride = ROWBLOCK + 4
    for v in range(8):
        spread[v * stride : v * stride + ROWBLOCK, :] = blocks[v // 2][v % 2].astype(F32)
    for ch in range(2 * WIDTH):
        for pp in range(HALF // 2):
            got = [spread[pl.ds(ch * HALF + 2 * pp + q, 8, stride=stride), :] for q in range(2)]
            out[pp * 16 : (pp + 1) * 16, ch * LANES : (ch + 1) * LANES] = jnp.concatenate(
                got, 0
            ).astype(BF16)


def pack_call(blocks, interpret=False):
    vmem = pl.BlockSpec(memory_space=VMEM)
    return pl.pallas_call(
        pack_kernel,
        out_shape=jax.ShapeDtypeStruct((8 * HALF, ROW), BF16),
        in_specs=[vmem] * 4,
        out_specs=vmem,
        scratch_shapes=[VMEM((8 * (ROWBLOCK + 4), LANES), F32)],
        compiler_params=pltpu.CompilerParams(vmem_limit_bytes=4 << 20),
        interpret=interpret,
        name="pack",
    )(*blocks)


def fetch(pieces, rows, sems):
    copies = []
    at = 0
    for i, piece in enumerate(pieces):
        size = piece.shape[0]
        copies.append(pltpu.make_async_copy(piece, rows.at[pl.ds(at, size), :], sems.at[i]))
        copies[-1].start()
        at += size
    return copies


def around(step):
    return jnp.where(step == 0, 0, jnp.where(step == 1, 3, jnp.where(step == 2, 1, 2)))


def assemble_kernel(place, *refs):
    cols = refs[:5]
    away_out, home_out, spread = refs[5:]
    me = place[0]
    band, y, x = me >> 7, (me >> 2) & 3, me & 3

    def take(first):
        for i in range(4):
            def move(q, carry, col=cols[first + i], i=i):
                for h in range(2):
                    at = pl.multiple_of((2 * i + h) * COLROWS + q * BLOCK, 4)
                    spread[pl.ds(at, BLOCK), :] = col[q, h].astype(F32)
                return carry

            lax.fori_loop(0, GCOL, move, 0, unroll=4)

    pl.when(band == 0)(lambda: take(1))
    pl.when(band == 1)(lambda: take(0))

    def assemble(j, carry):
        outer, inner = around(j >> 2), around(j & 3)
        dy = jnp.where(band == 0, outer, inner)
        dx = jnp.where(band == 0, inner, outer)
        base = (((y + dy) & 3) * 4 + ((x + dx) & 3)) * BLOCK
        weight = jnp.zeros((GROW, LANES), F32)
        for part in range(3):
            weight += spread[pl.ds(base + WIDTH * HALF + part, GROW, stride=COLROWS), :]
        other = pltpu.roll(weight, LANES - 16, 1)
        away = jnp.where(band == 0, other, weight)
        home = jnp.where(band == 0, weight, other)
        for pp in range(HALF // 2):
            ws = [
                [jnp.broadcast_to(w[:, 2 * pp + q : 2 * pp + q + 1], (GROW, LANES)) for q in range(2)]
                for w in (away, home)
            ]
            to = pl.ds(pl.multiple_of(j * GROW * HALF + pp * 16, 16), 16)
            for ch in range(WIDTH):
                got = [
                    spread[pl.ds(base + ch * HALF + 2 * pp + q, GROW, stride=COLROWS), :]
                    for q in range(2)
                ]
                where = slice(ch * LANES, (ch + 1) * LANES)
                for f, dest in enumerate((away_out, home_out)):
                    dest[to, where] = jnp.concatenate(
                        [got[0] * ws[f][0], got[1] * ws[f][1]], 0
                    ).astype(BF16)
        return carry

    lax.fori_loop(0, GCOL, assemble, 0)


def assemble_call(place, cols, interpret=False):
    vmem = pl.BlockSpec(memory_space=VMEM)
    return pl.pallas_call(
        assemble_kernel,
        out_shape=[jax.ShapeDtypeStruct((PANEL, NP), BF16)] * 2,
        in_specs=[pl.BlockSpec(memory_space=SMEM)] + [vmem] * 5,
        out_specs=[vmem] * 2,
        scratch_shapes=[VMEM((GROW * COLROWS, LANES), F32)],
        compiler_params=pltpu.CompilerParams(vmem_limit_bytes=14 << 20),
        interpret=interpret,
        name="assemble",
    )(place, *cols)


def away_kernel(weighted, *refs):
    pieces = refs[:5]
    away_out, turned_out, rows, sems = refs[5:]
    for copy in fetch(pieces, rows, sems):
        copy.wait()

    def product(m, carry):
        where = pl.ds(pl.multiple_of(m * 256, 256), 256)
        part = rows[:, where].T
        turned_out[where, :] = part
        away_out[where, :] = jnp.dot(part, weighted[...], preferred_element_type=F32).astype(BF16)
        return carry

    lax.fori_loop(0, ROW // 256, product, 0)


def away_call(weighted, pieces, interpret=False):
    vmem = pl.BlockSpec(memory_space=VMEM)
    return pl.pallas_call(
        away_kernel,
        out_shape=(
            jax.ShapeDtypeStruct((ROW, NP), BF16),
            jax.ShapeDtypeStruct((ROW, PANEL), BF16),
        ),
        in_specs=[vmem] + [pl.BlockSpec(memory_space=pl.ANY)] * 5,
        out_specs=(vmem, vmem),
        scratch_shapes=[VMEM((PANEL, ROW), BF16), pltpu.SemaphoreType.DMA((5,))],
        compiler_params=pltpu.CompilerParams(vmem_limit_bytes=20 << 20),
        interpret=interpret,
        name="away",
    )(weighted, *pieces)


def home_kernel(weighted, rows, home_out):
    def product(m, carry):
        where = pl.ds(pl.multiple_of(m * 256, 256), 256)
        home_out[where, :] = jnp.dot(rows[where, :], weighted[...], preferred_element_type=F32)
        return carry

    lax.fori_loop(0, ROW // 256, product, 0)


def home_call(weighted, rows, interpret=False):
    vmem = pl.BlockSpec(memory_space=VMEM)
    return pl.pallas_call(
        home_kernel,
        out_shape=jax.ShapeDtypeStruct((ROW, NP), F32),
        in_specs=[vmem, vmem],
        out_specs=vmem,
        compiler_params=pltpu.CompilerParams(vmem_limit_bytes=16 << 20),
        interpret=interpret,
        name="home",
    )(weighted, rows)


PLANE = ("band", "gcol_0", "gcol_1")


def turned(array, phase, step):
    pairs = []
    for band in range(2):
        along_x = (band == 0) == (phase == 0)
        for y in range(4):
            for x in range(4):
                to = (y, (x + step) % 4) if along_x else ((y + step) % 4, x)
                pairs.append((band * 16 + y * 4 + x, band * 16 + to[0] * 4 + to[1]))
    return lax.ppermute(array, PLANE, pairs)


def along(array, up_by, down_by):
    pairs = []
    for band, step in ((0, up_by), (1, -down_by if down_by is not None else None)):
        if step is not None:
            pairs += [(band * GROW + z, band * GROW + (z + step) % GROW) for z in range(GROW)]
    return lax.ppermute(array, ("band", "grow"), pairs)


def swap(array):
    return lax.ppermute(array, "band", [(0, 1), (1, 0)])


def per_device(
    valence_orbitals,
    conduction_orbitals,
    valence_energy,
    conduction_energy,
    coulomb_root,
    pair_bands,
    slot_counts,
):
    place = lax.axis_index(("band", "grow", "gcol_0", "gcol_1")).astype(jnp.int32).reshape(1)
    meta = jnp.concatenate([pair_bands.reshape(2 * SLOTS), slot_counts, jnp.zeros(7, jnp.int32)])
    other_con = swap(conduction_orbitals)
    other_meta = swap(meta)
    scale = coulomb_root.reshape(N1, NP)
    col, *rows = density_call(
        place, meta, other_meta, valence_energy, conduction_energy,
        valence_orbitals, conduction_orbitals, other_con, scale,
    )
    return exchange(place, col, rows)


def exchange(place, col, rows):
    rows = [along(rows[i], i + 1, i) for i in range(4)]
    col = lax.all_to_all(col, ("gcol_0", "gcol_1"), 0, 0, tiled=True)
    row = pack_call(rows)
    ring = [col]
    for i in range(1, 5):
        ring.append(along(ring[-1], 1, 1 if i < 4 else None))
    below, above, far = turned(row, 0, 1), turned(row, 0, -1), turned(row, 0, 2)
    line = jnp.concatenate([row, below, above, far], 0)
    half = line.shape[0] // 2
    below, above = turned(line, 1, 1), turned(line, 1, -1)
    far_a, far_b = turned(below[:half], 1, 1), turned(above[half:], 1, -1)
    weighted_away, weighted_home = assemble_call(place, ring)
    away, turned_rows = away_call(weighted_away, [line, below, above, far_a, far_b])
    received = swap(away)
    home = home_call(weighted_home, turned_rows)
    return -(home + received.astype(F32))[None]


def solution(mesh):
    finer = Mesh(
        mesh.devices.reshape(mesh.shape["band"], mesh.shape["grow"], 4, 4),
        ("band", "grow", "gcol_0", "gcol_1"),
    )
    everywhere = ("band", "grow", "gcol_0", "gcol_1")
    in_specs = (P(), P(everywhere, None), P(), P(), P(), P(None, everywhere), P(everywhere))
    return jax.shard_map(
        per_device,
        mesh=finer,
        in_specs=in_specs,
        out_specs=P("band", "grow", ("gcol_0", "gcol_1")),
        check_vma=False,
    )
```

```python
import math

import jax
import jax.numpy as jnp
import numpy as np
from jax import lax
from jax.experimental import pallas as pl
from jax.experimental.pallas import tpu as pltpu
from jax.sharding import Mesh
from jax.sharding import PartitionSpec as P


N1, N2, N3 = 16, 24, 32
M1, M2, M3 = 32, 48, 64
NP = N2 * N3
KP = M2 * M3
MG = M1 * KP
ROW = 2 * NP
TOTAL = 5120
SLOTS = 20
HALF = 10
GROW, GCOL = 8, 16
LANES = 128
CHUNKS = KP // LANES
LINES = MG // LANES + 4
PANEL = GROW * GCOL * HALF
BLOCK = 64
ROWBLOCK = 120
COLROWS = GCOL * BLOCK + 4
WIDTH = NP // LANES
STEP = 512
F32, BF16 = jnp.float32, jnp.bfloat16
VMEM = pltpu.VMEM
SMEM = pltpu.SMEM


def wave_table(keep, length):
    wave = (np.arange(keep)[:, None] - keep // 2) % length
    angles = 2.0 * np.pi * (wave * np.arange(length)[None, :] % length) / length
    return np.cos(angles) + np.sin(angles)


def halves(table):
    high = table.astype(np.float32).astype(BF16)
    return high, (table - high.astype(np.float64)).astype(np.float32).astype(BF16)


def tables():
    second = np.repeat(wave_table(N2, M2).T, N3, axis=1)
    third = np.tile(wave_table(N3, M3).T, (1, N2))
    first = wave_table(N1, M1)
    mixed = np.zeros((N1, 16, HALF, M1))
    for p in range(HALF):
        mixed[:, p, p] = first
    return (
        second.astype(np.float32),
        third.astype(np.float32),
        halves(mixed.reshape(N1 * 16, HALF * M1)),
    )


def density_kernel(
    place, mine, other, *refs,
):
    hbm, refs = refs[:10], refs[10:]
    col_out = refs[0]
    row_outs = refs[1:5]
    vals, cons, lhs, acc, table_a, table_b, done, lines, row_lines = refs[5:14]
    local, sems = refs[14:24], refs[24]
    copies = [pltpu.make_async_copy(a, b, sems.at[i]) for i, (a, b) in enumerate(zip(hbm, local))]
    for copy in copies:
        copy.start()
    val, con_mine, con_other, second, third, mix_hi, mix_lo, scale, val_e, con_e = local
    band = place[0] >> 7
    z = (place[0] >> 4) & 7
    skip = jnp.where((band == 0) == ((place[0] & 15) < 8), 1, 0)
    for copy in copies[:3]:
        copy.wait()

    def spread(a, carry):
        for t in range(CHUNKS):
            where = pl.ds(pl.multiple_of(a * KP + t * LANES, LANES), LANES)
            line = t * M1 + a
            vals[pl.ds(line, 16, stride=LINES), :] = val[:, where].astype(F32)
            cons[pl.ds(line, 8, stride=LINES), :] = jnp.concatenate(
                [con_mine[:, where].astype(F32), con_other[:, where].astype(F32)], 0
            )
        return carry

    lax.fori_loop(0, M1, spread, 0)
    for copy in copies[3:]:
        copy.wait()

    is_first = band == 0
    first_count = jnp.where(is_first, mine[2 * SLOTS], other[2 * SLOTS])
    both_count = mine[2 * SLOTS] + other[2 * SLOTS]
    lane = lax.broadcasted_iota(jnp.int32, (1, LANES), 1) & 15
    gaps = []
    for h in range(2):
        gap = jnp.ones((1, LANES), F32)
        for p in range(HALF):
            pos = h * HALF + p
            from_first = pos < first_count
            slot = jnp.minimum(jnp.where(from_first, pos, pos - first_count), SLOTS - 1)
            own = from_first == is_first
            v = jnp.where(own, mine[slot], other[slot])
            c = jnp.where(own, mine[SLOTS + slot], other[SLOTS + slot])
            gap = jnp.where(lane == p, con_e[c] - val_e[v], gap)
            v_line = v * LINES
            c_line = (jnp.where(own, 0, 4) + (c & 3)) * LINES
            top = pos * M1

            def product(t, carry):
                made = vals[pl.ds(v_line + t * M1, M1), :] * cons[pl.ds(c_line + t * M1, M1), :]
                where = pl.ds(pl.multiple_of(t * LANES, LANES), LANES)
                lhs[top : top + M1, where] = made.astype(BF16)
                return carry

            lax.fori_loop(0, CHUNKS, product, 0, unroll=6)
        gaps.append(gap)

    acc[...] = jnp.zeros_like(acc)

    def make(table, k):
        for i in range(STEP // M3):
            table[i * M3 : (i + 1) * M3, :] = (
                second[pl.ds(k * (STEP // M3) + i, 1), :] * third[...]
            ).astype(BF16)

    def add(table, k):
        where = pl.ds(pl.multiple_of(k * STEP, STEP), STEP)
        acc[...] += jnp.dot(lhs[:, where], table[...], preferred_element_type=F32)

    last = KP // STEP - 1
    make(table_a, 0)

    def transform(k, carry):
        make(table_b, 2 * k + 1)
        add(table_a, 2 * k)
        make(table_a, jnp.minimum(2 * k + 2, last))
        add(table_b, 2 * k + 1)
        return carry

    lax.fori_loop(0, KP // STEP // 2, transform, 0)
    at_lane = lax.broadcasted_iota(jnp.int32, (1, LANES), 1)
    frequency = (at_lane >> 4).astype(F32)
    norm = 1.0 / math.sqrt(MG)
    for h in range(2):
        mid = acc[h * HALF * M1 : (h + 1) * HALF * M1, :]
        mid_hi = mid.astype(BF16)
        mid_lo = (mid - mid_hi.astype(F32)).astype(BF16)
        done[...] = (
            jnp.dot(mix_hi[...], mid_hi, preferred_element_type=F32)
            + jnp.dot(mix_hi[...], mid_lo, preferred_element_type=F32)
            + jnp.dot(mix_lo[...], mid_hi, preferred_element_type=F32)
        )
        gap = gaps[h]
        live = (h * HALF + lane < both_count) & (lane < HALF) & (at_lane < 32)
        weight = jnp.where(
            live, 2.0 * gap / (gap * gap + frequency * frequency), 0.0
        ) * (1.0 / math.sqrt(TOTAL))
        w_hi = weight.astype(BF16).astype(F32)
        w_mid = (weight - w_hi).astype(BF16).astype(F32)
        lines[WIDTH * HALF : WIDTH * HALF + 1, :] = w_hi
        lines[WIDTH * HALF + 1 : WIDTH * HALF + 2, :] = w_mid
        lines[WIDTH * HALF + 2 : WIDTH * HALF + 3, :] = weight - w_hi - w_mid
        lines[WIDTH * HALF + 3 : WIDTH * HALF + 4, :] = jnp.zeros((1, LANES), F32)
        for k in range(N1):
            block = done[k * 16 : (k + 1) * 16, :] * (scale[k : k + 1, :] * norm)
            done[k * 16 : (k + 1) * 16, :] = block
            for ch in range(WIDTH):
                lines[ch * HALF : (ch + 1) * HALF, :] = block[:HALF, ch * LANES : (ch + 1) * LANES]
            col_out[k, h] = lines[...].astype(BF16)
        for i in range(4):
            target = jnp.where(band == 0, z + i + skip, z - i - skip + GROW) & 7
            for s in range(2):
                block = done[pl.ds(pl.multiple_of((2 * target + s) * 16, 16), 16), :]
                for ch in range(WIDTH):
                    at = (s * WIDTH + ch) * HALF
                    row_lines[at : at + HALF, :] = block[:HALF, ch * LANES : (ch + 1) * LANES]
            row_outs[i][h] = row_lines[...].astype(BF16)


def stay(array):
    return pltpu.with_memory_space_constraint(jnp.asarray(array), pltpu.HBM)


def density_call(place, mine, other, val_e, con_e, val, con_mine, con_other, scale, interpret=False):
    second, third, (mix_hi, mix_lo) = tables()
    smem = pl.BlockSpec(memory_space=SMEM)
    vmem = pl.BlockSpec(memory_space=VMEM)
    hbm = pl.BlockSpec(memory_space=pltpu.HBM)
    anywhere = pl.BlockSpec(memory_space=pl.ANY)
    return pl.pallas_call(
        density_kernel,
        out_shape=[
            jax.ShapeDtypeStruct((N1, 2, BLOCK, LANES), BF16),
        ]
        + [jax.ShapeDtypeStruct((2, ROWBLOCK, LANES), BF16)] * 4,
        in_specs=[smem] * 3 + [hbm, hbm, anywhere] + [hbm] * 4 + [anywhere, hbm, hbm],
        out_specs=[vmem] * 5,
        scratch_shapes=[
            VMEM((16 * LINES, LANES), F32),
            VMEM((8 * LINES, LANES), F32),
            VMEM((2 * HALF * M1, KP), BF16),
            VMEM((2 * HALF * M1, NP), F32),
            VMEM((STEP, NP), BF16),
            VMEM((STEP, NP), BF16),
            VMEM((N1 * 16, NP), F32),
            VMEM((BLOCK, LANES), F32),
            VMEM((ROWBLOCK, LANES), F32),
            VMEM((16, MG), BF16),
            VMEM((4, MG), BF16),
            VMEM((4, MG), BF16),
            VMEM((M2, NP), F32),
            VMEM((M3, NP), F32),
            VMEM((N1 * 16, HALF * M1), BF16),
            VMEM((N1 * 16, HALF * M1), BF16),
            VMEM((N1, NP), F32),
            SMEM((16,), F32),
            SMEM((1024,), F32),
            pltpu.SemaphoreType.DMA((10,)),
        ],
        compiler_params=pltpu.CompilerParams(vmem_limit_bytes=34 << 20),
        interpret=interpret,
        name="density",
    )(place, mine, other, stay(val), stay(con_mine), con_other, stay(second), stay(third),
      stay(mix_hi), stay(mix_lo), scale, stay(val_e), stay(con_e))


def pack_kernel(*refs):
    blocks, out, spread = refs[:4], refs[4], refs[5]
    stride = ROWBLOCK + 4
    for v in range(8):
        spread[v * stride : v * stride + ROWBLOCK, :] = blocks[v // 2][v % 2].astype(F32)
    for ch in range(2 * WIDTH):
        for pp in range(HALF // 2):
            got = [spread[pl.ds(ch * HALF + 2 * pp + q, 8, stride=stride), :] for q in range(2)]
            out[pp * 16 : (pp + 1) * 16, ch * LANES : (ch + 1) * LANES] = jnp.concatenate(
                got, 0
            ).astype(BF16)


def pack_call(blocks, interpret=False):
    vmem = pl.BlockSpec(memory_space=VMEM)
    return pl.pallas_call(
        pack_kernel,
        out_shape=jax.ShapeDtypeStruct((8 * HALF, ROW), BF16),
        in_specs=[vmem] * 4,
        out_specs=vmem,
        scratch_shapes=[VMEM((8 * (ROWBLOCK + 4), LANES), F32)],
        compiler_params=pltpu.CompilerParams(vmem_limit_bytes=4 << 20),
        interpret=interpret,
        name="pack",
    )(*blocks)


def fetch(pieces, rows, sems):
    copies = []
    at = 0
    for i, piece in enumerate(pieces):
        size = piece.shape[0]
        copies.append(pltpu.make_async_copy(piece, rows.at[pl.ds(at, size), :], sems.at[i]))
        copies[-1].start()
        at += size
    return copies


def around(step):
    return jnp.where(step == 0, 0, jnp.where(step == 1, 3, jnp.where(step == 2, 1, 2)))


def assemble_kernel(place, *refs):
    cols = refs[:10]
    away_out, home_out, spread = refs[10:]
    me = place[0]
    band, y, x = me >> 7, (me >> 2) & 3, me & 3

    def take(part, first):
        for i in range(4):
            col = cols[part * 5 + first + i]
            for q in range(GCOL // 2):
                for h in range(2):
                    at = (2 * i + h) * COLROWS + (part * 8 + q) * BLOCK
                    spread[at : at + BLOCK, :] = col[q, h].astype(F32)

    @pl.when(band == 0)
    def _():
        take(0, 1)
        take(1, 0)

    @pl.when(band == 1)
    def _():
        take(0, 0)
        take(1, 1)

    def assemble(j, carry):
        outer, inner = around(j >> 2), around(j & 3)
        dy = jnp.where(band == 0, outer, inner)
        dx = jnp.where(band == 0, inner, outer)
        base = (((y + dy) & 3) * 4 + ((x + dx) & 3)) * BLOCK
        weight = jnp.zeros((GROW, LANES), F32)
        for part in range(3):
            weight += spread[pl.ds(base + WIDTH * HALF + part, GROW, stride=COLROWS), :]
        other = pltpu.roll(weight, LANES - 16, 1)
        away = jnp.where(band == 0, other, weight)
        home = jnp.where(band == 0, weight, other)
        for pp in range(HALF // 2):
            ws = [
                [jnp.broadcast_to(w[:, 2 * pp + q : 2 * pp + q + 1], (GROW, LANES)) for q in range(2)]
                for w in (away, home)
            ]
            to = pl.ds(pl.multiple_of(j * GROW * HALF + pp * 16, 16), 16)
            for ch in range(WIDTH):
                got = [
                    spread[pl.ds(base + ch * HALF + 2 * pp + q, GROW, stride=COLROWS), :]
                    for q in range(2)
                ]
                where = slice(ch * LANES, (ch + 1) * LANES)
                for f, dest in enumerate((away_out, home_out)):
                    dest[to, where] = jnp.concatenate(
                        [got[0] * ws[f][0], got[1] * ws[f][1]], 0
                    ).astype(BF16)
        return carry

    lax.fori_loop(0, GCOL, assemble, 0)


def assemble_call(place, cols, interpret=False):
    vmem = pl.BlockSpec(memory_space=VMEM)
    return pl.pallas_call(
        assemble_kernel,
        out_shape=[jax.ShapeDtypeStruct((PANEL, NP), BF16)] * 2,
        in_specs=[pl.BlockSpec(memory_space=SMEM)] + [vmem] * 10,
        out_specs=[vmem] * 2,
        scratch_shapes=[VMEM((GROW * COLROWS, LANES), F32)],
        compiler_params=pltpu.CompilerParams(vmem_limit_bytes=14 << 20),
        interpret=interpret,
        name="assemble",
    )(place, *cols)


PIECES = 7


def away_kernel(weighted, *refs):
    pieces = refs[:PIECES]
    away_out, turned_out, rows, sems = refs[PIECES:]
    for copy in fetch(pieces, rows, sems):
        copy.wait()

    def product(m, carry):
        where = pl.ds(pl.multiple_of(m * 256, 256), 256)
        part = rows[:, where].T
        turned_out[where, :] = part
        away_out[where, :] = jnp.dot(part, weighted[...], preferred_element_type=F32).astype(BF16)
        return carry

    lax.fori_loop(0, ROW // 256, product, 0)


def away_call(weighted, pieces, interpret=False):
    vmem = pl.BlockSpec(memory_space=VMEM)
    return pl.pallas_call(
        away_kernel,
        out_shape=(
            jax.ShapeDtypeStruct((ROW, NP), BF16),
            jax.ShapeDtypeStruct((ROW, PANEL), BF16),
        ),
        in_specs=[vmem] + [pl.BlockSpec(memory_space=pl.ANY)] * PIECES,
        out_specs=(vmem, vmem),
        scratch_shapes=[VMEM((PANEL, ROW), BF16), pltpu.SemaphoreType.DMA((PIECES,))],
        compiler_params=pltpu.CompilerParams(vmem_limit_bytes=20 << 20),
        interpret=interpret,
        name="away",
    )(weighted, *pieces)


def home_kernel(weighted, rows, home_out):
    def product(m, carry):
        where = pl.ds(pl.multiple_of(m * 256, 256), 256)
        home_out[where, :] = jnp.dot(rows[where, :], weighted[...], preferred_element_type=F32)
        return carry

    lax.fori_loop(0, ROW // 256, product, 0)


def home_call(weighted, rows, interpret=False):
    vmem = pl.BlockSpec(memory_space=VMEM)
    return pl.pallas_call(
        home_kernel,
        out_shape=jax.ShapeDtypeStruct((ROW, NP), F32),
        in_specs=[vmem, vmem],
        out_specs=vmem,
        compiler_params=pltpu.CompilerParams(vmem_limit_bytes=16 << 20),
        interpret=interpret,
        name="home",
    )(weighted, rows)


PLANE = ("band", "gcol_0", "gcol_1")


def turned(array, phase, step):
    pairs = []
    for band in range(2):
        along_x = (band == 0) == (phase == 0)
        for y in range(4):
            for x in range(4):
                to = (y, (x + step) % 4) if along_x else ((y + step) % 4, x)
                pairs.append((band * 16 + y * 4 + x, band * 16 + to[0] * 4 + to[1]))
    return lax.ppermute(array, PLANE, pairs)


ALL = ("band", "grow", "gcol_0", "gcol_1")


def along(array, steps):
    pairs = []
    for band in range(2):
        for plane in range(GCOL):
            step = steps((band == 0) == (plane < 8), band)
            if step is None:
                continue
            for z in range(GROW):
                to = (z + step) % GROW if band == 0 else (z - step) % GROW
                pairs.append(((band * GROW + z) * GCOL + plane, (band * GROW + to) * GCOL + plane))
    return lax.ppermute(array, ALL, pairs)


def swap(array):
    return lax.ppermute(array, "band", [(0, 1), (1, 0)])


def per_device(
    valence_orbitals,
    conduction_orbitals,
    valence_energy,
    conduction_energy,
    coulomb_root,
    pair_bands,
    slot_counts,
):
    place = lax.axis_index(("band", "grow", "gcol_0", "gcol_1")).astype(jnp.int32).reshape(1)
    meta = jnp.concatenate([pair_bands.reshape(2 * SLOTS), slot_counts, jnp.zeros(7, jnp.int32)])
    other_con = swap(conduction_orbitals)
    other_meta = swap(meta)
    scale = coulomb_root.reshape(N1, NP)
    col, *rows = density_call(
        place, meta, other_meta, valence_energy, conduction_energy,
        valence_orbitals, conduction_orbitals, other_con, scale,
    )
    return exchange(place, col, rows)


def exchange(place, col, rows):
    rows = [along(rows[i], lambda f, b, i=i: i + 1 if f else i) for i in range(4)]
    col = lax.all_to_all(col, ("gcol_0", "gcol_1"), 0, 0, tiled=True)
    row = pack_call(rows)
    rings = []
    for part in range(2):
        ring = [col[part * 8 : part * 8 + 8]]
        for i in range(1, 5):
            ring.append(
                along(ring[-1], lambda f, b, i=i, part=part: 1 if i < 4 or b == part else None)
            )
        rings += ring
    below, above, far = turned(row, 0, 1), turned(row, 0, -1), turned(row, 0, 2)
    line = jnp.concatenate([row, below, above, far], 0)
    half = line.shape[0] // 2
    below_a, above_b = turned(line[:half], 1, 1), turned(line[half:], 1, -1)
    below_b, above_a = turned(line[half:], 1, 1), turned(line[:half], 1, -1)
    far_a, far_b = turned(below_a, 1, 1), turned(above_b, 1, -1)
    weighted_away, weighted_home = assemble_call(place, rings)
    pieces = [line, below_a, below_b, above_a, above_b, far_a, far_b]
    away, turned_rows = away_call(weighted_away, pieces)
    received = swap(away)
    home = home_call(weighted_home, turned_rows)
    return -(home + received.astype(F32))[None]


def solution(mesh):
    finer = Mesh(
        mesh.devices.reshape(mesh.shape["band"], mesh.shape["grow"], 4, 4),
        ("band", "grow", "gcol_0", "gcol_1"),
    )
    everywhere = ("band", "grow", "gcol_0", "gcol_1")
    in_specs = (P(), P(everywhere, None), P(), P(), P(), P(None, everywhere), P(everywhere))
    return jax.shard_map(
        per_device,
        mesh=finer,
        in_specs=in_specs,
        out_specs=P("band", "grow", ("gcol_0", "gcol_1")),
        check_vma=False,
    )
```

```python
import math

import jax
import jax.numpy as jnp
import numpy as np
from jax import lax
from jax.experimental import pallas as pl
from jax.experimental.pallas import tpu as pltpu
from jax.sharding import Mesh
from jax.sharding import PartitionSpec as P


N1, N2, N3 = 16, 24, 32
M1, M2, M3 = 32, 48, 64
NP = N2 * N3
KP = M2 * M3
MG = M1 * KP
ROW = 2 * NP
TOTAL = 5120
SLOTS = 20
HALF = 10
GROW, GCOL = 8, 16
LANES = 128
CHUNKS = KP // LANES
LINES = MG // LANES + 4
PANEL = GROW * GCOL * HALF
BLOCK = 64
ROWBLOCK = 120
COLROWS = GCOL * BLOCK + 4
WIDTH = NP // LANES
STEP = 1536
F32, BF16 = jnp.float32, jnp.bfloat16
VMEM = pltpu.VMEM
SMEM = pltpu.SMEM


def wave_table(keep, length):
    wave = (np.arange(keep)[:, None] - keep // 2) % length
    angles = 2.0 * np.pi * (wave * np.arange(length)[None, :] % length) / length
    return np.cos(angles) + np.sin(angles)


def halves(table):
    high = table.astype(np.float32).astype(BF16)
    return high, (table - high.astype(np.float64)).astype(np.float32).astype(BF16)


def tables():
    second = np.repeat(wave_table(N2, M2).T, N3, axis=1)
    third = np.tile(wave_table(N3, M3).T, (1, N2))
    first = wave_table(N1, M1)
    mixed = np.zeros((N1, 16, HALF, M1))
    for p in range(HALF):
        mixed[:, p, p] = first
    return (
        second.astype(np.float32),
        third.astype(np.float32),
        halves(mixed.reshape(N1 * 16, HALF * M1)),
    )


def ready_kernel(source, vals, val, sems):
    count = 4
    size = MG // count
    copies = []
    for i in range(count):
        where = pl.ds(i * size, size)
        copies.append(pltpu.make_async_copy(source.at[:, where], val.at[:, where], sems.at[i]))
        copies[-1].start()
    for i, copy in enumerate(copies):
        copy.wait()

        def spread(a, carry):
            for t in range(CHUNKS):
                where = pl.ds(pl.multiple_of(a * KP + t * LANES, LANES), LANES)
                vals[pl.ds(t * M1 + a, 16, stride=LINES), :] = val[:, where].astype(F32)
            return carry

        lax.fori_loop(i * M1 // count, (i + 1) * M1 // count, spread, 0)


def ready_call(val, interpret=False):
    return pl.pallas_call(
        ready_kernel,
        out_shape=jax.ShapeDtypeStruct((16 * LINES, LANES), F32),
        in_specs=[pl.BlockSpec(memory_space=pltpu.HBM)],
        out_specs=pl.BlockSpec(memory_space=VMEM),
        scratch_shapes=[VMEM((16, MG), BF16), pltpu.SemaphoreType.DMA((4,))],
        compiler_params=pltpu.CompilerParams(vmem_limit_bytes=12 << 20),
        interpret=interpret,
        name="ready",
    )(stay(val))


def density_kernel(
    place, mine, other, my_count, other_count, vals, *refs,
):
    hbm, refs = refs[:9], refs[9:]
    col_out = refs[0]
    row_outs = refs[1:5]
    cons, lhs, acc, table_a, table_b, done, lines, row_lines = refs[5:13]
    local, sems = refs[13:22], refs[22]
    copies = [pltpu.make_async_copy(a, b, sems.at[i]) for i, (a, b) in enumerate(zip(hbm, local))]
    for copy in copies:
        copy.start()
    con_mine, con_other, second, third, mix_hi, mix_lo, scale, val_e, con_e = local
    band = place[0] >> 7
    z = (place[0] >> 4) & 7
    skip = jnp.where((band == 0) == ((place[0] & 15) < 8), 1, 0)
    for copy in copies[:2]:
        copy.wait()

    def spread(a, carry):
        for t in range(CHUNKS):
            where = pl.ds(pl.multiple_of(a * KP + t * LANES, LANES), LANES)
            line = t * M1 + a
            cons[pl.ds(line, 8, stride=LINES), :] = jnp.concatenate(
                [con_mine[:, where].astype(F32), con_other[:, where].astype(F32)], 0
            )
        return carry

    lax.fori_loop(0, M1, spread, 0)
    for copy in copies[2:]:
        copy.wait()

    is_first = band == 0
    first_count = jnp.where(is_first, my_count[0], other_count[0])
    both_count = my_count[0] + other_count[0]
    lane = lax.broadcasted_iota(jnp.int32, (1, LANES), 1) & 15
    gaps = []
    for h in range(2):
        gap = jnp.ones((1, LANES), F32)
        for p in range(HALF):
            pos = h * HALF + p
            from_first = pos < first_count
            slot = jnp.minimum(jnp.where(from_first, pos, pos - first_count), SLOTS - 1)
            own = from_first == is_first
            v = jnp.where(own, mine[0, slot], other[0, slot])
            c = jnp.where(own, mine[1, slot], other[1, slot])
            gap = jnp.where(lane == p, con_e[c] - val_e[v], gap)
            v_line = v * LINES
            c_line = (jnp.where(own, 0, 4) + (c & 3)) * LINES
            top = pos * M1

            def product(t, carry):
                made = vals[pl.ds(v_line + t * M1, M1), :] * cons[pl.ds(c_line + t * M1, M1), :]
                where = pl.ds(pl.multiple_of(t * LANES, LANES), LANES)
                lhs[top : top + M1, where] = made.astype(BF16)
                return carry

            lax.fori_loop(0, CHUNKS, product, 0, unroll=6)
        gaps.append(gap)

    acc[...] = jnp.zeros_like(acc)

    def make(table, k):
        for i in range(STEP // M3):
            table[i * M3 : (i + 1) * M3, :] = (
                second[pl.ds(k * (STEP // M3) + i, 1), :] * third[...]
            ).astype(BF16)

    def add(table, k):
        where = pl.ds(pl.multiple_of(k * STEP, STEP), STEP)
        acc[...] += jnp.dot(lhs[:, where], table[...], preferred_element_type=F32)

    last = KP // STEP - 1
    make(table_a, 0)

    def transform(k, carry):
        make(table_b, 2 * k + 1)
        add(table_a, 2 * k)
        make(table_a, jnp.minimum(2 * k + 2, last))
        add(table_b, 2 * k + 1)
        return carry

    lax.fori_loop(0, KP // STEP // 2, transform, 0)
    at_lane = lax.broadcasted_iota(jnp.int32, (1, LANES), 1)
    frequency = (at_lane >> 4).astype(F32)
    norm = 1.0 / math.sqrt(MG)
    for h in range(2):
        mid = acc[h * HALF * M1 : (h + 1) * HALF * M1, :]
        mid_hi = mid.astype(BF16)
        mid_lo = (mid - mid_hi.astype(F32)).astype(BF16)
        done[...] = (
            jnp.dot(mix_hi[...], mid_hi, preferred_element_type=F32)
            + jnp.dot(mix_hi[...], mid_lo, preferred_element_type=F32)
            + jnp.dot(mix_lo[...], mid_hi, preferred_element_type=F32)
        )
        gap = gaps[h]
        live = (h * HALF + lane < both_count) & (lane < HALF) & (at_lane < 32)
        weight = jnp.where(
            live, 2.0 * gap / (gap * gap + frequency * frequency), 0.0
        ) * (1.0 / math.sqrt(TOTAL))
        w_hi = weight.astype(BF16).astype(F32)
        w_mid = (weight - w_hi).astype(BF16).astype(F32)
        lines[WIDTH * HALF : WIDTH * HALF + 1, :] = w_hi
        lines[WIDTH * HALF + 1 : WIDTH * HALF + 2, :] = w_mid
        lines[WIDTH * HALF + 2 : WIDTH * HALF + 3, :] = weight - w_hi - w_mid
        lines[WIDTH * HALF + 3 : WIDTH * HALF + 4, :] = jnp.zeros((1, LANES), F32)
        for k in range(N1):
            block = done[k * 16 : (k + 1) * 16, :] * (scale[:, k * NP : (k + 1) * NP] * norm)
            done[k * 16 : (k + 1) * 16, :] = block
            for ch in range(WIDTH):
                lines[ch * HALF : (ch + 1) * HALF, :] = block[:HALF, ch * LANES : (ch + 1) * LANES]
            col_out[k, h] = lines[...].astype(BF16)
        for i in range(4):
            target = jnp.where(band == 0, z + i + skip, z - i - skip + GROW) & 7
            for s in range(2):
                block = done[pl.ds(pl.multiple_of((2 * target + s) * 16, 16), 16), :]
                for ch in range(WIDTH):
                    at = (s * WIDTH + ch) * HALF
                    row_lines[at : at + HALF, :] = block[:HALF, ch * LANES : (ch + 1) * LANES]
            row_outs[i][h] = row_lines[...].astype(BF16)


def stay(array):
    return pltpu.with_memory_space_constraint(jnp.asarray(array), pltpu.HBM)


def density_call(
    place, mine, other, my_count, other_count, val_e, con_e, vals, con_mine, con_other, scale, interpret=False
):
    second, third, (mix_hi, mix_lo) = tables()
    smem = pl.BlockSpec(memory_space=SMEM)
    vmem = pl.BlockSpec(memory_space=VMEM)
    hbm = pl.BlockSpec(memory_space=pltpu.HBM)
    anywhere = pl.BlockSpec(memory_space=pl.ANY)
    return pl.pallas_call(
        density_kernel,
        out_shape=[
            jax.ShapeDtypeStruct((N1, 2, BLOCK, LANES), BF16),
        ]
        + [jax.ShapeDtypeStruct((2, ROWBLOCK, LANES), BF16)] * 4,
        in_specs=[smem] * 5 + [vmem, hbm, anywhere] + [hbm] * 7,
        out_specs=[vmem] * 5,
        scratch_shapes=[
            VMEM((8 * LINES, LANES), F32),
            VMEM((2 * HALF * M1, KP), BF16),
            VMEM((2 * HALF * M1, NP), F32),
            VMEM((STEP, NP), BF16),
            VMEM((STEP, NP), BF16),
            VMEM((N1 * 16, NP), F32),
            VMEM((BLOCK, LANES), F32),
            VMEM((ROWBLOCK, LANES), F32),
            VMEM((4, MG), BF16),
            VMEM((4, MG), BF16),
            VMEM((M2, NP), F32),
            VMEM((M3, NP), F32),
            VMEM((N1 * 16, HALF * M1), BF16),
            VMEM((N1 * 16, HALF * M1), BF16),
            VMEM((1, N1 * NP), F32),
            SMEM((16,), F32),
            SMEM((1024,), F32),
            pltpu.SemaphoreType.DMA((9,)),
        ],
        compiler_params=pltpu.CompilerParams(vmem_limit_bytes=26 << 20),
        interpret=interpret,
        name="density",
    )(place, mine, other, my_count, other_count, vals, stay(con_mine), con_other, stay(second), stay(third),
      stay(mix_hi), stay(mix_lo), stay(scale), stay(val_e), stay(con_e))


def pack_kernel(*refs):
    blocks, out, spread = refs[:4], refs[4], refs[5]
    stride = ROWBLOCK + 4
    for v in range(8):
        spread[v * stride : v * stride + ROWBLOCK, :] = blocks[v // 2][v % 2].astype(F32)
    for ch in range(2 * WIDTH):
        for pp in range(HALF // 2):
            got = [spread[pl.ds(ch * HALF + 2 * pp + q, 8, stride=stride), :] for q in range(2)]
            out[pp * 16 : (pp + 1) * 16, ch * LANES : (ch + 1) * LANES] = jnp.concatenate(
                got, 0
            ).astype(BF16)


def pack_call(blocks, interpret=False):
    vmem = pl.BlockSpec(memory_space=VMEM)
    return pl.pallas_call(
        pack_kernel,
        out_shape=jax.ShapeDtypeStruct((8 * HALF, ROW), BF16),
        in_specs=[vmem] * 4,
        out_specs=vmem,
        scratch_shapes=[VMEM((8 * (ROWBLOCK + 4), LANES), F32)],
        compiler_params=pltpu.CompilerParams(vmem_limit_bytes=4 << 20),
        interpret=interpret,
        name="pack",
    )(*blocks)


def fetch(pieces, rows, sems):
    copies = []
    at = 0
    for i, piece in enumerate(pieces):
        size = piece.shape[0]
        copies.append(pltpu.make_async_copy(piece, rows.at[pl.ds(at, size), :], sems.at[i]))
        copies[-1].start()
        at += size
    return copies


def around(step):
    return jnp.where(step == 0, 0, jnp.where(step == 1, 3, jnp.where(step == 2, 1, 2)))


def assemble_kernel(place, *refs):
    cols = refs[:10]
    away_out, home_out, spread = refs[10:]
    me = place[0]
    band, y, x = me >> 7, (me >> 2) & 3, me & 3

    def take(part, first):
        for i in range(4):
            col = cols[part * 5 + first + i]
            for q in range(GCOL // 2):
                for h in range(2):
                    at = (2 * i + h) * COLROWS + (part * 8 + q) * BLOCK
                    spread[at : at + BLOCK, :] = col[q, h].astype(F32)

    @pl.when(band == 0)
    def _():
        take(0, 1)
        take(1, 0)

    @pl.when(band == 1)
    def _():
        take(0, 0)
        take(1, 1)

    def assemble(j, carry):
        outer, inner = around(j >> 2), around(j & 3)
        dy = jnp.where(band == 0, outer, inner)
        dx = jnp.where(band == 0, inner, outer)
        base = (((y + dy) & 3) * 4 + ((x + dx) & 3)) * BLOCK
        weight = jnp.zeros((GROW, LANES), F32)
        for part in range(3):
            weight += spread[pl.ds(base + WIDTH * HALF + part, GROW, stride=COLROWS), :]
        other = pltpu.roll(weight, LANES - 16, 1)
        away = jnp.where(band == 0, other, weight)
        home = jnp.where(band == 0, weight, other)
        for pp in range(HALF // 2):
            ws = [
                [jnp.broadcast_to(w[:, 2 * pp + q : 2 * pp + q + 1], (GROW, LANES)) for q in range(2)]
                for w in (away, home)
            ]
            to = pl.ds(pl.multiple_of(j * GROW * HALF + pp * 16, 16), 16)
            for ch in range(WIDTH):
                got = [
                    spread[pl.ds(base + ch * HALF + 2 * pp + q, GROW, stride=COLROWS), :]
                    for q in range(2)
                ]
                where = slice(ch * LANES, (ch + 1) * LANES)
                for f, dest in enumerate((away_out, home_out)):
                    dest[to, where] = jnp.concatenate(
                        [got[0] * ws[f][0], got[1] * ws[f][1]], 0
                    ).astype(BF16)
        return carry

    lax.fori_loop(0, GCOL, assemble, 0)


def assemble_call(place, cols, interpret=False):
    vmem = pl.BlockSpec(memory_space=VMEM)
    return pl.pallas_call(
        assemble_kernel,
        out_shape=[jax.ShapeDtypeStruct((PANEL, NP), BF16)] * 2,
        in_specs=[pl.BlockSpec(memory_space=SMEM)] + [vmem] * 10,
        out_specs=[vmem] * 2,
        scratch_shapes=[VMEM((GROW * COLROWS, LANES), F32)],
        compiler_params=pltpu.CompilerParams(vmem_limit_bytes=14 << 20),
        interpret=interpret,
        name="assemble",
    )(place, *cols)


PIECES = 8


def away_kernel(weighted, *refs):
    pieces = refs[:PIECES]
    away_out, turned_out, rows, sems = refs[PIECES:]
    for copy in fetch(pieces, rows, sems):
        copy.wait()

    def product(m, carry):
        where = pl.ds(pl.multiple_of(m * 256, 256), 256)
        part = rows[:, where].T
        turned_out[where, :] = part
        away_out[where, :] = jnp.dot(part, weighted[...], preferred_element_type=F32).astype(BF16)
        return carry

    lax.fori_loop(0, ROW // 256, product, 0)


def away_call(weighted, pieces, interpret=False):
    vmem = pl.BlockSpec(memory_space=VMEM)
    return pl.pallas_call(
        away_kernel,
        out_shape=(
            jax.ShapeDtypeStruct((ROW, NP), BF16),
            jax.ShapeDtypeStruct((ROW, PANEL), BF16),
        ),
        in_specs=[vmem] + [pl.BlockSpec(memory_space=pl.ANY)] * PIECES,
        out_specs=(vmem, vmem),
        scratch_shapes=[VMEM((PANEL, ROW), BF16), pltpu.SemaphoreType.DMA((PIECES,))],
        compiler_params=pltpu.CompilerParams(vmem_limit_bytes=20 << 20),
        interpret=interpret,
        name="away",
    )(weighted, *pieces)


def home_kernel(weighted, rows, home_out):
    def product(m, carry):
        where = pl.ds(pl.multiple_of(m * 256, 256), 256)
        home_out[where, :] = jnp.dot(rows[where, :], weighted[...], preferred_element_type=F32)
        return carry

    lax.fori_loop(0, ROW // 256, product, 0)


def home_call(weighted, rows, interpret=False):
    vmem = pl.BlockSpec(memory_space=VMEM)
    return pl.pallas_call(
        home_kernel,
        out_shape=jax.ShapeDtypeStruct((ROW, NP), F32),
        in_specs=[vmem, vmem],
        out_specs=vmem,
        compiler_params=pltpu.CompilerParams(vmem_limit_bytes=16 << 20),
        interpret=interpret,
        name="home",
    )(weighted, rows)


PLANE = ("band", "gcol_0", "gcol_1")


def turned(array, phase, step):
    pairs = []
    for band in range(2):
        along_x = (band == 0) == (phase == 0)
        for y in range(4):
            for x in range(4):
                to = (y, (x + step) % 4) if along_x else ((y + step) % 4, x)
                pairs.append((band * 16 + y * 4 + x, band * 16 + to[0] * 4 + to[1]))
    return lax.ppermute(array, PLANE, pairs)


ALL = ("band", "grow", "gcol_0", "gcol_1")


def along(array, steps):
    pairs = []
    for band in range(2):
        for plane in range(GCOL):
            step = steps((band == 0) == (plane < 8), band)
            if step is None:
                continue
            for z in range(GROW):
                to = (z + step) % GROW if band == 0 else (z - step) % GROW
                pairs.append(((band * GROW + z) * GCOL + plane, (band * GROW + to) * GCOL + plane))
    return lax.ppermute(array, ALL, pairs)


def swap(array):
    return lax.ppermute(array, "band", [(0, 1), (1, 0)])


def per_device(
    valence_orbitals,
    conduction_orbitals,
    valence_energy,
    conduction_energy,
    coulomb_root,
    pair_bands,
    slot_counts,
):
    place = lax.axis_index(("band", "grow", "gcol_0", "gcol_1")).astype(jnp.int32).reshape(1)
    other_con = swap(conduction_orbitals)
    other_pairs, other_count = swap(pair_bands), swap(slot_counts)
    vals = ready_call(valence_orbitals)
    col, *rows = density_call(
        place, pair_bands, other_pairs, slot_counts, other_count, valence_energy, conduction_energy,
        vals, conduction_orbitals, other_con, coulomb_root.reshape(1, N1 * NP),
    )
    return exchange(place, col, rows)


def exchange(place, col, rows):
    rows = [along(rows[i], lambda f, b, i=i: i + 1 if f else i) for i in range(4)]
    col = lax.all_to_all(col, ("gcol_0", "gcol_1"), 0, 0, tiled=True)
    row = pack_call(rows)
    parts = [col[:8], col[8:]]
    rings = []
    for part in range(2):
        ring = [parts[part]]
        for i in range(1, 5):
            ring.append(
                along(ring[-1], lambda f, b, i=i, part=part: 1 if i < 4 or b == part else None)
            )
        rings += ring
    half = row.shape[0] // 2
    below, above = turned(row, 0, 1), turned(row, 0, -1)
    far_a, far_b = turned(below[:half], 0, 1), turned(above[half:], 0, -1)
    first = jnp.concatenate([row, below], 0)
    second = jnp.concatenate([above, far_a, far_b], 0)
    below_a, above_a = turned(first, 1, 1), turned(first, 1, -1)
    above_b, below_b = turned(second, 1, -1), turned(second, 1, 1)
    far_a, far_b = turned(below_a, 1, 1), turned(above_b, 1, -1)
    weighted_away, weighted_home = assemble_call(place, rings)
    pieces = [first, second, below_a, below_b, above_a, above_b, far_a, far_b]
    away, turned_rows = away_call(weighted_away, pieces)
    received = swap(away)
    home = home_call(weighted_home, turned_rows)
    return -(home + received.astype(F32))[None]


def solution(mesh):
    finer = Mesh(
        mesh.devices.reshape(mesh.shape["band"], mesh.shape["grow"], 4, 4),
        ("band", "grow", "gcol_0", "gcol_1"),
    )
    everywhere = ("band", "grow", "gcol_0", "gcol_1")
    in_specs = (P(), P(everywhere, None), P(), P(), P(), P(None, everywhere), P(everywhere))
    return jax.shard_map(
        per_device,
        mesh=finer,
        in_specs=in_specs,
        out_specs=P("band", "grow", ("gcol_0", "gcol_1")),
        check_vma=False,
    )
```

```python
import math

import jax
import jax.numpy as jnp
import numpy as np
from jax import lax
from jax.experimental import pallas as pl
from jax.experimental.pallas import tpu as pltpu
from jax.sharding import Mesh
from jax.sharding import PartitionSpec as P


N1, N2, N3 = 16, 24, 32
M1, M2, M3 = 32, 48, 64
NP = N2 * N3
KP = M2 * M3
MG = M1 * KP
ROW = 2 * NP
TOTAL = 5120
SLOTS = 20
HALF = 10
GROW, GCOL = 8, 16
LANES = 128
CHUNKS = KP // LANES
LINES = MG // LANES + 4
PANEL = GROW * GCOL * HALF
BLOCK = 64
ROWBLOCK = 120
COLROWS = GCOL * BLOCK + 4
WIDTH = NP // LANES
STEP = 512
F32, BF16 = jnp.float32, jnp.bfloat16
VMEM = pltpu.VMEM
SMEM = pltpu.SMEM


def wave_table(keep, length):
    wave = (np.arange(keep)[:, None] - keep // 2) % length
    angles = 2.0 * np.pi * (wave * np.arange(length)[None, :] % length) / length
    return np.cos(angles) + np.sin(angles)


def halves(table):
    high = table.astype(np.float32).astype(BF16)
    return high, (table - high.astype(np.float64)).astype(np.float32).astype(BF16)


def tables():
    second = np.repeat(wave_table(N2, M2).T, N3, axis=1)
    third = np.tile(wave_table(N3, M3).T, (1, N2))
    first = wave_table(N1, M1)
    mixed = np.zeros((N1, 16, HALF, M1))
    for p in range(HALF):
        mixed[:, p, p] = first
    return (
        second.astype(np.float32),
        third.astype(np.float32),
        halves(mixed.reshape(N1 * 16, HALF * M1)),
    )


def ready_kernel(source, vals, val, sems):
    count = 4
    size = MG // count
    copies = []
    for i in range(count):
        where = pl.ds(i * size, size)
        copies.append(pltpu.make_async_copy(source.at[:, where], val.at[:, where], sems.at[i]))
        copies[-1].start()
    for i, copy in enumerate(copies):
        copy.wait()

        def spread(a, carry):
            for t in range(CHUNKS):
                where = pl.ds(pl.multiple_of(a * KP + t * LANES, LANES), LANES)
                vals[pl.ds(t * M1 + a, 16, stride=LINES), :] = val[:, where].astype(F32)
            return carry

        lax.fori_loop(i * M1 // count, (i + 1) * M1 // count, spread, 0)


def ready_call(val, interpret=False):
    return pl.pallas_call(
        ready_kernel,
        out_shape=jax.ShapeDtypeStruct((16 * LINES, LANES), F32),
        in_specs=[pl.BlockSpec(memory_space=pltpu.HBM)],
        out_specs=pl.BlockSpec(memory_space=VMEM),
        scratch_shapes=[VMEM((16, MG), BF16), pltpu.SemaphoreType.DMA((4,))],
        compiler_params=pltpu.CompilerParams(vmem_limit_bytes=12 << 20),
        interpret=interpret,
        name="ready",
    )(stay(val))


def density_kernel(
    place, mine, other, my_count, other_count, vals, *refs,
):
    hbm, refs = refs[:9], refs[9:]
    col_out = refs[0]
    row_outs = refs[1:5]
    cons, lhs, acc, table_a, table_b, done, lines, row_lines = refs[5:13]
    local, sems = refs[13:22], refs[22]
    copies = [pltpu.make_async_copy(a, b, sems.at[i]) for i, (a, b) in enumerate(zip(hbm, local))]
    for copy in copies:
        copy.start()
    con_mine, con_other, second, third, mix_hi, mix_lo, scale, val_e, con_e = local
    band = place[0] >> 7
    z = (place[0] >> 4) & 7
    skip = jnp.where((band == 0) == ((place[0] & 15) < 8), 1, 0)
    for copy in copies[:2]:
        copy.wait()

    def spread(a, carry):
        for t in range(CHUNKS):
            where = pl.ds(pl.multiple_of(a * KP + t * LANES, LANES), LANES)
            line = t * M1 + a
            cons[pl.ds(line, 8, stride=LINES), :] = jnp.concatenate(
                [con_mine[:, where].astype(F32), con_other[:, where].astype(F32)], 0
            )
        return carry

    lax.fori_loop(0, M1, spread, 0)
    for copy in copies[2:]:
        copy.wait()

    is_first = band == 0
    first_count = jnp.where(is_first, my_count[0], other_count[0])
    both_count = my_count[0] + other_count[0]
    lane = lax.broadcasted_iota(jnp.int32, (1, LANES), 1) & 15
    gaps = []
    for h in range(2):
        gap = jnp.ones((1, LANES), F32)
        for p in range(HALF):
            pos = h * HALF + p
            from_first = pos < first_count
            slot = jnp.minimum(jnp.where(from_first, pos, pos - first_count), SLOTS - 1)
            own = from_first == is_first
            v = jnp.where(own, mine[0, slot], other[0, slot])
            c = jnp.where(own, mine[1, slot], other[1, slot])
            gap = jnp.where(lane == p, con_e[c] - val_e[v], gap)
            v_line = v * LINES
            c_line = (jnp.where(own, 0, 4) + (c & 3)) * LINES
            top = pos * M1

            def product(t, carry):
                made = vals[pl.ds(v_line + t * M1, M1), :] * cons[pl.ds(c_line + t * M1, M1), :]
                where = pl.ds(pl.multiple_of(t * LANES, LANES), LANES)
                lhs[top : top + M1, where] = made.astype(BF16)
                return carry

            lax.fori_loop(0, CHUNKS, product, 0, unroll=6)
        gaps.append(gap)

    acc[...] = jnp.zeros_like(acc)

    def make(table, k):
        for i in range(STEP // M3):
            table[i * M3 : (i + 1) * M3, :] = (
                second[pl.ds(k * (STEP // M3) + i, 1), :] * third[...]
            ).astype(BF16)

    def add(table, k):
        where = pl.ds(pl.multiple_of(k * STEP, STEP), STEP)
        acc[...] += jnp.dot(lhs[:, where], table[...], preferred_element_type=F32)

    last = KP // STEP - 1
    make(table_a, 0)

    def transform(k, carry):
        make(table_b, 2 * k + 1)
        add(table_a, 2 * k)
        make(table_a, jnp.minimum(2 * k + 2, last))
        add(table_b, 2 * k + 1)
        return carry

    lax.fori_loop(0, KP // STEP // 2, transform, 0)
    at_lane = lax.broadcasted_iota(jnp.int32, (1, LANES), 1)
    frequency = (at_lane >> 4).astype(F32)
    norm = 1.0 / math.sqrt(MG)
    for h in range(2):
        mid = acc[h * HALF * M1 : (h + 1) * HALF * M1, :]
        mid_hi = mid.astype(BF16)
        mid_lo = (mid - mid_hi.astype(F32)).astype(BF16)
        done[...] = (
            jnp.dot(mix_hi[...], mid_hi, preferred_element_type=F32)
            + jnp.dot(mix_hi[...], mid_lo, preferred_element_type=F32)
            + jnp.dot(mix_lo[...], mid_hi, preferred_element_type=F32)
        )
        gap = gaps[h]
        live = (h * HALF + lane < both_count) & (lane < HALF) & (at_lane < 32)
        weight = jnp.where(
            live, 2.0 * gap / (gap * gap + frequency * frequency), 0.0
        ) * (1.0 / math.sqrt(TOTAL))
        w_hi = weight.astype(BF16).astype(F32)
        w_mid = (weight - w_hi).astype(BF16).astype(F32)
        lines[WIDTH * HALF : WIDTH * HALF + 1, :] = w_hi
        lines[WIDTH * HALF + 1 : WIDTH * HALF + 2, :] = w_mid
        lines[WIDTH * HALF + 2 : WIDTH * HALF + 3, :] = weight - w_hi - w_mid
        lines[WIDTH * HALF + 3 : WIDTH * HALF + 4, :] = jnp.zeros((1, LANES), F32)
        for k in range(N1):
            block = done[k * 16 : (k + 1) * 16, :] * (scale[:, k * NP : (k + 1) * NP] * norm)
            done[k * 16 : (k + 1) * 16, :] = block
            for ch in range(WIDTH):
                lines[ch * HALF : (ch + 1) * HALF, :] = block[:HALF, ch * LANES : (ch + 1) * LANES]
            col_out[k, h] = lines[...].astype(BF16)
        for i in range(4):
            target = jnp.where(band == 0, z + i + skip, z - i - skip + GROW) & 7
            for s in range(2):
                block = done[pl.ds(pl.multiple_of((2 * target + s) * 16, 16), 16), :]
                for ch in range(WIDTH):
                    at = (s * WIDTH + ch) * HALF
                    row_lines[at : at + HALF, :] = block[:HALF, ch * LANES : (ch + 1) * LANES]
            row_outs[i][h] = row_lines[...].astype(BF16)


def stay(array):
    return pltpu.with_memory_space_constraint(jnp.asarray(array), pltpu.HBM)


def density_call(
    place, mine, other, my_count, other_count, val_e, con_e, vals, con_mine, con_other, scale, interpret=False
):
    second, third, (mix_hi, mix_lo) = tables()
    smem = pl.BlockSpec(memory_space=SMEM)
    vmem = pl.BlockSpec(memory_space=VMEM)
    hbm = pl.BlockSpec(memory_space=pltpu.HBM)
    anywhere = pl.BlockSpec(memory_space=pl.ANY)
    return pl.pallas_call(
        density_kernel,
        out_shape=[
            jax.ShapeDtypeStruct((N1, 2, BLOCK, LANES), BF16),
        ]
        + [jax.ShapeDtypeStruct((2, ROWBLOCK, LANES), BF16)] * 4,
        in_specs=[smem] * 5 + [vmem, hbm, anywhere] + [hbm] * 7,
        out_specs=[vmem] * 5,
        scratch_shapes=[
            VMEM((8 * LINES, LANES), F32),
            VMEM((2 * HALF * M1, KP), BF16),
            VMEM((2 * HALF * M1, NP), F32),
            VMEM((STEP, NP), BF16),
            VMEM((STEP, NP), BF16),
            VMEM((N1 * 16, NP), F32),
            VMEM((BLOCK, LANES), F32),
            VMEM((ROWBLOCK, LANES), F32),
            VMEM((4, MG), BF16),
            VMEM((4, MG), BF16),
            VMEM((M2, NP), F32),
            VMEM((M3, NP), F32),
            VMEM((N1 * 16, HALF * M1), BF16),
            VMEM((N1 * 16, HALF * M1), BF16),
            VMEM((1, N1 * NP), F32),
            SMEM((16,), F32),
            SMEM((1024,), F32),
            pltpu.SemaphoreType.DMA((9,)),
        ],
        compiler_params=pltpu.CompilerParams(vmem_limit_bytes=26 << 20),
        interpret=interpret,
        name="density",
    )(place, mine, other, my_count, other_count, vals, stay(con_mine), con_other, stay(second), stay(third),
      stay(mix_hi), stay(mix_lo), stay(scale), stay(val_e), stay(con_e))


def pack_kernel(*refs):
    blocks, out, spread = refs[:4], refs[4], refs[5]
    stride = ROWBLOCK + 4
    for v in range(8):
        spread[v * stride : v * stride + ROWBLOCK, :] = blocks[v // 2][v % 2].astype(F32)
    for ch in range(2 * WIDTH):
        for pp in range(HALF // 2):
            got = [spread[pl.ds(ch * HALF + 2 * pp + q, 8, stride=stride), :] for q in range(2)]
            out[pp * 16 : (pp + 1) * 16, ch * LANES : (ch + 1) * LANES] = jnp.concatenate(
                got, 0
            ).astype(BF16)


def pack_call(blocks, interpret=False):
    vmem = pl.BlockSpec(memory_space=VMEM)
    return pl.pallas_call(
        pack_kernel,
        out_shape=jax.ShapeDtypeStruct((8 * HALF, ROW), BF16),
        in_specs=[vmem] * 4,
        out_specs=vmem,
        scratch_shapes=[VMEM((8 * (ROWBLOCK + 4), LANES), F32)],
        compiler_params=pltpu.CompilerParams(vmem_limit_bytes=4 << 20),
        interpret=interpret,
        name="pack",
    )(*blocks)


def fetch(pieces, rows, sems):
    copies = []
    at = 0
    for i, piece in enumerate(pieces):
        size = piece.shape[0]
        copies.append(pltpu.make_async_copy(piece, rows.at[pl.ds(at, size), :], sems.at[i]))
        copies[-1].start()
        at += size
    return copies


def around(step):
    return jnp.where(step == 0, 0, jnp.where(step == 1, 3, jnp.where(step == 2, 1, 2)))


def assemble_kernel(place, *refs):
    cols = refs[:10]
    away_out, home_out, spread = refs[10:]
    me = place[0]
    band, y, x = me >> 7, (me >> 2) & 3, me & 3

    def take(part, first):
        for i in range(4):
            col = cols[part * 5 + first + i]
            for q in range(GCOL // 2):
                for h in range(2):
                    at = (2 * i + h) * COLROWS + (part * 8 + q) * BLOCK
                    spread[at : at + BLOCK, :] = col[q, h].astype(F32)

    @pl.when(band == 0)
    def _():
        take(0, 1)
        take(1, 0)

    @pl.when(band == 1)
    def _():
        take(0, 0)
        take(1, 1)

    def assemble(j, carry):
        outer, inner = around(j >> 2), around(j & 3)
        dy = jnp.where(band == 0, outer, inner)
        dx = jnp.where(band == 0, inner, outer)
        base = (((y + dy) & 3) * 4 + ((x + dx) & 3)) * BLOCK
        weight = jnp.zeros((GROW, LANES), F32)
        for part in range(3):
            weight += spread[pl.ds(base + WIDTH * HALF + part, GROW, stride=COLROWS), :]
        other = pltpu.roll(weight, LANES - 16, 1)
        away = jnp.where(band == 0, other, weight)
        home = jnp.where(band == 0, weight, other)
        for pp in range(HALF // 2):
            ws = [
                [jnp.broadcast_to(w[:, 2 * pp + q : 2 * pp + q + 1], (GROW, LANES)) for q in range(2)]
                for w in (away, home)
            ]
            to = pl.ds(pl.multiple_of(j * GROW * HALF + pp * 16, 16), 16)
            for ch in range(WIDTH):
                got = [
                    spread[pl.ds(base + ch * HALF + 2 * pp + q, GROW, stride=COLROWS), :]
                    for q in range(2)
                ]
                where = slice(ch * LANES, (ch + 1) * LANES)
                for f, dest in enumerate((away_out, home_out)):
                    dest[to, where] = jnp.concatenate(
                        [got[0] * ws[f][0], got[1] * ws[f][1]], 0
                    ).astype(BF16)
        return carry

    lax.fori_loop(0, GCOL, assemble, 0)


def assemble_call(place, cols, interpret=False):
    vmem = pl.BlockSpec(memory_space=VMEM)
    return pl.pallas_call(
        assemble_kernel,
        out_shape=[jax.ShapeDtypeStruct((PANEL, NP), BF16)] * 2,
        in_specs=[pl.BlockSpec(memory_space=SMEM)] + [vmem] * 10,
        out_specs=[vmem] * 2,
        scratch_shapes=[VMEM((GROW * COLROWS, LANES), F32)],
        compiler_params=pltpu.CompilerParams(vmem_limit_bytes=14 << 20),
        interpret=interpret,
        name="assemble",
    )(place, *cols)


PIECES = 5


def away_kernel(weighted, *refs):
    pieces = refs[:PIECES]
    away_out, turned_out, rows, sems = refs[PIECES:]
    for copy in fetch(pieces, rows, sems):
        copy.wait()

    def product(m, carry):
        where = pl.ds(pl.multiple_of(m * 256, 256), 256)
        part = rows[:, where].T
        turned_out[where, :] = part
        away_out[where, :] = jnp.dot(part, weighted[...], preferred_element_type=F32).astype(BF16)
        return carry

    lax.fori_loop(0, ROW // 256, product, 0)


def away_call(weighted, pieces, interpret=False):
    vmem = pl.BlockSpec(memory_space=VMEM)
    return pl.pallas_call(
        away_kernel,
        out_shape=(
            jax.ShapeDtypeStruct((ROW, NP), BF16),
            jax.ShapeDtypeStruct((ROW, PANEL), BF16),
        ),
        in_specs=[vmem] + [pl.BlockSpec(memory_space=pl.ANY)] * PIECES,
        out_specs=(vmem, vmem),
        scratch_shapes=[VMEM((PANEL, ROW), BF16), pltpu.SemaphoreType.DMA((PIECES,))],
        compiler_params=pltpu.CompilerParams(vmem_limit_bytes=20 << 20),
        interpret=interpret,
        name="away",
    )(weighted, *pieces)


def home_kernel(weighted, rows, home_out):
    def product(m, carry):
        where = pl.ds(pl.multiple_of(m * 256, 256), 256)
        home_out[where, :] = jnp.dot(rows[where, :], weighted[...], preferred_element_type=F32)
        return carry

    lax.fori_loop(0, ROW // 256, product, 0)


def home_call(weighted, rows, interpret=False):
    vmem = pl.BlockSpec(memory_space=VMEM)
    return pl.pallas_call(
        home_kernel,
        out_shape=jax.ShapeDtypeStruct((ROW, NP), F32),
        in_specs=[vmem, vmem],
        out_specs=vmem,
        compiler_params=pltpu.CompilerParams(vmem_limit_bytes=16 << 20),
        interpret=interpret,
        name="home",
    )(weighted, rows)


PLANE = ("band", "gcol_0", "gcol_1")


def turned(array, phase, step):
    pairs = []
    for band in range(2):
        along_x = (band == 0) == (phase == 0)
        for y in range(4):
            for x in range(4):
                to = (y, (x + step) % 4) if along_x else ((y + step) % 4, x)
                pairs.append((band * 16 + y * 4 + x, band * 16 + to[0] * 4 + to[1]))
    return lax.ppermute(array, PLANE, pairs)


ALL = ("band", "grow", "gcol_0", "gcol_1")


def along(array, steps):
    pairs = []
    for band in range(2):
        for plane in range(GCOL):
            step = steps((band == 0) == (plane < 8), band)
            if step is None:
                continue
            for z in range(GROW):
                to = (z + step) % GROW if band == 0 else (z - step) % GROW
                pairs.append(((band * GROW + z) * GCOL + plane, (band * GROW + to) * GCOL + plane))
    return lax.ppermute(array, ALL, pairs)


def swap(array):
    return lax.ppermute(array, "band", [(0, 1), (1, 0)])


def per_device(
    valence_orbitals,
    conduction_orbitals,
    valence_energy,
    conduction_energy,
    coulomb_root,
    pair_bands,
    slot_counts,
):
    place = lax.axis_index(("band", "grow", "gcol_0", "gcol_1")).astype(jnp.int32).reshape(1)
    other_con = swap(conduction_orbitals)
    other_pairs, other_count = swap(pair_bands), swap(slot_counts)
    vals = ready_call(valence_orbitals)
    col, *rows = density_call(
        place, pair_bands, other_pairs, slot_counts, other_count, valence_energy, conduction_energy,
        vals, conduction_orbitals, other_con, coulomb_root.reshape(1, N1 * NP),
    )
    return exchange(place, col, rows)


def exchange(place, col, rows):
    rows = [along(rows[i], lambda f, b, i=i: i + 1 if f else i) for i in range(4)]
    col = lax.all_to_all(col, ("gcol_0", "gcol_1"), 0, 0, tiled=True)
    row = pack_call(rows)
    parts = [col[:8], col[8:]]
    rings = []
    for part in range(2):
        ring = [parts[part]]
        for i in range(1, 5):
            ring.append(
                along(ring[-1], lambda f, b, i=i, part=part: 1 if i < 4 or b == part else None)
            )
        rings += ring
    far = turned(row, 0, 2)
    below, above = turned(row, 0, 1), turned(row, 0, -1)
    line = jnp.concatenate([row, below, above, far], 0)
    half = line.shape[0] // 2
    below, above = turned(line, 1, 1), turned(line, 1, -1)
    far_a, far_b = turned(below[:half], 1, 1), turned(above[half:], 1, -1)
    weighted_away, weighted_home = assemble_call(place, rings)
    pieces = [line, below, above, far_a, far_b]
    away, turned_rows = away_call(weighted_away, pieces)
    received = swap(away)
    home = home_call(weighted_home, turned_rows)
    return -(home + received.astype(F32))[None]


def solution(mesh):
    finer = Mesh(
        mesh.devices.reshape(mesh.shape["band"], mesh.shape["grow"], 4, 4),
        ("band", "grow", "gcol_0", "gcol_1"),
    )
    everywhere = ("band", "grow", "gcol_0", "gcol_1")
    in_specs = (P(), P(everywhere, None), P(), P(), P(), P(None, everywhere), P(everywhere))
    return jax.shard_map(
        per_device,
        mesh=finer,
        in_specs=in_specs,
        out_specs=P("band", "grow", ("gcol_0", "gcol_1")),
        check_vma=False,
    )
```

```python
import math

import jax
import jax.numpy as jnp
import numpy as np
from jax import lax
from jax.experimental import pallas as pl
from jax.experimental.pallas import tpu as pltpu
from jax.sharding import Mesh
from jax.sharding import PartitionSpec as P


N1, N2, N3 = 16, 24, 32
M1, M2, M3 = 32, 48, 64
NP = N2 * N3
KP = M2 * M3
MG = M1 * KP
ROW = 2 * NP
TOTAL = 5120
SLOTS = 20
HALF = 10
GROW, GCOL = 8, 16
LANES = 128
CHUNKS = KP // LANES
LINES = MG // LANES + 4
PANEL = GROW * GCOL * HALF
BLOCK = 64
ROWBLOCK = 120
COLROWS = GCOL * BLOCK + 4
WIDTH = NP // LANES
STEP = 512
F32, BF16 = jnp.float32, jnp.bfloat16
VMEM = pltpu.VMEM
SMEM = pltpu.SMEM


def wave_table(keep, length):
    wave = (np.arange(keep)[:, None] - keep // 2) % length
    angles = 2.0 * np.pi * (wave * np.arange(length)[None, :] % length) / length
    return np.cos(angles) + np.sin(angles)


def halves(table):
    high = table.astype(np.float32).astype(BF16)
    return high, (table - high.astype(np.float64)).astype(np.float32).astype(BF16)


def tables():
    second = np.repeat(wave_table(N2, M2).T, N3, axis=1)
    third = np.tile(wave_table(N3, M3).T, (1, N2))
    first = wave_table(N1, M1)
    mixed = np.zeros((N1, 16, HALF, M1))
    for p in range(HALF):
        mixed[:, p, p] = first
    return (
        second.astype(np.float32),
        third.astype(np.float32),
        halves(mixed.reshape(N1 * 16, HALF * M1)),
    )


def ready_kernel(source, vals, val, sems):
    count = 4
    size = MG // count
    copies = []
    for i in range(count):
        where = pl.ds(i * size, size)
        copies.append(pltpu.make_async_copy(source.at[:, where], val.at[:, where], sems.at[i]))
        copies[-1].start()
    for i, copy in enumerate(copies):
        copy.wait()

        def spread(a, carry):
            for t in range(CHUNKS):
                where = pl.ds(pl.multiple_of(a * KP + t * LANES, LANES), LANES)
                vals[pl.ds(t * M1 + a, 16, stride=LINES), :] = val[:, where].astype(F32)
            return carry

        lax.fori_loop(i * M1 // count, (i + 1) * M1 // count, spread, 0)


def ready_call(val, interpret=False):
    return pl.pallas_call(
        ready_kernel,
        out_shape=jax.ShapeDtypeStruct((16 * LINES, LANES), F32),
        in_specs=[pl.BlockSpec(memory_space=pltpu.HBM)],
        out_specs=pl.BlockSpec(memory_space=VMEM),
        scratch_shapes=[VMEM((16, MG), BF16), pltpu.SemaphoreType.DMA((4,))],
        compiler_params=pltpu.CompilerParams(vmem_limit_bytes=12 << 20),
        interpret=interpret,
        name="ready",
    )(stay(val))


def density_kernel(
    place, mine, other, my_count, other_count, vals, *refs,
):
    hbm, refs = refs[:9], refs[9:]
    col_out = refs[0]
    row_outs = refs[1:5]
    cons, lhs, acc, table_a, table_b, done, lines, row_lines = refs[5:13]
    local, sems = refs[13:22], refs[22]
    copies = [pltpu.make_async_copy(a, b, sems.at[i]) for i, (a, b) in enumerate(zip(hbm, local))]
    for copy in copies:
        copy.start()
    con_mine, con_other, second, third, mix_hi, mix_lo, scale, val_e, con_e = local
    band = place[0] >> 7
    z = (place[0] >> 4) & 7
    skip = jnp.where((band == 0) == ((place[0] & 15) < 8), 1, 0)
    for copy in copies[:2]:
        copy.wait()

    def spread(a, carry):
        for t in range(CHUNKS):
            where = pl.ds(pl.multiple_of(a * KP + t * LANES, LANES), LANES)
            line = t * M1 + a
            cons[pl.ds(line, 8, stride=LINES), :] = jnp.concatenate(
                [con_mine[:, where].astype(F32), con_other[:, where].astype(F32)], 0
            )
        return carry

    lax.fori_loop(0, M1, spread, 0)
    for copy in copies[2:]:
        copy.wait()

    is_first = band == 0
    first_count = jnp.where(is_first, my_count[0], other_count[0])
    both_count = my_count[0] + other_count[0]
    lane = lax.broadcasted_iota(jnp.int32, (1, LANES), 1) & 15
    gaps = []
    for h in range(2):
        gap = jnp.ones((1, LANES), F32)
        for p in range(HALF):
            pos = h * HALF + p
            from_first = pos < first_count
            slot = jnp.minimum(jnp.where(from_first, pos, pos - first_count), SLOTS - 1)
            own = from_first == is_first
            v = jnp.where(own, mine[0, slot], other[0, slot])
            c = jnp.where(own, mine[1, slot], other[1, slot])
            gap = jnp.where(lane == p, con_e[c] - val_e[v], gap)
            v_line = v * LINES
            c_line = (jnp.where(own, 0, 4) + (c & 3)) * LINES
            top = pos * M1

            def product(t, carry):
                made = vals[pl.ds(v_line + t * M1, M1), :] * cons[pl.ds(c_line + t * M1, M1), :]
                where = pl.ds(pl.multiple_of(t * LANES, LANES), LANES)
                lhs[top : top + M1, where] = made.astype(BF16)
                return carry

            lax.fori_loop(0, CHUNKS, product, 0, unroll=6)
        gaps.append(gap)

    acc[...] = jnp.zeros_like(acc)

    def make(table, k):
        for i in range(STEP // M3):
            table[i * M3 : (i + 1) * M3, :] = (
                second[pl.ds(k * (STEP // M3) + i, 1), :] * third[...]
            ).astype(BF16)

    def add(table, k):
        where = pl.ds(pl.multiple_of(k * STEP, STEP), STEP)
        acc[...] += jnp.dot(lhs[:, where], table[...], preferred_element_type=F32)

    last = KP // STEP - 1
    make(table_a, 0)

    def transform(k, carry):
        make(table_b, 2 * k + 1)
        add(table_a, 2 * k)
        make(table_a, jnp.minimum(2 * k + 2, last))
        add(table_b, 2 * k + 1)
        return carry

    lax.fori_loop(0, KP // STEP // 2, transform, 0)
    at_lane = lax.broadcasted_iota(jnp.int32, (1, LANES), 1)
    frequency = (at_lane >> 4).astype(F32)
    norm = 1.0 / math.sqrt(MG)
    for h in range(2):
        mid = acc[h * HALF * M1 : (h + 1) * HALF * M1, :]
        mid_hi = mid.astype(BF16)
        mid_lo = (mid - mid_hi.astype(F32)).astype(BF16)
        done[...] = (
            jnp.dot(mix_hi[...], mid_hi, preferred_element_type=F32)
            + jnp.dot(mix_hi[...], mid_lo, preferred_element_type=F32)
            + jnp.dot(mix_lo[...], mid_hi, preferred_element_type=F32)
        )
        gap = gaps[h]
        live = (h * HALF + lane < both_count) & (lane < HALF) & (at_lane < 32)
        weight = jnp.where(
            live, 2.0 * gap / (gap * gap + frequency * frequency), 0.0
        ) * (1.0 / math.sqrt(TOTAL))
        w_hi = weight.astype(BF16).astype(F32)
        w_mid = (weight - w_hi).astype(BF16).astype(F32)
        lines[WIDTH * HALF : WIDTH * HALF + 1, :] = w_hi
        lines[WIDTH * HALF + 1 : WIDTH * HALF + 2, :] = w_mid
        lines[WIDTH * HALF + 2 : WIDTH * HALF + 3, :] = weight - w_hi - w_mid
        lines[WIDTH * HALF + 3 : WIDTH * HALF + 4, :] = jnp.zeros((1, LANES), F32)
        for k in range(N1):
            block = done[k * 16 : (k + 1) * 16, :] * (scale[:, k * NP : (k + 1) * NP] * norm)
            done[k * 16 : (k + 1) * 16, :] = block
            for ch in range(WIDTH):
                lines[ch * HALF : (ch + 1) * HALF, :] = block[:HALF, ch * LANES : (ch + 1) * LANES]
            col_out[k, h] = lines[...].astype(BF16)
        for i in range(4):
            target = jnp.where(band == 0, z + i + skip, z - i - skip + GROW) & 7
            for s in range(2):
                block = done[pl.ds(pl.multiple_of((2 * target + s) * 16, 16), 16), :]
                for ch in range(WIDTH):
                    at = (s * WIDTH + ch) * HALF
                    row_lines[at : at + HALF, :] = block[:HALF, ch * LANES : (ch + 1) * LANES]
            row_outs[i][h] = row_lines[...].astype(BF16)


def stay(array):
    return pltpu.with_memory_space_constraint(jnp.asarray(array), pltpu.HBM)


def density_call(
    place, mine, other, my_count, other_count, val_e, con_e, vals, con_mine, con_other, scale, interpret=False
):
    second, third, (mix_hi, mix_lo) = tables()
    smem = pl.BlockSpec(memory_space=SMEM)
    vmem = pl.BlockSpec(memory_space=VMEM)
    hbm = pl.BlockSpec(memory_space=pltpu.HBM)
    anywhere = pl.BlockSpec(memory_space=pl.ANY)
    return pl.pallas_call(
        density_kernel,
        out_shape=[
            jax.ShapeDtypeStruct((N1, 2, BLOCK, LANES), BF16),
        ]
        + [jax.ShapeDtypeStruct((2, ROWBLOCK, LANES), BF16)] * 4,
        in_specs=[smem] * 5 + [vmem, hbm, anywhere] + [hbm] * 7,
        out_specs=[vmem] * 5,
        scratch_shapes=[
            VMEM((8 * LINES, LANES), F32),
            VMEM((2 * HALF * M1, KP), BF16),
            VMEM((2 * HALF * M1, NP), F32),
            VMEM((STEP, NP), BF16),
            VMEM((STEP, NP), BF16),
            VMEM((N1 * 16, NP), F32),
            VMEM((BLOCK, LANES), F32),
            VMEM((ROWBLOCK, LANES), F32),
            VMEM((4, MG), BF16),
            VMEM((4, MG), BF16),
            VMEM((M2, NP), F32),
            VMEM((M3, NP), F32),
            VMEM((N1 * 16, HALF * M1), BF16),
            VMEM((N1 * 16, HALF * M1), BF16),
            VMEM((1, N1 * NP), F32),
            SMEM((16,), F32),
            SMEM((1024,), F32),
            pltpu.SemaphoreType.DMA((9,)),
        ],
        compiler_params=pltpu.CompilerParams(vmem_limit_bytes=24 << 20),
        interpret=interpret,
        name="density",
    )(place, mine, other, my_count, other_count, vals, stay(con_mine), con_other, stay(second), stay(third),
      stay(mix_hi), stay(mix_lo), stay(scale), stay(val_e), stay(con_e))


def pack_kernel(*refs):
    blocks, out, spread = refs[:4], refs[4], refs[5]
    stride = ROWBLOCK + 4
    for v in range(8):
        spread[v * stride : v * stride + ROWBLOCK, :] = blocks[v // 2][v % 2].astype(F32)
    for ch in range(2 * WIDTH):
        for pp in range(HALF // 2):
            got = [spread[pl.ds(ch * HALF + 2 * pp + q, 8, stride=stride), :] for q in range(2)]
            out[pp * 16 : (pp + 1) * 16, ch * LANES : (ch + 1) * LANES] = jnp.concatenate(
                got, 0
            ).astype(BF16)


def pack_call(blocks, interpret=False):
    vmem = pl.BlockSpec(memory_space=VMEM)
    return pl.pallas_call(
        pack_kernel,
        out_shape=jax.ShapeDtypeStruct((8 * HALF, ROW), BF16),
        in_specs=[vmem] * 4,
        out_specs=vmem,
        scratch_shapes=[VMEM((8 * (ROWBLOCK + 4), LANES), F32)],
        compiler_params=pltpu.CompilerParams(vmem_limit_bytes=4 << 20),
        interpret=interpret,
        name="pack",
    )(*blocks)


def fetch(pieces, rows, sems):
    copies = []
    at = 0
    for i, piece in enumerate(pieces):
        size = piece.shape[0]
        copies.append(pltpu.make_async_copy(piece, rows.at[pl.ds(at, size), :], sems.at[i]))
        copies[-1].start()
        at += size
    return copies


def around(step):
    return jnp.where(step == 0, 0, jnp.where(step == 1, 3, jnp.where(step == 2, 1, 2)))


def choose_kernel(place, one, two, out):
    @pl.when(place[0] < GROW * GCOL)
    def _():
        out[...] = one[...]

    @pl.when(place[0] >= GROW * GCOL)
    def _():
        out[...] = two[...]


def choose_call(place, one, two, interpret=False):
    vmem = pl.BlockSpec(memory_space=VMEM)
    return pl.pallas_call(
        choose_kernel,
        out_shape=jax.ShapeDtypeStruct(one.shape, one.dtype),
        in_specs=[pl.BlockSpec(memory_space=SMEM), vmem, vmem],
        out_specs=vmem,
        compiler_params=pltpu.CompilerParams(vmem_limit_bytes=4 << 20),
        interpret=interpret,
        name="choose",
    )(place, one, two)


def assemble_kernel(place, *refs):
    cols = [*refs[:4], refs[8], *refs[4:9]]
    away_out, home_out, spread = refs[9:]
    me = place[0]
    band, y, x = me >> 7, (me >> 2) & 3, me & 3

    def take(part, first):
        for i in range(4):
            col = cols[part * 5 + first + i]
            for q in range(GCOL // 2):
                for h in range(2):
                    at = (2 * i + h) * COLROWS + (part * 8 + q) * BLOCK
                    spread[at : at + BLOCK, :] = col[q, h].astype(F32)

    @pl.when(band == 0)
    def _():
        take(0, 1)
        take(1, 0)

    @pl.when(band == 1)
    def _():
        take(0, 0)
        take(1, 1)

    def assemble(j, carry):
        outer, inner = around(j >> 2), around(j & 3)
        dy = jnp.where(band == 0, outer, inner)
        dx = jnp.where(band == 0, inner, outer)
        base = (((y + dy) & 3) * 4 + ((x + dx) & 3)) * BLOCK
        weight = jnp.zeros((GROW, LANES), F32)
        for part in range(3):
            weight += spread[pl.ds(base + WIDTH * HALF + part, GROW, stride=COLROWS), :]
        other = pltpu.roll(weight, LANES - 16, 1)
        away = jnp.where(band == 0, other, weight)
        home = jnp.where(band == 0, weight, other)
        for pp in range(HALF // 2):
            ws = [
                [jnp.broadcast_to(w[:, 2 * pp + q : 2 * pp + q + 1], (GROW, LANES)) for q in range(2)]
                for w in (away, home)
            ]
            to = pl.ds(pl.multiple_of(j * GROW * HALF + pp * 16, 16), 16)
            for ch in range(WIDTH):
                got = [
                    spread[pl.ds(base + ch * HALF + 2 * pp + q, GROW, stride=COLROWS), :]
                    for q in range(2)
                ]
                where = slice(ch * LANES, (ch + 1) * LANES)
                for f, dest in enumerate((away_out, home_out)):
                    dest[to, where] = jnp.concatenate(
                        [got[0] * ws[f][0], got[1] * ws[f][1]], 0
                    ).astype(BF16)
        return carry

    lax.fori_loop(0, GCOL, assemble, 0)


def assemble_call(place, cols, interpret=False):
    vmem = pl.BlockSpec(memory_space=VMEM)
    return pl.pallas_call(
        assemble_kernel,
        out_shape=[jax.ShapeDtypeStruct((PANEL, NP), BF16)] * 2,
        in_specs=[pl.BlockSpec(memory_space=SMEM)] + [vmem] * 9,
        out_specs=[vmem] * 2,
        scratch_shapes=[VMEM((GROW * COLROWS, LANES), F32)],
        compiler_params=pltpu.CompilerParams(vmem_limit_bytes=14 << 20),
        interpret=interpret,
        name="assemble",
    )(place, *cols)


PIECES = 5


def away_kernel(weighted, *refs):
    pieces = refs[:PIECES]
    away_out, turned_out, rows, sems = refs[PIECES:]
    for copy in fetch(pieces, rows, sems):
        copy.wait()

    def product(m, carry):
        where = pl.ds(pl.multiple_of(m * 256, 256), 256)
        part = rows[:, where].T
        turned_out[where, :] = part
        away_out[where, :] = jnp.dot(part, weighted[...], preferred_element_type=F32).astype(BF16)
        return carry

    lax.fori_loop(0, ROW // 256, product, 0)


def away_call(weighted, pieces, interpret=False):
    vmem = pl.BlockSpec(memory_space=VMEM)
    return pl.pallas_call(
        away_kernel,
        out_shape=(
            jax.ShapeDtypeStruct((ROW, NP), BF16),
            jax.ShapeDtypeStruct((ROW, PANEL), BF16),
        ),
        in_specs=[vmem] + [pl.BlockSpec(memory_space=pl.ANY)] * PIECES,
        out_specs=(vmem, vmem),
        scratch_shapes=[VMEM((PANEL, ROW), BF16), pltpu.SemaphoreType.DMA((PIECES,))],
        compiler_params=pltpu.CompilerParams(vmem_limit_bytes=20 << 20),
        interpret=interpret,
        name="away",
    )(weighted, *pieces)


def home_kernel(weighted, rows, home_out):
    def product(m, carry):
        where = pl.ds(pl.multiple_of(m * 256, 256), 256)
        home_out[where, :] = jnp.dot(rows[where, :], weighted[...], preferred_element_type=F32)
        return carry

    lax.fori_loop(0, ROW // 256, product, 0)


def home_call(weighted, rows, interpret=False):
    vmem = pl.BlockSpec(memory_space=VMEM)
    return pl.pallas_call(
        home_kernel,
        out_shape=jax.ShapeDtypeStruct((ROW, NP), F32),
        in_specs=[vmem, vmem],
        out_specs=vmem,
        compiler_params=pltpu.CompilerParams(vmem_limit_bytes=16 << 20),
        interpret=interpret,
        name="home",
    )(weighted, rows)


PLANE = ("band", "gcol_0", "gcol_1")


def turned(array, phase, step):
    pairs = []
    for band in range(2):
        along_x = (band == 0) == (phase == 0)
        for y in range(4):
            for x in range(4):
                to = (y, (x + step) % 4) if along_x else ((y + step) % 4, x)
                pairs.append((band * 16 + y * 4 + x, band * 16 + to[0] * 4 + to[1]))
    return lax.ppermute(array, PLANE, pairs)


ALL = ("band", "grow", "gcol_0", "gcol_1")


def along(array, steps):
    pairs = []
    for band in range(2):
        for plane in range(GCOL):
            step = steps((band == 0) == (plane < 8), band)
            if step is None:
                continue
            for z in range(GROW):
                to = (z + step) % GROW if band == 0 else (z - step) % GROW
                pairs.append(((band * GROW + z) * GCOL + plane, (band * GROW + to) * GCOL + plane))
    return lax.ppermute(array, ALL, pairs)


def swap(array):
    return lax.ppermute(array, "band", [(0, 1), (1, 0)])


def per_device(
    valence_orbitals,
    conduction_orbitals,
    valence_energy,
    conduction_energy,
    coulomb_root,
    pair_bands,
    slot_counts,
):
    place = lax.axis_index(("band", "grow", "gcol_0", "gcol_1")).astype(jnp.int32).reshape(1)
    other_con = swap(conduction_orbitals)
    other_pairs, other_count = swap(pair_bands), swap(slot_counts)
    vals = ready_call(valence_orbitals)
    col, *rows = density_call(
        place, pair_bands, other_pairs, slot_counts, other_count, valence_energy, conduction_energy,
        vals, conduction_orbitals, other_con, coulomb_root.reshape(1, N1 * NP),
    )
    return exchange(place, col, rows)


def exchange(place, col, rows):
    rows = [along(rows[i], lambda f, b, i=i: i + 1 if f else i) for i in range(4)]
    col = lax.all_to_all(col, ("gcol_0", "gcol_1"), 0, 0, tiled=True)
    row = pack_call(rows)
    parts = [col[:8], col[8:]]
    rings = [[part] for part in parts]
    for _ in range(1, 4):
        for part in range(2):
            rings[part].append(along(rings[part][-1], lambda f, b: 1))
    last = choose_call(place, rings[0][-1], rings[1][-1])
    rings = rings[0] + rings[1] + [along(last, lambda f, b: 1)]
    far = turned(row, 0, 2)
    below, above = turned(row, 0, 1), turned(row, 0, -1)
    line = jnp.concatenate([row, below, above, far], 0)
    half = line.shape[0] // 2
    below, above = turned(line, 1, 1), turned(line, 1, -1)
    far_a, far_b = turned(below[:half], 1, 1), turned(above[half:], 1, -1)
    weighted_away, weighted_home = assemble_call(place, rings)
    pieces = [line, below, above, far_a, far_b]
    away, turned_rows = away_call(weighted_away, pieces)
    received = swap(away)
    home = home_call(weighted_home, turned_rows)
    return -(home + received.astype(F32))[None]


def solution(mesh):
    finer = Mesh(
        mesh.devices.reshape(mesh.shape["band"], mesh.shape["grow"], 4, 4),
        ("band", "grow", "gcol_0", "gcol_1"),
    )
    everywhere = ("band", "grow", "gcol_0", "gcol_1")
    in_specs = (P(), P(everywhere, None), P(), P(), P(), P(None, everywhere), P(everywhere))
    return jax.shard_map(
        per_device,
        mesh=finer,
        in_specs=in_specs,
        out_specs=P("band", "grow", ("gcol_0", "gcol_1")),
        check_vma=False,
    )
```

```python
import math

import jax
import jax.numpy as jnp
import numpy as np
from jax import lax
from jax.experimental import pallas as pl
from jax.experimental.pallas import tpu as pltpu
from jax.sharding import Mesh
from jax.sharding import PartitionSpec as P


N1, N2, N3 = 16, 24, 32
M1, M2, M3 = 32, 48, 64
NP = N2 * N3
KP = M2 * M3
MG = M1 * KP
ROW = 2 * NP
TOTAL = 5120
SLOTS = 20
HALF = 10
GROW, GCOL = 8, 16
LANES = 128
CHUNKS = KP // LANES
LINES = MG // LANES + 4
PANEL = GROW * GCOL * HALF
BLOCK = 64
ROWBLOCK = 120
COLROWS = GCOL * BLOCK + 4
WIDTH = NP // LANES
STEP = 512
F32, BF16 = jnp.float32, jnp.bfloat16
VMEM = pltpu.VMEM
SMEM = pltpu.SMEM


def wave_table(keep, length):
    wave = (np.arange(keep)[:, None] - keep // 2) % length
    angles = 2.0 * np.pi * (wave * np.arange(length)[None, :] % length) / length
    return np.cos(angles) + np.sin(angles)


def halves(table):
    high = table.astype(np.float32).astype(BF16)
    return high, (table - high.astype(np.float64)).astype(np.float32).astype(BF16)


def tables():
    second = np.repeat(wave_table(N2, M2).T, N3, axis=1)
    third = np.tile(wave_table(N3, M3).T, (1, N2))
    first = wave_table(N1, M1)
    mixed = np.zeros((N1, 16, HALF, M1))
    for p in range(HALF):
        mixed[:, p, p] = first
    return (
        second.astype(np.float32),
        third.astype(np.float32),
        halves(mixed.reshape(N1 * 16, HALF * M1)),
    )


def ready_kernel(source, vals, val, sems):
    count = 4
    size = MG // count
    copies = []
    for i in range(count):
        where = pl.ds(i * size, size)
        copies.append(pltpu.make_async_copy(source.at[:, where], val.at[:, where], sems.at[i]))
        copies[-1].start()
    for i, copy in enumerate(copies):
        copy.wait()

        def spread(a, carry):
            for t in range(CHUNKS):
                where = pl.ds(pl.multiple_of(a * KP + t * LANES, LANES), LANES)
                vals[pl.ds(t * M1 + a, 16, stride=LINES), :] = val[:, where].astype(F32)
            return carry

        lax.fori_loop(i * M1 // count, (i + 1) * M1 // count, spread, 0)


def ready_call(val, interpret=False):
    return pl.pallas_call(
        ready_kernel,
        out_shape=jax.ShapeDtypeStruct((16 * LINES, LANES), F32),
        in_specs=[pl.BlockSpec(memory_space=pltpu.HBM)],
        out_specs=pl.BlockSpec(memory_space=VMEM),
        scratch_shapes=[VMEM((16, MG), BF16), pltpu.SemaphoreType.DMA((4,))],
        compiler_params=pltpu.CompilerParams(vmem_limit_bytes=12 << 20),
        interpret=interpret,
        name="ready",
    )(stay(val))


def density_kernel(
    place, mine, other, my_count, other_count, vals, *refs,
):
    hbm, refs = refs[:9], refs[9:]
    col_out = refs[0]
    row_outs = refs[1:6]
    cons, lhs, acc, table_a, table_b, done, lines, row_lines = refs[6:14]
    local, sems = refs[14:23], refs[23]
    copies = [pltpu.make_async_copy(a, b, sems.at[i]) for i, (a, b) in enumerate(zip(hbm, local))]
    for copy in copies:
        copy.start()
    con_mine, con_other, second, third, mix_hi, mix_lo, scale, val_e, con_e = local
    band = place[0] >> 7
    z = (place[0] >> 4) & 7
    for copy in copies[:2]:
        copy.wait()

    def spread(a, carry):
        for t in range(CHUNKS):
            where = pl.ds(pl.multiple_of(a * KP + t * LANES, LANES), LANES)
            line = t * M1 + a
            cons[pl.ds(line, 8, stride=LINES), :] = jnp.concatenate(
                [con_mine[:, where].astype(F32), con_other[:, where].astype(F32)], 0
            )
        return carry

    lax.fori_loop(0, M1, spread, 0)
    for copy in copies[2:]:
        copy.wait()

    is_first = band == 0
    first_count = jnp.where(is_first, my_count[0], other_count[0])
    both_count = my_count[0] + other_count[0]
    lane = lax.broadcasted_iota(jnp.int32, (1, LANES), 1) & 15
    gaps = []
    for h in range(2):
        gap = jnp.ones((1, LANES), F32)
        for p in range(HALF):
            pos = h * HALF + p
            from_first = pos < first_count
            slot = jnp.minimum(jnp.where(from_first, pos, pos - first_count), SLOTS - 1)
            own = from_first == is_first
            v = jnp.where(own, mine[0, slot], other[0, slot])
            c = jnp.where(own, mine[1, slot], other[1, slot])
            gap = jnp.where(lane == p, con_e[c] - val_e[v], gap)
            v_line = v * LINES
            c_line = (jnp.where(own, 0, 4) + (c & 3)) * LINES
            top = pos * M1

            def product(t, carry):
                made = vals[pl.ds(v_line + t * M1, M1), :] * cons[pl.ds(c_line + t * M1, M1), :]
                where = pl.ds(pl.multiple_of(t * LANES, LANES), LANES)
                lhs[top : top + M1, where] = made.astype(BF16)
                return carry

            lax.fori_loop(0, CHUNKS, product, 0, unroll=6)
        gaps.append(gap)

    acc[...] = jnp.zeros_like(acc)

    def make(table, k):
        for i in range(STEP // M3):
            table[i * M3 : (i + 1) * M3, :] = (
                second[pl.ds(k * (STEP // M3) + i, 1), :] * third[...]
            ).astype(BF16)

    def add(table, k):
        where = pl.ds(pl.multiple_of(k * STEP, STEP), STEP)
        acc[...] += jnp.dot(lhs[:, where], table[...], preferred_element_type=F32)

    last = KP // STEP - 1
    make(table_a, 0)

    def transform(k, carry):
        make(table_b, 2 * k + 1)
        add(table_a, 2 * k)
        make(table_a, jnp.minimum(2 * k + 2, last))
        add(table_b, 2 * k + 1)
        return carry

    lax.fori_loop(0, KP // STEP // 2, transform, 0)
    at_lane = lax.broadcasted_iota(jnp.int32, (1, LANES), 1)
    frequency = (at_lane >> 4).astype(F32)
    norm = 1.0 / math.sqrt(MG)
    for h in range(2):
        mid = acc[h * HALF * M1 : (h + 1) * HALF * M1, :]
        mid_hi = mid.astype(BF16)
        mid_lo = (mid - mid_hi.astype(F32)).astype(BF16)
        done[...] = (
            jnp.dot(mix_hi[...], mid_hi, preferred_element_type=F32)
            + jnp.dot(mix_hi[...], mid_lo, preferred_element_type=F32)
            + jnp.dot(mix_lo[...], mid_hi, preferred_element_type=F32)
        )
        gap = gaps[h]
        live = (h * HALF + lane < both_count) & (lane < HALF) & (at_lane < 32)
        weight = jnp.where(
            live, 2.0 * gap / (gap * gap + frequency * frequency), 0.0
        ) * (1.0 / math.sqrt(TOTAL))
        w_hi = weight.astype(BF16).astype(F32)
        w_mid = (weight - w_hi).astype(BF16).astype(F32)
        lines[WIDTH * HALF : WIDTH * HALF + 1, :] = w_hi
        lines[WIDTH * HALF + 1 : WIDTH * HALF + 2, :] = w_mid
        lines[WIDTH * HALF + 2 : WIDTH * HALF + 3, :] = weight - w_hi - w_mid
        lines[WIDTH * HALF + 3 : WIDTH * HALF + 4, :] = jnp.zeros((1, LANES), F32)
        done[...] = done[...] * jnp.concatenate(
            [
                jnp.broadcast_to(scale[:, k * NP : (k + 1) * NP] * norm, (16, NP))
                for k in range(N1)
            ],
            0,
        )

        @pl.when(band == h)
        def _():
            for k in range(N1):
                for ch in range(WIDTH):
                    lines[ch * HALF : (ch + 1) * HALF, :] = done[
                        k * 16 : k * 16 + HALF, ch * LANES : (ch + 1) * LANES
                    ]
                col_out[k] = lines[...].astype(BF16)

        def message(step):
            target = jnp.where(band == 0, z + step, z - step + GROW) & 7
            for s in range(2):
                block = done[pl.ds(pl.multiple_of((2 * target + s) * 16, 16), 16), :]
                for ch in range(WIDTH):
                    at = (s * WIDTH + ch) * HALF
                    row_lines[at : at + HALF, :] = block[:HALF, ch * LANES : (ch + 1) * LANES]
            return row_lines[...].astype(BF16)

        for step in range(1, 4):
            row_outs[step][jnp.where(band == h, 0, 1)] = message(step)

        @pl.when(band == h)
        def _():
            row_outs[4][0] = message(4)

        @pl.when(band != h)
        def _():
            row_outs[0][0] = message(0)


def stay(array):
    return pltpu.with_memory_space_constraint(jnp.asarray(array), pltpu.HBM)


def density_call(
    place, mine, other, my_count, other_count, val_e, con_e, vals, con_mine, con_other, scale, interpret=False
):
    second, third, (mix_hi, mix_lo) = tables()
    smem = pl.BlockSpec(memory_space=SMEM)
    vmem = pl.BlockSpec(memory_space=VMEM)
    hbm = pl.BlockSpec(memory_space=pltpu.HBM)
    anywhere = pl.BlockSpec(memory_space=pl.ANY)
    return pl.pallas_call(
        density_kernel,
        out_shape=[
            jax.ShapeDtypeStruct((N1, BLOCK, LANES), BF16),
        ]
        + [jax.ShapeDtypeStruct((n, ROWBLOCK, LANES), BF16) for n in (1, 2, 2, 2, 1)],
        in_specs=[smem] * 5 + [vmem, hbm, anywhere] + [hbm] * 7,
        out_specs=[vmem] * 6,
        scratch_shapes=[
            VMEM((8 * LINES, LANES), F32),
            VMEM((2 * HALF * M1, KP), BF16),
            VMEM((2 * HALF * M1, NP), F32),
            VMEM((STEP, NP), BF16),
            VMEM((STEP, NP), BF16),
            VMEM((N1 * 16, NP), F32),
            VMEM((BLOCK, LANES), F32),
            VMEM((ROWBLOCK, LANES), F32),
            VMEM((4, MG), BF16),
            VMEM((4, MG), BF16),
            VMEM((M2, NP), F32),
            VMEM((M3, NP), F32),
            VMEM((N1 * 16, HALF * M1), BF16),
            VMEM((N1 * 16, HALF * M1), BF16),
            VMEM((1, N1 * NP), F32),
            SMEM((16,), F32),
            SMEM((1024,), F32),
            pltpu.SemaphoreType.DMA((9,)),
        ],
        compiler_params=pltpu.CompilerParams(vmem_limit_bytes=26 << 20),
        interpret=interpret,
        name="density",
    )(place, mine, other, my_count, other_count, vals, stay(con_mine), con_other, stay(second), stay(third),
      stay(mix_hi), stay(mix_lo), stay(scale), stay(val_e), stay(con_e))


def pack_kernel(*refs):
    blocks, out, spread = refs[:5], refs[5], refs[6]
    stride = ROWBLOCK + 4
    for i in range(4):
        for m, block in enumerate((blocks[i + 1][0], blocks[i][1 if i else 0])):
            at = (2 * i + m) * stride
            spread[at : at + ROWBLOCK, :] = block.astype(F32)
    for ch in range(2 * WIDTH):
        for pp in range(HALF // 2):
            got = [spread[pl.ds(ch * HALF + 2 * pp + q, 8, stride=stride), :] for q in range(2)]
            out[pp * 16 : (pp + 1) * 16, ch * LANES : (ch + 1) * LANES] = jnp.concatenate(
                got, 0
            ).astype(BF16)


def pack_call(blocks, interpret=False):
    vmem = pl.BlockSpec(memory_space=VMEM)
    return pl.pallas_call(
        pack_kernel,
        out_shape=jax.ShapeDtypeStruct((8 * HALF, ROW), BF16),
        in_specs=[vmem] * 5,
        out_specs=vmem,
        scratch_shapes=[VMEM((8 * (ROWBLOCK + 4), LANES), F32)],
        compiler_params=pltpu.CompilerParams(vmem_limit_bytes=4 << 20),
        interpret=interpret,
        name="pack",
    )(*blocks)


def fetch(pieces, rows, sems):
    copies = []
    at = 0
    for i, piece in enumerate(pieces):
        size = piece.shape[0]
        copies.append(pltpu.make_async_copy(piece, rows.at[pl.ds(at, size), :], sems.at[i]))
        copies[-1].start()
        at += size
    return copies


def around(step):
    return jnp.where(step == 0, 0, jnp.where(step == 1, 3, jnp.where(step == 2, 1, 2)))


def assemble_kernel(place, *refs):
    cols = refs[:8]
    away_out, home_out, spread = refs[8:]
    me = place[0]
    band, y, x = me >> 7, (me >> 2) & 3, me & 3
    for v, col in enumerate(cols):
        for q in range(GCOL):
            at = v * COLROWS + q * BLOCK
            spread[at : at + BLOCK, :] = col[q].astype(F32)

    def assemble(j, carry):
        outer, inner = around(j >> 2), around(j & 3)
        dy = jnp.where(band == 0, outer, inner)
        dx = jnp.where(band == 0, inner, outer)
        base = (((y + dy) & 3) * 4 + ((x + dx) & 3)) * BLOCK
        weight = jnp.zeros((GROW, LANES), F32)
        for part in range(3):
            weight += spread[pl.ds(base + WIDTH * HALF + part, GROW, stride=COLROWS), :]
        other = pltpu.roll(weight, LANES - 16, 1)
        away = jnp.where(band == 0, other, weight)
        home = jnp.where(band == 0, weight, other)
        for pp in range(HALF // 2):
            ws = [
                [jnp.broadcast_to(w[:, 2 * pp + q : 2 * pp + q + 1], (GROW, LANES)) for q in range(2)]
                for w in (away, home)
            ]
            to = pl.ds(pl.multiple_of(j * GROW * HALF + pp * 16, 16), 16)
            for ch in range(WIDTH):
                got = [
                    spread[pl.ds(base + ch * HALF + 2 * pp + q, GROW, stride=COLROWS), :]
                    for q in range(2)
                ]
                where = slice(ch * LANES, (ch + 1) * LANES)
                for f, dest in enumerate((away_out, home_out)):
                    dest[to, where] = jnp.concatenate(
                        [got[0] * ws[f][0], got[1] * ws[f][1]], 0
                    ).astype(BF16)
        return carry

    lax.fori_loop(0, GCOL, assemble, 0)


def assemble_call(place, cols, interpret=False):
    vmem = pl.BlockSpec(memory_space=VMEM)
    return pl.pallas_call(
        assemble_kernel,
        out_shape=[jax.ShapeDtypeStruct((PANEL, NP), BF16)] * 2,
        in_specs=[pl.BlockSpec(memory_space=SMEM)] + [vmem] * 8,
        out_specs=[vmem] * 2,
        scratch_shapes=[VMEM((GROW * COLROWS, LANES), F32)],
        compiler_params=pltpu.CompilerParams(vmem_limit_bytes=14 << 20),
        interpret=interpret,
        name="assemble",
    )(place, *cols)


PIECES = 5


def away_kernel(weighted, *refs):
    pieces = refs[:PIECES]
    away_out, turned_out, rows, sems = refs[PIECES:]
    for copy in fetch(pieces, rows, sems):
        copy.wait()

    def product(m, carry):
        where = pl.ds(pl.multiple_of(m * 256, 256), 256)
        part = rows[:, where].T
        turned_out[where, :] = part
        away_out[where, :] = jnp.dot(part, weighted[...], preferred_element_type=F32).astype(BF16)
        return carry

    lax.fori_loop(0, ROW // 256, product, 0)


def away_call(weighted, pieces, interpret=False):
    vmem = pl.BlockSpec(memory_space=VMEM)
    return pl.pallas_call(
        away_kernel,
        out_shape=(
            jax.ShapeDtypeStruct((ROW, NP), BF16),
            jax.ShapeDtypeStruct((ROW, PANEL), BF16),
        ),
        in_specs=[vmem] + [pl.BlockSpec(memory_space=pl.ANY)] * PIECES,
        out_specs=(vmem, vmem),
        scratch_shapes=[VMEM((PANEL, ROW), BF16), pltpu.SemaphoreType.DMA((PIECES,))],
        compiler_params=pltpu.CompilerParams(vmem_limit_bytes=20 << 20),
        interpret=interpret,
        name="away",
    )(weighted, *pieces)


def home_kernel(weighted, rows, home_out):
    def product(m, carry):
        where = pl.ds(pl.multiple_of(m * 256, 256), 256)
        home_out[where, :] = jnp.dot(rows[where, :], weighted[...], preferred_element_type=F32)
        return carry

    lax.fori_loop(0, ROW // 256, product, 0)


def home_call(weighted, rows, interpret=False):
    vmem = pl.BlockSpec(memory_space=VMEM)
    return pl.pallas_call(
        home_kernel,
        out_shape=jax.ShapeDtypeStruct((ROW, NP), F32),
        in_specs=[vmem, vmem],
        out_specs=vmem,
        compiler_params=pltpu.CompilerParams(vmem_limit_bytes=16 << 20),
        interpret=interpret,
        name="home",
    )(weighted, rows)


PLANE = ("band", "gcol_0", "gcol_1")


def turned(array, phase, step):
    pairs = []
    for band in range(2):
        along_x = (band == 0) == (phase == 0)
        for y in range(4):
            for x in range(4):
                to = (y, (x + step) % 4) if along_x else ((y + step) % 4, x)
                pairs.append((band * 16 + y * 4 + x, band * 16 + to[0] * 4 + to[1]))
    return lax.ppermute(array, PLANE, pairs)


def along(array, step):
    pairs = []
    for band in range(2):
        for z in range(GROW):
            to = (z + step) % GROW if band == 0 else (z - step) % GROW
            pairs.append((band * GROW + z, band * GROW + to))
    return lax.ppermute(array, ("band", "grow"), pairs)


def swap(array):
    return lax.ppermute(array, "band", [(0, 1), (1, 0)])


def per_device(
    valence_orbitals,
    conduction_orbitals,
    valence_energy,
    conduction_energy,
    coulomb_root,
    pair_bands,
    slot_counts,
):
    place = lax.axis_index(("band", "grow", "gcol_0", "gcol_1")).astype(jnp.int32).reshape(1)
    other_con = swap(conduction_orbitals)
    other_pairs, other_count = swap(pair_bands), swap(slot_counts)
    vals = ready_call(valence_orbitals)
    col, *rows = density_call(
        place, pair_bands, other_pairs, slot_counts, other_count, valence_energy, conduction_energy,
        vals, conduction_orbitals, other_con, coulomb_root.reshape(1, N1 * NP),
    )
    return exchange(place, col, rows)


def exchange(place, col, rows):
    rows = [rows[0]] + [along(rows[i], i) for i in range(1, 5)]
    col = lax.all_to_all(col, ("gcol_0", "gcol_1"), 0, 0, tiled=True)
    row = pack_call(rows)
    main, other = [col], [swap(col)]
    for _ in range(1, 5):
        main.append(along(main[-1], 1))
    for _ in range(1, 4):
        other.append(along(other[-1], 1))
    rings = []
    for i in range(4):
        rings += [main[i + 1], other[i]]
    far = turned(row, 0, 2)
    below, above = turned(row, 0, 1), turned(row, 0, -1)
    line = jnp.concatenate([row, below, above, far], 0)
    half = line.shape[0] // 2
    below, above = turned(line, 1, 1), turned(line, 1, -1)
    far_a, far_b = turned(below[:half], 1, 1), turned(above[half:], 1, -1)
    weighted_away, weighted_home = assemble_call(place, rings)
    pieces = [line, below, above, far_a, far_b]
    away, turned_rows = away_call(weighted_away, pieces)
    received = swap(away)
    home = home_call(weighted_home, turned_rows)
    return -(home + received.astype(F32))[None]


def solution(mesh):
    finer = Mesh(
        mesh.devices.reshape(mesh.shape["band"], mesh.shape["grow"], 4, 4),
        ("band", "grow", "gcol_0", "gcol_1"),
    )
    everywhere = ("band", "grow", "gcol_0", "gcol_1")
    in_specs = (P(), P(everywhere, None), P(), P(), P(), P(None, everywhere), P(everywhere))
    return jax.shard_map(
        per_device,
        mesh=finer,
        in_specs=in_specs,
        out_specs=P("band", "grow", ("gcol_0", "gcol_1")),
        check_vma=False,
    )
```

```python
import math

import jax
import jax.numpy as jnp
import numpy as np
from jax import lax
from jax.experimental import pallas as pl
from jax.experimental.pallas import tpu as pltpu
from jax.sharding import Mesh
from jax.sharding import PartitionSpec as P


N1, N2, N3 = 16, 24, 32
M1, M2, M3 = 32, 48, 64
NP = N2 * N3
KP = M2 * M3
MG = M1 * KP
ROW = 2 * NP
TOTAL = 5120
SLOTS = 20
HALF = 10
GROW, GCOL = 8, 16
LANES = 128
CHUNKS = KP // LANES
LINES = MG // LANES + 4
PANEL = GROW * GCOL * HALF
BLOCK = 64
ROWBLOCK = 120
COLROWS = GCOL * BLOCK + 4
WIDTH = NP // LANES
STEP = 512
F32, BF16 = jnp.float32, jnp.bfloat16
VMEM = pltpu.VMEM
SMEM = pltpu.SMEM


def wave_table(keep, length):
    wave = (np.arange(keep)[:, None] - keep // 2) % length
    angles = 2.0 * np.pi * (wave * np.arange(length)[None, :] % length) / length
    return np.cos(angles) + np.sin(angles)


def halves(table):
    high = table.astype(np.float32).astype(BF16)
    return high, (table - high.astype(np.float64)).astype(np.float32).astype(BF16)


def tables():
    second = np.repeat(wave_table(N2, M2).T, N3, axis=1)
    third = np.tile(wave_table(N3, M3).T, (1, N2))
    first = wave_table(N1, M1)
    mixed = np.zeros((N1, 16, HALF, M1))
    for p in range(HALF):
        mixed[:, p, p] = first
    return (
        second.astype(np.float32),
        third.astype(np.float32),
        halves(mixed.reshape(N1 * 16, HALF * M1)),
    )


def ready_kernel(source, vals, val, sems):
    count = 4
    size = MG // count
    copies = []
    for i in range(count):
        where = pl.ds(i * size, size)
        copies.append(pltpu.make_async_copy(source.at[:, where], val.at[:, where], sems.at[i]))
        copies[-1].start()
    for i, copy in enumerate(copies):
        copy.wait()

        def spread(a, carry):
            for t in range(CHUNKS):
                where = pl.ds(pl.multiple_of(a * KP + t * LANES, LANES), LANES)
                vals[pl.ds(t * M1 + a, 16, stride=LINES), :] = val[:, where].astype(F32)
            return carry

        lax.fori_loop(i * M1 // count, (i + 1) * M1 // count, spread, 0)


def ready_call(val, interpret=False):
    return pl.pallas_call(
        ready_kernel,
        out_shape=jax.ShapeDtypeStruct((16 * LINES, LANES), F32),
        in_specs=[pl.BlockSpec(memory_space=pltpu.HBM)],
        out_specs=pl.BlockSpec(memory_space=VMEM),
        scratch_shapes=[VMEM((16, MG), BF16), pltpu.SemaphoreType.DMA((4,))],
        compiler_params=pltpu.CompilerParams(vmem_limit_bytes=12 << 20),
        interpret=interpret,
        name="ready",
    )(stay(val))


def density_kernel(
    place, mine, other, my_count, other_count, vals, *refs,
):
    hbm, refs = refs[:9], refs[9:]
    col_out = refs[0]
    row_outs = refs[1:6]
    cons, lhs, acc, table_a, table_b, done, lines, row_lines = refs[6:14]
    local, sems = refs[14:23], refs[23]
    copies = [pltpu.make_async_copy(a, b, sems.at[i]) for i, (a, b) in enumerate(zip(hbm, local))]
    for copy in copies:
        copy.start()
    con_mine, con_other, second, third, mix_hi, mix_lo, scale, val_e, con_e = local
    band = place[0] >> 7
    z = (place[0] >> 4) & 7
    for copy in copies[:2]:
        copy.wait()

    def spread(a, carry):
        for t in range(CHUNKS):
            where = pl.ds(pl.multiple_of(a * KP + t * LANES, LANES), LANES)
            line = t * M1 + a
            cons[pl.ds(line, 8, stride=LINES), :] = jnp.concatenate(
                [con_mine[:, where].astype(F32), con_other[:, where].astype(F32)], 0
            )
        return carry

    lax.fori_loop(0, M1, spread, 0)
    for copy in copies[2:]:
        copy.wait()

    is_first = band == 0
    first_count = jnp.where(is_first, my_count[0], other_count[0])
    both_count = my_count[0] + other_count[0]
    lane = lax.broadcasted_iota(jnp.int32, (1, LANES), 1) & 15
    gaps = []
    for h in range(2):
        gap = jnp.ones((1, LANES), F32)
        for p in range(HALF):
            pos = h * HALF + p
            from_first = pos < first_count
            slot = jnp.minimum(jnp.where(from_first, pos, pos - first_count), SLOTS - 1)
            own = from_first == is_first
            v = jnp.where(own, mine[0, slot], other[0, slot])
            c = jnp.where(own, mine[1, slot], other[1, slot])
            gap = jnp.where(lane == p, con_e[c] - val_e[v], gap)
            v_line = v * LINES
            c_line = (jnp.where(own, 0, 4) + (c & 3)) * LINES
            top = pos * M1

            def product(t, carry):
                made = vals[pl.ds(v_line + t * M1, M1), :] * cons[pl.ds(c_line + t * M1, M1), :]
                where = pl.ds(pl.multiple_of(t * LANES, LANES), LANES)
                lhs[top : top + M1, where] = made.astype(BF16)
                return carry

            lax.fori_loop(0, CHUNKS, product, 0, unroll=6)
        gaps.append(gap)

    acc[...] = jnp.zeros_like(acc)

    def make(table, k):
        for i in range(STEP // M3):
            table[i * M3 : (i + 1) * M3, :] = (
                second[pl.ds(k * (STEP // M3) + i, 1), :] * third[...]
            ).astype(BF16)

    def add(table, k):
        where = pl.ds(pl.multiple_of(k * STEP, STEP), STEP)
        acc[...] += jnp.dot(lhs[:, where], table[...], preferred_element_type=F32)

    last = KP // STEP - 1
    make(table_a, 0)

    def transform(k, carry):
        make(table_b, 2 * k + 1)
        add(table_a, 2 * k)
        make(table_a, jnp.minimum(2 * k + 2, last))
        add(table_b, 2 * k + 1)
        return carry

    lax.fori_loop(0, KP // STEP // 2, transform, 0)
    at_lane = lax.broadcasted_iota(jnp.int32, (1, LANES), 1)
    frequency = (at_lane >> 4).astype(F32)
    norm = 1.0 / math.sqrt(MG)
    for h in range(2):
        mid = acc[h * HALF * M1 : (h + 1) * HALF * M1, :]
        mid_hi = mid.astype(BF16)
        mid_lo = (mid - mid_hi.astype(F32)).astype(BF16)
        done[...] = (
            jnp.dot(mix_hi[...], mid_hi, preferred_element_type=F32)
            + jnp.dot(mix_hi[...], mid_lo, preferred_element_type=F32)
            + jnp.dot(mix_lo[...], mid_hi, preferred_element_type=F32)
        ) * jnp.concatenate(
            [jnp.broadcast_to(scale[:, k * NP : (k + 1) * NP] * norm, (16, NP)) for k in range(N1)], 0
        )
        gap = gaps[h]
        live = (h * HALF + lane < both_count) & (lane < HALF) & (at_lane < 32)
        weight = jnp.where(
            live, 2.0 * gap / (gap * gap + frequency * frequency), 0.0
        ) * (1.0 / math.sqrt(TOTAL))
        w_hi = weight.astype(BF16).astype(F32)
        w_mid = (weight - w_hi).astype(BF16).astype(F32)
        lines[WIDTH * HALF : WIDTH * HALF + 1, :] = w_hi
        lines[WIDTH * HALF + 1 : WIDTH * HALF + 2, :] = w_mid
        lines[WIDTH * HALF + 2 : WIDTH * HALF + 3, :] = weight - w_hi - w_mid
        lines[WIDTH * HALF + 3 : WIDTH * HALF + 4, :] = jnp.zeros((1, LANES), F32)

        @pl.when(band == h)
        def _():
            for k in range(N1):
                for ch in range(WIDTH):
                    lines[ch * HALF : (ch + 1) * HALF, :] = done[
                        k * 16 : k * 16 + HALF, ch * LANES : (ch + 1) * LANES
                    ]
                col_out[k] = lines[...].astype(BF16)

        def message(step):
            target = jnp.where(band == 0, z + step, z - step + GROW) & 7
            for s in range(2):
                block = done[pl.ds(pl.multiple_of((2 * target + s) * 16, 16), 16), :]
                for ch in range(WIDTH):
                    at = (s * WIDTH + ch) * HALF
                    row_lines[at : at + HALF, :] = block[:HALF, ch * LANES : (ch + 1) * LANES]
            return row_lines[...].astype(BF16)

        for step in range(1, 4):
            row_outs[step][jnp.where(band == h, 0, 1)] = message(step)

        @pl.when(band == h)
        def _():
            row_outs[4][0] = message(4)

        @pl.when(band != h)
        def _():
            row_outs[0][0] = message(0)


def stay(array):
    return pltpu.with_memory_space_constraint(jnp.asarray(array), pltpu.HBM)


def density_call(
    place, mine, other, my_count, other_count, val_e, con_e, vals, con_mine, con_other, scale, interpret=False
):
    second, third, (mix_hi, mix_lo) = tables()
    smem = pl.BlockSpec(memory_space=SMEM)
    vmem = pl.BlockSpec(memory_space=VMEM)
    hbm = pl.BlockSpec(memory_space=pltpu.HBM)
    anywhere = pl.BlockSpec(memory_space=pl.ANY)
    return pl.pallas_call(
        density_kernel,
        out_shape=[
            jax.ShapeDtypeStruct((N1, BLOCK, LANES), BF16),
        ]
        + [jax.ShapeDtypeStruct((n, ROWBLOCK, LANES), BF16) for n in (1, 2, 2, 2, 1)],
        in_specs=[smem] * 5 + [vmem, hbm, anywhere] + [hbm] * 7,
        out_specs=[vmem] * 6,
        scratch_shapes=[
            VMEM((8 * LINES, LANES), F32),
            VMEM((2 * HALF * M1, KP), BF16),
            VMEM((2 * HALF * M1, NP), F32),
            VMEM((STEP, NP), BF16),
            VMEM((STEP, NP), BF16),
            VMEM((N1 * 16, NP), F32),
            VMEM((BLOCK, LANES), F32),
            VMEM((ROWBLOCK, LANES), F32),
            VMEM((4, MG), BF16),
            VMEM((4, MG), BF16),
            VMEM((M2, NP), F32),
            VMEM((M3, NP), F32),
            VMEM((N1 * 16, HALF * M1), BF16),
            VMEM((N1 * 16, HALF * M1), BF16),
            VMEM((1, N1 * NP), F32),
            SMEM((16,), F32),
            SMEM((1024,), F32),
            pltpu.SemaphoreType.DMA((9,)),
        ],
        compiler_params=pltpu.CompilerParams(vmem_limit_bytes=26 << 20),
        interpret=interpret,
        name="density",
    )(place, mine, other, my_count, other_count, vals, stay(con_mine), con_other, stay(second), stay(third),
      stay(mix_hi), stay(mix_lo), stay(scale), stay(val_e), stay(con_e))


def pack_kernel(*refs):
    blocks, out, spread = refs[:5], refs[5], refs[6]
    stride = ROWBLOCK + 4
    for i in range(4):
        for m, block in enumerate((blocks[i + 1][0], blocks[i][1 if i else 0])):
            at = (2 * i + m) * stride
            spread[at : at + ROWBLOCK, :] = block.astype(F32)
    for ch in range(2 * WIDTH):
        for pp in range(HALF // 2):
            got = [spread[pl.ds(ch * HALF + 2 * pp + q, 8, stride=stride), :] for q in range(2)]
            out[pp * 16 : (pp + 1) * 16, ch * LANES : (ch + 1) * LANES] = jnp.concatenate(
                got, 0
            ).astype(BF16)


def pack_call(blocks, interpret=False):
    vmem = pl.BlockSpec(memory_space=VMEM)
    return pl.pallas_call(
        pack_kernel,
        out_shape=jax.ShapeDtypeStruct((8 * HALF, ROW), BF16),
        in_specs=[vmem] * 5,
        out_specs=vmem,
        scratch_shapes=[VMEM((8 * (ROWBLOCK + 4), LANES), F32)],
        compiler_params=pltpu.CompilerParams(vmem_limit_bytes=4 << 20),
        interpret=interpret,
        name="pack",
    )(*blocks)


def around(step):
    return jnp.where(step == 0, 0, jnp.where(step == 1, 3, jnp.where(step == 2, 1, 2)))


def assemble_kernel(place, *refs):
    cols = refs[:8]
    away_out, home_out, spread = refs[8:]
    me = place[0]
    band, y, x = me >> 7, (me >> 2) & 3, me & 3
    for v, col in enumerate(cols):
        for q in range(GCOL):
            at = v * COLROWS + q * BLOCK
            spread[at : at + BLOCK, :] = col[q].astype(F32)

    def assemble(j, carry):
        outer, inner = around(j >> 2), around(j & 3)
        dy = jnp.where(band == 0, outer, inner)
        dx = jnp.where(band == 0, inner, outer)
        base = (((y + dy) & 3) * 4 + ((x + dx) & 3)) * BLOCK
        weight = jnp.zeros((GROW, LANES), F32)
        for part in range(3):
            weight += spread[pl.ds(base + WIDTH * HALF + part, GROW, stride=COLROWS), :]
        other = pltpu.roll(weight, LANES - 16, 1)
        away = jnp.where(band == 0, other, weight)
        home = jnp.where(band == 0, weight, other)
        for pp in range(HALF // 2):
            ws = [
                [jnp.broadcast_to(w[:, 2 * pp + q : 2 * pp + q + 1], (GROW, LANES)) for q in range(2)]
                for w in (away, home)
            ]
            to = pl.ds(pl.multiple_of(j * GROW * HALF + pp * 16, 16), 16)
            for ch in range(WIDTH):
                got = [
                    spread[pl.ds(base + ch * HALF + 2 * pp + q, GROW, stride=COLROWS), :]
                    for q in range(2)
                ]
                where = slice(ch * LANES, (ch + 1) * LANES)
                for f, dest in enumerate((away_out, home_out)):
                    dest[to, where] = jnp.concatenate(
                        [got[0] * ws[f][0], got[1] * ws[f][1]], 0
                    ).astype(BF16)
        return carry

    lax.fori_loop(0, GCOL, assemble, 0)


def assemble_call(place, cols, interpret=False):
    vmem = pl.BlockSpec(memory_space=VMEM)
    return pl.pallas_call(
        assemble_kernel,
        out_shape=[jax.ShapeDtypeStruct((PANEL, NP), BF16)] * 2,
        in_specs=[pl.BlockSpec(memory_space=SMEM)] + [vmem] * 8,
        out_specs=[vmem] * 2,
        scratch_shapes=[VMEM((GROW * COLROWS, LANES), F32)],
        compiler_params=pltpu.CompilerParams(vmem_limit_bytes=14 << 20),
        interpret=interpret,
        name="assemble",
    )(place, *cols)


EARLY = 768
LATE = PANEL - EARLY
OVER = EARLY - 640


def flip_kernel(line, below, above, out):
    def turn(m, carry):
        where = pl.ds(pl.multiple_of(m * 256, 256), 256)
        out[where, :] = jnp.concatenate(
            [line[:, where], below[:, where], above[:OVER, where]], 0
        ).T
        return carry

    lax.fori_loop(0, ROW // 256, turn, 0)


def flip_call(line, below, above, interpret=False):
    vmem = pl.BlockSpec(memory_space=VMEM)
    return pl.pallas_call(
        flip_kernel,
        out_shape=jax.ShapeDtypeStruct((ROW, EARLY), BF16),
        in_specs=[vmem] * 3,
        out_specs=vmem,
        compiler_params=pltpu.CompilerParams(vmem_limit_bytes=8 << 20),
        interpret=interpret,
        name="flip",
    )(line, below, above)


def away_kernel(weighted, early, above, far_a, far_b, away_out, late_out, rows, sems):
    size = far_a.shape[0]
    copies = [
        pltpu.make_async_copy(above.at[pl.ds(OVER, 320 - OVER), :], rows.at[pl.ds(0, 320 - OVER), :], sems.at[0]),
        pltpu.make_async_copy(far_a, rows.at[pl.ds(320 - OVER, size), :], sems.at[1]),
        pltpu.make_async_copy(far_b, rows.at[pl.ds(320 - OVER + size, size), :], sems.at[2]),
    ]
    for copy in copies:
        copy.start()
    for copy in copies:
        copy.wait()

    def product(m, carry):
        where = pl.ds(pl.multiple_of(m * 256, 256), 256)
        part = rows[:, where].T
        late_out[where, :] = part
        away_out[where, :] = (
            jnp.dot(early[where, :], weighted[:EARLY, :], preferred_element_type=F32)
            + jnp.dot(part, weighted[EARLY:, :], preferred_element_type=F32)
        ).astype(BF16)
        return carry

    lax.fori_loop(0, ROW // 256, product, 0)


def away_call(weighted, early, above, far_a, far_b, interpret=False):
    vmem = pl.BlockSpec(memory_space=VMEM)
    anywhere = pl.BlockSpec(memory_space=pl.ANY)
    return pl.pallas_call(
        away_kernel,
        out_shape=(
            jax.ShapeDtypeStruct((ROW, NP), BF16),
            jax.ShapeDtypeStruct((ROW, LATE), BF16),
        ),
        in_specs=[vmem, vmem] + [anywhere] * 3,
        out_specs=(vmem, vmem),
        scratch_shapes=[VMEM((LATE, ROW), BF16), pltpu.SemaphoreType.DMA((3,))],
        compiler_params=pltpu.CompilerParams(vmem_limit_bytes=20 << 20),
        interpret=interpret,
        name="away",
    )(weighted, early, above, far_a, far_b)


def home_kernel(weighted, early, home_out):
    def product(m, carry):
        where = pl.ds(pl.multiple_of(m * 256, 256), 256)
        home_out[where, :] = jnp.dot(
            early[where, :], weighted[:EARLY, :], preferred_element_type=F32
        )
        return carry

    lax.fori_loop(0, ROW // 256, product, 0)


def home_call(weighted, early, interpret=False):
    vmem = pl.BlockSpec(memory_space=VMEM)
    return pl.pallas_call(
        home_kernel,
        out_shape=jax.ShapeDtypeStruct((ROW, NP), F32),
        in_specs=[vmem] * 2,
        out_specs=vmem,
        compiler_params=pltpu.CompilerParams(vmem_limit_bytes=16 << 20),
        interpret=interpret,
        name="home",
    )(weighted, early)


def finish_kernel(weighted, home, late, received, out, buffers, sems):
    copies = []
    for m in range(ROW // 256):
        where = slice(m * 256, (m + 1) * 256)
        slot = m % 2
        if m >= 2:
            copies[m - 2].wait()
        made = jnp.dot(late[where, :], weighted[EARLY:, :], preferred_element_type=F32)
        buffers[slot] = -(home[where, :] + made + received[where, :].astype(F32))
        copies.append(pltpu.make_async_copy(buffers.at[slot], out.at[0, pl.ds(m * 256, 256), :], sems.at[m]))
        copies[m].start()
    copies[-2].wait()
    copies[-1].wait()


def finish_call(weighted, home, late, received, interpret=False):
    vmem = pl.BlockSpec(memory_space=VMEM)
    return pl.pallas_call(
        finish_kernel,
        out_shape=jax.ShapeDtypeStruct((1, ROW, NP), F32),
        in_specs=[vmem] * 4,
        out_specs=pl.BlockSpec(memory_space=pltpu.HBM),
        scratch_shapes=[VMEM((2, 256, NP), F32), pltpu.SemaphoreType.DMA((ROW // 256,))],
        compiler_params=pltpu.CompilerParams(vmem_limit_bytes=16 << 20),
        interpret=interpret,
        name="finish",
    )(weighted, home, late, received)


PLANE = ("band", "gcol_0", "gcol_1")


def turned(array, phase, step):
    pairs = []
    for band in range(2):
        along_x = (band == 0) == (phase == 0)
        for y in range(4):
            for x in range(4):
                to = (y, (x + step) % 4) if along_x else ((y + step) % 4, x)
                pairs.append((band * 16 + y * 4 + x, band * 16 + to[0] * 4 + to[1]))
    return lax.ppermute(array, PLANE, pairs)


def along(array, step):
    pairs = []
    for band in range(2):
        for z in range(GROW):
            to = (z + step) % GROW if band == 0 else (z - step) % GROW
            pairs.append((band * GROW + z, band * GROW + to))
    return lax.ppermute(array, ("band", "grow"), pairs)


def swap(array):
    return lax.ppermute(array, "band", [(0, 1), (1, 0)])


def per_device(
    valence_orbitals,
    conduction_orbitals,
    valence_energy,
    conduction_energy,
    coulomb_root,
    pair_bands,
    slot_counts,
):
    place = lax.axis_index(("band", "grow", "gcol_0", "gcol_1")).astype(jnp.int32).reshape(1)
    other_con = swap(conduction_orbitals)
    other_pairs, other_count = swap(pair_bands), swap(slot_counts)
    vals = ready_call(valence_orbitals)
    col, *rows = density_call(
        place, pair_bands, other_pairs, slot_counts, other_count, valence_energy, conduction_energy,
        vals, conduction_orbitals, other_con, coulomb_root.reshape(1, N1 * NP),
    )
    return exchange(place, col, rows)


def exchange(place, col, rows):
    rows = [rows[0]] + [along(rows[i], i) for i in range(1, 5)]
    col = lax.all_to_all(col, ("gcol_0", "gcol_1"), 0, 0, tiled=True)
    row = pack_call(rows)
    main, other = [col], [swap(col)]
    for _ in range(1, 5):
        main.append(along(main[-1], 1))
    for _ in range(1, 4):
        other.append(along(other[-1], 1))
    rings = []
    for i in range(4):
        rings += [main[i + 1], other[i]]
    far = turned(row, 0, 2)
    below, above = turned(row, 0, 1), turned(row, 0, -1)
    line = jnp.concatenate([row, below, above, far], 0)
    half = line.shape[0] // 2
    below, above = turned(line, 1, 1), turned(line, 1, -1)
    far_a, far_b = turned(below[:half], 1, 1), turned(above[half:], 1, -1)
    weighted_away, weighted_home = assemble_call(place, rings)
    early = flip_call(line, below, above)
    away, late = away_call(weighted_away, early, above, far_a, far_b)
    received = swap(away)
    home = home_call(weighted_home, early)
    return finish_call(weighted_home, home, late, received)


def solution(mesh):
    finer = Mesh(
        mesh.devices.reshape(mesh.shape["band"], mesh.shape["grow"], 4, 4),
        ("band", "grow", "gcol_0", "gcol_1"),
    )
    everywhere = ("band", "grow", "gcol_0", "gcol_1")
    in_specs = (P(), P(everywhere, None), P(), P(), P(), P(None, everywhere), P(everywhere))
    return jax.shard_map(
        per_device,
        mesh=finer,
        in_specs=in_specs,
        out_specs=P("band", "grow", ("gcol_0", "gcol_1")),
        check_vma=False,
    )
```

```python
import math

import jax
import jax.numpy as jnp
import numpy as np
from jax import lax
from jax.experimental import pallas as pl
from jax.experimental.pallas import tpu as pltpu
from jax.sharding import Mesh
from jax.sharding import PartitionSpec as P


N1, N2, N3 = 16, 24, 32
M1, M2, M3 = 32, 48, 64
NP = N2 * N3
KP = M2 * M3
MG = M1 * KP
ROW = 2 * NP
TOTAL = 5120
SLOTS = 20
HALF = 10
GROW, GCOL = 8, 16
LANES = 128
CHUNKS = KP // LANES
LINES = MG // LANES + 4
PANEL = GROW * GCOL * HALF
BLOCK = 64
ROWBLOCK = 120
COLROWS = GCOL * BLOCK + 4
WIDTH = NP // LANES
STEP = 512
F32, BF16 = jnp.float32, jnp.bfloat16
VMEM = pltpu.VMEM
SMEM = pltpu.SMEM


def wave_table(keep, length):
    wave = (np.arange(keep)[:, None] - keep // 2) % length
    angles = 2.0 * np.pi * (wave * np.arange(length)[None, :] % length) / length
    return np.cos(angles) + np.sin(angles)


def halves(table):
    high = table.astype(np.float32).astype(BF16)
    return high, (table - high.astype(np.float64)).astype(np.float32).astype(BF16)


def tables():
    second = np.repeat(wave_table(N2, M2).T, N3, axis=1)
    third = np.tile(wave_table(N3, M3).T, (1, N2))
    first = wave_table(N1, M1)
    mixed = np.zeros((N1, 16, HALF, M1))
    for p in range(HALF):
        mixed[:, p, p] = first
    return (
        second.astype(np.float32),
        third.astype(np.float32),
        halves(mixed.reshape(N1 * 16, HALF * M1)),
    )


def ready_kernel(source, vals, val, sems):
    count = 4
    size = MG // count
    copies = []
    for i in range(count):
        where = pl.ds(i * size, size)
        copies.append(pltpu.make_async_copy(source.at[:, where], val.at[:, where], sems.at[i]))
        copies[-1].start()
    for i, copy in enumerate(copies):
        copy.wait()

        def spread(a, carry):
            for t in range(CHUNKS):
                where = pl.ds(pl.multiple_of(a * KP + t * LANES, LANES), LANES)
                vals[pl.ds(t * M1 + a, 16, stride=LINES), :] = val[:, where].astype(F32)
            return carry

        lax.fori_loop(i * M1 // count, (i + 1) * M1 // count, spread, 0)


def ready_call(val, interpret=False):
    return pl.pallas_call(
        ready_kernel,
        out_shape=jax.ShapeDtypeStruct((16 * LINES, LANES), F32),
        in_specs=[pl.BlockSpec(memory_space=pltpu.HBM)],
        out_specs=pl.BlockSpec(memory_space=VMEM),
        scratch_shapes=[VMEM((16, MG), BF16), pltpu.SemaphoreType.DMA((4,))],
        compiler_params=pltpu.CompilerParams(vmem_limit_bytes=12 << 20),
        interpret=interpret,
        name="ready",
    )(stay(val))


def density_kernel(
    place, mine, other, my_count, other_count, vals, *refs,
):
    hbm, refs = refs[:9], refs[9:]
    col_out = refs[0]
    row_outs = refs[1:6]
    cons, lhs, acc, table_a, table_b, done, lines, row_lines = refs[6:14]
    local, sems = refs[14:23], refs[23]
    copies = [pltpu.make_async_copy(a, b, sems.at[i]) for i, (a, b) in enumerate(zip(hbm, local))]
    for copy in copies:
        copy.start()
    con_mine, con_other, second, third, mix_hi, mix_lo, scale, val_e, con_e = local
    band = place[0] >> 7
    z = (place[0] >> 4) & 7
    for copy in copies[:2]:
        copy.wait()

    def spread(a, carry):
        for t in range(CHUNKS):
            where = pl.ds(pl.multiple_of(a * KP + t * LANES, LANES), LANES)
            line = t * M1 + a
            cons[pl.ds(line, 8, stride=LINES), :] = jnp.concatenate(
                [con_mine[:, where].astype(F32), con_other[:, where].astype(F32)], 0
            )
        return carry

    lax.fori_loop(0, M1, spread, 0)
    for copy in copies[2:]:
        copy.wait()

    is_first = band == 0
    first_count = jnp.where(is_first, my_count[0], other_count[0])
    both_count = my_count[0] + other_count[0]
    lane = lax.broadcasted_iota(jnp.int32, (1, LANES), 1) & 15
    gaps = []
    for h in range(2):
        gap = jnp.ones((1, LANES), F32)
        for p in range(HALF):
            pos = h * HALF + p
            from_first = pos < first_count
            slot = jnp.minimum(jnp.where(from_first, pos, pos - first_count), SLOTS - 1)
            own = from_first == is_first
            v = jnp.where(own, mine[0, slot], other[0, slot])
            c = jnp.where(own, mine[1, slot], other[1, slot])
            gap = jnp.where(lane == p, con_e[c] - val_e[v], gap)
            v_line = v * LINES
            c_line = (jnp.where(own, 0, 4) + (c & 3)) * LINES
            top = pos * M1

            def product(t, carry):
                made = vals[pl.ds(v_line + t * M1, M1), :] * cons[pl.ds(c_line + t * M1, M1), :]
                where = pl.ds(pl.multiple_of(t * LANES, LANES), LANES)
                lhs[top : top + M1, where] = made.astype(BF16)
                return carry

            lax.fori_loop(0, CHUNKS, product, 0, unroll=12)
        gaps.append(gap)

    acc[...] = jnp.zeros_like(acc)

    def make(table, k):
        for i in range(STEP // M3):
            table[i * M3 : (i + 1) * M3, :] = (
                second[pl.ds(k * (STEP // M3) + i, 1), :] * third[...]
            ).astype(BF16)

    def add(table, k):
        where = pl.ds(pl.multiple_of(k * STEP, STEP), STEP)
        acc[...] += jnp.dot(lhs[:, where], table[...], preferred_element_type=F32)

    last = KP // STEP - 1
    make(table_a, 0)

    def transform(k, carry):
        make(table_b, 2 * k + 1)
        add(table_a, 2 * k)
        make(table_a, jnp.minimum(2 * k + 2, last))
        add(table_b, 2 * k + 1)
        return carry

    lax.fori_loop(0, KP // STEP // 2, transform, 0)
    at_lane = lax.broadcasted_iota(jnp.int32, (1, LANES), 1)
    frequency = (at_lane >> 4).astype(F32)
    norm = 1.0 / math.sqrt(MG)
    for h in range(2):
        mid = acc[h * HALF * M1 : (h + 1) * HALF * M1, :]
        mid_hi = mid.astype(BF16)
        mid_lo = (mid - mid_hi.astype(F32)).astype(BF16)
        done[...] = (
            jnp.dot(mix_hi[...], mid_hi, preferred_element_type=F32)
            + jnp.dot(mix_hi[...], mid_lo, preferred_element_type=F32)
            + jnp.dot(mix_lo[...], mid_hi, preferred_element_type=F32)
        ) * jnp.concatenate(
            [jnp.broadcast_to(scale[:, k * NP : (k + 1) * NP] * norm, (16, NP)) for k in range(N1)], 0
        )
        gap = gaps[h]
        live = (h * HALF + lane < both_count) & (lane < HALF) & (at_lane < 32)
        weight = jnp.where(
            live, 2.0 * gap / (gap * gap + frequency * frequency), 0.0
        ) * (1.0 / math.sqrt(TOTAL))
        w_hi = weight.astype(BF16).astype(F32)
        w_mid = (weight - w_hi).astype(BF16).astype(F32)
        lines[WIDTH * HALF : WIDTH * HALF + 1, :] = w_hi
        lines[WIDTH * HALF + 1 : WIDTH * HALF + 2, :] = w_mid
        lines[WIDTH * HALF + 2 : WIDTH * HALF + 3, :] = weight - w_hi - w_mid
        lines[WIDTH * HALF + 3 : WIDTH * HALF + 4, :] = jnp.zeros((1, LANES), F32)

        @pl.when(band == h)
        def _():
            for k in range(N1):
                for ch in range(WIDTH):
                    lines[ch * HALF : (ch + 1) * HALF, :] = done[
                        k * 16 : k * 16 + HALF, ch * LANES : (ch + 1) * LANES
                    ]
                col_out[k] = lines[...].astype(BF16)

        def message(step):
            target = jnp.where(band == 0, z + step, z - step + GROW) & 7
            for s in range(2):
                block = done[pl.ds(pl.multiple_of((2 * target + s) * 16, 16), 16), :]
                for ch in range(WIDTH):
                    at = (s * WIDTH + ch) * HALF
                    row_lines[at : at + HALF, :] = block[:HALF, ch * LANES : (ch + 1) * LANES]
            return row_lines[...].astype(BF16)

        for step in range(1, 4):
            row_outs[step][jnp.where(band == h, 0, 1)] = message(step)

        @pl.when(band == h)
        def _():
            row_outs[4][0] = message(4)

        @pl.when(band != h)
        def _():
            row_outs[0][0] = message(0)


def stay(array):
    return pltpu.with_memory_space_constraint(jnp.asarray(array), pltpu.HBM)


def density_call(
    place, mine, other, my_count, other_count, val_e, con_e, vals, con_mine, con_other, scale, interpret=False
):
    second, third, (mix_hi, mix_lo) = tables()
    smem = pl.BlockSpec(memory_space=SMEM)
    vmem = pl.BlockSpec(memory_space=VMEM)
    hbm = pl.BlockSpec(memory_space=pltpu.HBM)
    anywhere = pl.BlockSpec(memory_space=pl.ANY)
    return pl.pallas_call(
        density_kernel,
        out_shape=[
            jax.ShapeDtypeStruct((N1, BLOCK, LANES), BF16),
        ]
        + [jax.ShapeDtypeStruct((n, ROWBLOCK, LANES), BF16) for n in (1, 2, 2, 2, 1)],
        in_specs=[smem] * 5 + [vmem, hbm, anywhere] + [hbm] * 7,
        out_specs=[vmem] * 6,
        scratch_shapes=[
            VMEM((8 * LINES, LANES), F32),
            VMEM((2 * HALF * M1, KP), BF16),
            VMEM((2 * HALF * M1, NP), F32),
            VMEM((STEP, NP), BF16),
            VMEM((STEP, NP), BF16),
            VMEM((N1 * 16, NP), F32),
            VMEM((BLOCK, LANES), F32),
            VMEM((ROWBLOCK, LANES), F32),
            VMEM((4, MG), BF16),
            VMEM((4, MG), BF16),
            VMEM((M2, NP), F32),
            VMEM((M3, NP), F32),
            VMEM((N1 * 16, HALF * M1), BF16),
            VMEM((N1 * 16, HALF * M1), BF16),
            VMEM((1, N1 * NP), F32),
            SMEM((16,), F32),
            SMEM((1024,), F32),
            pltpu.SemaphoreType.DMA((9,)),
        ],
        compiler_params=pltpu.CompilerParams(vmem_limit_bytes=26 << 20),
        interpret=interpret,
        name="density",
    )(place, mine, other, my_count, other_count, vals, stay(con_mine), con_other, stay(second), stay(third),
      stay(mix_hi), stay(mix_lo), stay(scale), stay(val_e), stay(con_e))


def pack_kernel(*refs):
    blocks, out, spread = refs[:5], refs[5], refs[6]
    stride = ROWBLOCK + 4
    for i in range(4):
        for m, block in enumerate((blocks[i + 1][0], blocks[i][1 if i else 0])):
            at = (2 * i + m) * stride
            spread[at : at + ROWBLOCK, :] = block.astype(F32)
    for ch in range(2 * WIDTH):
        for pp in range(HALF // 2):
            got = [spread[pl.ds(ch * HALF + 2 * pp + q, 8, stride=stride), :] for q in range(2)]
            out[pp * 16 : (pp + 1) * 16, ch * LANES : (ch + 1) * LANES] = jnp.concatenate(
                got, 0
            ).astype(BF16)


def pack_call(blocks, interpret=False):
    vmem = pl.BlockSpec(memory_space=VMEM)
    return pl.pallas_call(
        pack_kernel,
        out_shape=jax.ShapeDtypeStruct((8 * HALF, ROW), BF16),
        in_specs=[vmem] * 5,
        out_specs=vmem,
        scratch_shapes=[VMEM((8 * (ROWBLOCK + 4), LANES), F32)],
        compiler_params=pltpu.CompilerParams(vmem_limit_bytes=4 << 20),
        interpret=interpret,
        name="pack",
    )(*blocks)


def around(step):
    return jnp.where(step == 0, 0, jnp.where(step == 1, 3, jnp.where(step == 2, 1, 2)))


def assemble_kernel(place, *refs):
    cols = refs[:8]
    away_out, home_out, spread = refs[8:]
    me = place[0]
    band, y, x = me >> 7, (me >> 2) & 3, me & 3
    for v, col in enumerate(cols):
        for q in range(GCOL):
            at = v * COLROWS + q * BLOCK
            spread[at : at + BLOCK, :] = col[q].astype(F32)

    def assemble(j, carry):
        outer, inner = around(j >> 2), around(j & 3)
        dy = jnp.where(band == 0, outer, inner)
        dx = jnp.where(band == 0, inner, outer)
        base = (((y + dy) & 3) * 4 + ((x + dx) & 3)) * BLOCK
        weight = jnp.zeros((GROW, LANES), F32)
        for part in range(3):
            weight += spread[pl.ds(base + WIDTH * HALF + part, GROW, stride=COLROWS), :]
        other = pltpu.roll(weight, LANES - 16, 1)
        away = jnp.where(band == 0, other, weight)
        home = jnp.where(band == 0, weight, other)
        for pp in range(HALF // 2):
            ws = [
                [jnp.broadcast_to(w[:, 2 * pp + q : 2 * pp + q + 1], (GROW, LANES)) for q in range(2)]
                for w in (away, home)
            ]
            to = pl.ds(pl.multiple_of(j * GROW * HALF + pp * 16, 16), 16)
            for ch in range(WIDTH):
                got = [
                    spread[pl.ds(base + ch * HALF + 2 * pp + q, GROW, stride=COLROWS), :]
                    for q in range(2)
                ]
                where = slice(ch * LANES, (ch + 1) * LANES)
                for f, dest in enumerate((away_out, home_out)):
                    dest[to, where] = jnp.concatenate(
                        [got[0] * ws[f][0], got[1] * ws[f][1]], 0
                    ).astype(BF16)
        return carry

    lax.fori_loop(0, GCOL, assemble, 0)


def assemble_call(place, cols, interpret=False):
    vmem = pl.BlockSpec(memory_space=VMEM)
    return pl.pallas_call(
        assemble_kernel,
        out_shape=[jax.ShapeDtypeStruct((PANEL, NP), BF16)] * 2,
        in_specs=[pl.BlockSpec(memory_space=SMEM)] + [vmem] * 8,
        out_specs=[vmem] * 2,
        scratch_shapes=[VMEM((GROW * COLROWS, LANES), F32)],
        compiler_params=pltpu.CompilerParams(vmem_limit_bytes=14 << 20),
        interpret=interpret,
        name="assemble",
    )(place, *cols)


EARLY = 768
LATE = PANEL - EARLY
OVER = EARLY - 640


def flip_kernel(line, below, above, out):
    def turn(m, carry):
        where = pl.ds(pl.multiple_of(m * 256, 256), 256)
        out[where, :] = jnp.concatenate(
            [line[:, where], below[:, where], above[:OVER, where]], 0
        ).T
        return carry

    lax.fori_loop(0, ROW // 256, turn, 0)


def flip_call(line, below, above, interpret=False):
    vmem = pl.BlockSpec(memory_space=VMEM)
    return pl.pallas_call(
        flip_kernel,
        out_shape=jax.ShapeDtypeStruct((ROW, EARLY), BF16),
        in_specs=[vmem] * 3,
        out_specs=vmem,
        compiler_params=pltpu.CompilerParams(vmem_limit_bytes=8 << 20),
        interpret=interpret,
        name="flip",
    )(line, below, above)


def away_kernel(weighted, early, above, far_a, far_b, away_out, late_out, rows, sems):
    size = far_a.shape[0]
    copies = [
        pltpu.make_async_copy(above.at[pl.ds(OVER, 320 - OVER), :], rows.at[pl.ds(0, 320 - OVER), :], sems.at[0]),
        pltpu.make_async_copy(far_a, rows.at[pl.ds(320 - OVER, size), :], sems.at[1]),
        pltpu.make_async_copy(far_b, rows.at[pl.ds(320 - OVER + size, size), :], sems.at[2]),
    ]
    for copy in copies:
        copy.start()
    for copy in copies:
        copy.wait()

    def product(m, carry):
        where = pl.ds(pl.multiple_of(m * 256, 256), 256)
        part = rows[:, where].T
        late_out[where, :] = part
        away_out[where, :] = (
            jnp.dot(early[where, :], weighted[:EARLY, :], preferred_element_type=F32)
            + jnp.dot(part, weighted[EARLY:, :], preferred_element_type=F32)
        ).astype(BF16)
        return carry

    lax.fori_loop(0, ROW // 256, product, 0)


def away_call(weighted, early, above, far_a, far_b, interpret=False):
    vmem = pl.BlockSpec(memory_space=VMEM)
    anywhere = pl.BlockSpec(memory_space=pl.ANY)
    return pl.pallas_call(
        away_kernel,
        out_shape=(
            jax.ShapeDtypeStruct((ROW, NP), BF16),
            jax.ShapeDtypeStruct((ROW, LATE), BF16),
        ),
        in_specs=[vmem, vmem] + [anywhere] * 3,
        out_specs=(vmem, vmem),
        scratch_shapes=[VMEM((LATE, ROW), BF16), pltpu.SemaphoreType.DMA((3,))],
        compiler_params=pltpu.CompilerParams(vmem_limit_bytes=20 << 20),
        interpret=interpret,
        name="away",
    )(weighted, early, above, far_a, far_b)


def home_kernel(weighted, early, late, home_out):
    def product(m, carry):
        where = pl.ds(pl.multiple_of(m * 256, 256), 256)
        home_out[where, :] = jnp.dot(
            early[where, :], weighted[:EARLY, :], preferred_element_type=F32
        ) + jnp.dot(late[where, :], weighted[EARLY:, :], preferred_element_type=F32)
        return carry

    lax.fori_loop(0, ROW // 256, product, 0)


def home_call(weighted, early, late, interpret=False):
    vmem = pl.BlockSpec(memory_space=VMEM)
    return pl.pallas_call(
        home_kernel,
        out_shape=jax.ShapeDtypeStruct((ROW, NP), F32),
        in_specs=[vmem] * 3,
        out_specs=vmem,
        compiler_params=pltpu.CompilerParams(vmem_limit_bytes=16 << 20),
        interpret=interpret,
        name="home",
    )(weighted, early, late)


PLANE = ("band", "gcol_0", "gcol_1")


def turned(array, phase, step):
    pairs = []
    for band in range(2):
        along_x = (band == 0) == (phase == 0)
        for y in range(4):
            for x in range(4):
                to = (y, (x + step) % 4) if along_x else ((y + step) % 4, x)
                pairs.append((band * 16 + y * 4 + x, band * 16 + to[0] * 4 + to[1]))
    return lax.ppermute(array, PLANE, pairs)


def along(array, step):
    pairs = []
    for band in range(2):
        for z in range(GROW):
            to = (z + step) % GROW if band == 0 else (z - step) % GROW
            pairs.append((band * GROW + z, band * GROW + to))
    return lax.ppermute(array, ("band", "grow"), pairs)


def swap(array):
    return lax.ppermute(array, "band", [(0, 1), (1, 0)])


def per_device(
    valence_orbitals,
    conduction_orbitals,
    valence_energy,
    conduction_energy,
    coulomb_root,
    pair_bands,
    slot_counts,
):
    place = lax.axis_index(("band", "grow", "gcol_0", "gcol_1")).astype(jnp.int32).reshape(1)
    other_con = swap(conduction_orbitals)
    other_pairs, other_count = swap(pair_bands), swap(slot_counts)
    vals = ready_call(valence_orbitals)
    col, *rows = density_call(
        place, pair_bands, other_pairs, slot_counts, other_count, valence_energy, conduction_energy,
        vals, conduction_orbitals, other_con, coulomb_root.reshape(1, N1 * NP),
    )
    return exchange(place, col, rows)


def exchange(place, col, rows):
    rows = [rows[0]] + [along(rows[i], i) for i in range(1, 5)]
    col = lax.all_to_all(col, ("gcol_0", "gcol_1"), 0, 0, tiled=True)
    row = pack_call(rows)
    main, other = [col], [swap(col)]
    for _ in range(1, 5):
        main.append(along(main[-1], 1))
    for _ in range(1, 4):
        other.append(along(other[-1], 1))
    rings = []
    for i in range(4):
        rings += [main[i + 1], other[i]]
    far = turned(row, 0, 2)
    below, above = turned(row, 0, 1), turned(row, 0, -1)
    line = jnp.concatenate([row, below, above, far], 0)
    half = line.shape[0] // 2
    below, above = turned(line, 1, 1), turned(line, 1, -1)
    far_a, far_b = turned(below[:half], 1, 1), turned(above[half:], 1, -1)
    weighted_away, weighted_home = assemble_call(place, rings)
    early = flip_call(line, below, above)
    away, late = away_call(weighted_away, early, above, far_a, far_b)
    received = swap(away)
    home = home_call(weighted_home, early, late)
    return -(home + received.astype(F32))[None]


def solution(mesh):
    finer = Mesh(
        mesh.devices.reshape(mesh.shape["band"], mesh.shape["grow"], 4, 4),
        ("band", "grow", "gcol_0", "gcol_1"),
    )
    everywhere = ("band", "grow", "gcol_0", "gcol_1")
    in_specs = (P(), P(everywhere, None), P(), P(), P(), P(None, everywhere), P(everywhere))
    return jax.shard_map(
        per_device,
        mesh=finer,
        in_specs=in_specs,
        out_specs=P("band", "grow", ("gcol_0", "gcol_1")),
        check_vma=False,
    )
```
